32 devices in a mesh: batch: 8 (over y, x, core), mp: 4 (over z).
Axes of the slice: x: 2, y: 2, z: 4, core: 2. Of those that a mesh axis runs over, the one named last changes fastest.
Arguments:
- token_ids: int32 [8, 1536], P('batch'), may hold values from 0 to 30527
- segment_ids: int32 [8, 1536], P('batch'), may hold values from 0 to 8, never falling along the last dimension, each value on 1 to 1024 neighbouring positions
- row_of: int32 [30528], replicated, may hold values from 0 to 30527, each once
- query_count: int32 [1], replicated, may hold values from 16 to 32
- table: float32 [30528, 768], P('batch'), may hold values from -8 to 8
- qkv_weight: float32 [768, 3, 768], P('batch', None, 'mp'), may hold values from -0.21875 to 0.21875
- out_weight: float32 [768, 768], P('mp', 'batch'), may hold values from -0.875 to 0.875
- gate_up_weight: float32 [768, 2, 3072], P('batch', None, 'mp'), may hold values from -0.21875 to 0.21875
- down_weight: float32 [3072, 768], P('mp', 'batch'), may hold values from -0.109375 to 0.109375
- gains: float32 [2, 768], P(None, 'batch'), may hold values from 0.3 to 2.5
- table_m: float32 [30528, 768], P('batch'), may hold values from -0.0009765625 to 0.0009765625
- qkv_m: float32 [768, 3, 768], P('batch', None, 'mp'), may hold values from -0.0009765625 to 0.0009765625
- out_m: float32 [768, 768], P('mp', 'batch'), may hold values from -0.0009765625 to 0.0009765625
- gate_up_m: float32 [768, 2, 3072], P('batch', None, 'mp'), may hold values from -0.0009765625 to 0.0009765625
- down_m: float32 [3072, 768], P('mp', 'batch'), may hold values from -0.0009765625 to 0.0009765625
- gains_m: float32 [2, 768], P(None, 'batch'), may hold values from -0.0009765625 to 0.0009765625
- table_v: float32 [30528, 768], P('batch'), may hold values from 3.040972e-08 to 1.2163888e-07
- qkv_v: float32 [768, 3, 768], P('batch', None, 'mp'), may hold values from 3.040972e-08 to 1.2163888e-07
- out_v: float32 [768, 768], P('mp', 'batch'), may hold values from 3.040972e-08 to 1.2163888e-07
- gate_up_v: float32 [768, 2, 3072], P('batch', None, 'mp'), may hold values from 3.040972e-08 to 1.2163888e-07
- down_v: float32 [3072, 768], P('mp', 'batch'), may hold values from 3.040972e-08 to 1.2163888e-07
- gains_v: float32 [2, 768], P(None, 'batch'), may hold values from 3.040972e-08 to 1.2163888e-07
Outputs:
- loss: float32 [1], replicated
- grad_norm: float32 [1], replicated
- new_table: float32 [30528, 768], P('batch')
- new_qkv_weight: float32 [768, 3, 768], P('batch', None, 'mp')
- new_out_weight: float32 [768, 768], P('mp', 'batch')
- new_gate_up_weight: float32 [768, 2, 3072], P('batch', None, 'mp')
- new_down_weight: float32 [3072, 768], P('mp', 'batch')
- new_gains: float32 [2, 768], P(None, 'batch')
- clipped_table_grad: float32 [30528, 768], P('batch')
- new_qkv_m: float32 [768, 3, 768], P('batch', None, 'mp')
- new_out_m: float32 [768, 768], P('mp', 'batch')
- new_gate_up_m: float32 [768, 2, 3072], P('batch', None, 'mp')
- new_down_m: float32 [3072, 768], P('mp', 'batch')
- new_gains_m: float32 [2, 768], P(None, 'batch')
- new_table_v: float32 [30528, 768], P('batch')
- new_qkv_v: float32 [768, 3, 768], P('batch', None, 'mp')
- new_out_v: float32 [768, 768], P('mp', 'batch')
- new_gate_up_v: float32 [768, 2, 3072], P('batch', None, 'mp')
- new_down_v: float32 [3072, 768], P('mp', 'batch')
- new_gains_v: float32 [2, 768], P(None, 'batch')
The draws below stay inside these ranges and needn't reach their ends.
Inputs may be any that keep to these rules, and one draw needn't show every extreme that they name: `segment_ids`: in each row the ids never fall, every id 0 to 8 appears, id 8 marks padding, each segment has 1 to 1024 tokens and one has exactly 1024. A permutation: token t's embedding is table row row_of[t]. The first query_count queries count.
All inputs are finite; a program needn't handle non-finite values.
Results may differ from the reference program's by a relative error of at most 0.0075.
The reference program's roundings to bfloat16 on the way count: a program that leaves them out, or rounds other values in their place, can miss the bound.
Values may be sent and summed in bfloat16 or wider, within the bound.
A program may use at most 320 MiB of HBM per device.

```python
import math
from functools import partial
import jax
import jax.numpy as jnp
import numpy as np
from jax import lax

D = 768
HEADS = 12
HEAD_DIM = 64
FF = 3072
VOCAB = 30528
ROW_LEN = 1536
SEGS = 8
MOST = 1024
ROWS = 8
QUERIES = 32
PARAMS = 32884224


def draw_table(key, part):
    column = jnp.arange(D, dtype=jnp.float32) / (D - 1)
    base = jax.random.normal(key, (VOCAB, D), jnp.float32)
    scale = jnp.exp(jnp.log(3.0) * (column - 0.5))
    return jnp.clip(base * scale[None, :], -8.0, 8.0)


def draw_gains(key, part):
    column = jnp.arange(D, dtype=jnp.float32) / (D - 1)
    noise = jax.random.uniform(key, (2, D), jnp.float32, 0.9, 1.1)
    scale = 0.5 * jnp.exp(jnp.log(3.0) * column)
    return jnp.clip(noise * scale[None, :], 0.3, 2.5)


def set_ends(drawn, rng, smallest, largest):
    longest = drawn.shape.index(max(drawn.shape))
    spots = []
    for shift in (0, 1):
        where = [jax.random.randint(jax.random.fold_in(rng, axis), (), 0, length) for axis, length in enumerate(drawn.shape)]
        where[longest] = (where[longest] + shift) % drawn.shape[longest]
        spots.append(tuple(where))
    return drawn.at[spots[0]].set(smallest).at[spots[1]].set(largest)


def level_of(stream_key, dims, shards, least, high):
    factor_of, own = 1.0, jax.random.fold_in(stream_key, 6)
    for position, blocks in shards:
        heights = jnp.exp(jax.random.uniform(jax.random.fold_in(own, position), (blocks,), jnp.float32, least / len(shards), high / len(shards)))
        factor_of = factor_of * jnp.repeat(heights, dims[position] // blocks).reshape([-1 if axis == position else 1 for axis in range(len(dims))])
    return factor_of


def rank_bounds(count, lean):
    weights = [(1 << 20) // math.isqrt(grade ** lean) + 1 for grade in range(1, count + 1)]
    width = 1 + sum(weights) // (1 << 30)
    return np.cumsum(np.array([max(1, weight // width) for weight in weights]))


def ranked_ids(rng, shape, amount, slope):
    grid = rank_bounds(amount, slope)
    pick = jax.random.randint(jax.random.fold_in(rng, 1), shape, 0, int(grid[amount - 1]))
    grade = jnp.searchsorted(jnp.asarray(grid, jnp.int32), pick, side="right")
    return jax.random.permutation(jax.random.fold_in(rng, 2), amount)[grade].astype(jnp.int32)


def split_up(number_of, total, most, slope):
    loads = [(1 << 20) // math.isqrt(rank ** slope) + 1 for rank in range(2, number_of + 1)]
    rest, holding = total - most - (number_of - 1), [1] * (number_of - 1)
    while rest > 0:
        candidates = [i for i in range(number_of - 1) if holding[i] < most]
        pool, remaining = sum([loads[i] for i in candidates]), rest
        for i in candidates:
            extra = min(most - holding[i], max(1, remaining * loads[i] // pool), rest)
            holding[i] = holding[i] + extra
            rest = rest - extra
    return np.array([most] + holding)


def ragged(rng, count, total, most, skew):
    if count == 2:
        one = jax.random.randint(rng, (), max(1, total - most), min(most, total - 1) + 1)
        return jnp.stack([one, total - one])
    tallies = jnp.asarray(split_up(count, total, most, skew), jnp.int32)
    couples = (count - 1) // 2
    giver, receiver = tallies[1:1 + 2 * couples:2], tallies[2:2 + 2 * couples:2]
    slack = jnp.minimum(giver - 1, most - receiver)
    shifted = jax.random.randint(jax.random.fold_in(rng, 1), (couples,), 0, 1 << 20) % (slack + 1)
    tallies = tallies.at[1:1 + 2 * couples:2].set(giver - shifted).at[2:2 + 2 * couples:2].set(receiver + shifted)
    return tallies[jax.random.permutation(jax.random.fold_in(rng, 2), count)]


def normal_values(rng, extent, scale, most, pieces=(), held_as=jnp.bfloat16):
    values = scale * jax.random.normal(rng, extent, jnp.float32)
    if pieces:
        values = values * level_of(rng, extent, pieces, -0.22, 0.18)
    return jnp.clip(values, -most, most).astype(held_as)


def setup_inputs(seed: int = 0) -> dict:
    streams_of = jax.random.split(jax.random.key(seed), 23)
    return {
        "token_ids": set_ends(ranked_ids(streams_of[0], (ROWS, ROW_LEN), VOCAB, 2), jax.random.fold_in(streams_of[0], 3), 0, VOCAB - 1).astype(jnp.int32),
        "segment_ids": jax.vmap(lambda own: jnp.searchsorted(jnp.cumsum(ragged(own, SEGS + 1, ROW_LEN, MOST, 2)), jnp.arange(ROW_LEN), side="right"))(jax.random.split(streams_of[1], ROWS)).reshape((ROWS, ROW_LEN)).astype(jnp.int32),
        "row_of": jax.random.permutation(streams_of[2], VOCAB).astype(jnp.int32),
        "query_count": jax.random.randint(streams_of[3], (1,), QUERIES // 2, QUERIES + 1).astype(jnp.int32),
        "table": draw_table(jax.random.fold_in(streams_of[22], 71), 0),
        "qkv_weight": normal_values(streams_of[5], (D, 3, D), D ** -0.5, 0.21875, ((0, 8), (2, 4)), jnp.float32),
        "out_weight": normal_values(streams_of[6], (D, D), (D // 16) ** -0.5, 0.875, ((0, 4), (1, 8)), jnp.float32),
        "gate_up_weight": normal_values(streams_of[7], (D, 2, FF), D ** -0.5, 0.21875, ((0, 8), (2, 4)), jnp.float32),
        "down_weight": normal_values(streams_of[8], (FF, D), FF ** -0.5, 0.109375, ((0, 4), (1, 8)), jnp.float32),
        "gains": draw_gains(jax.random.fold_in(streams_of[22], 71), 0),
        "table_m": normal_values(streams_of[10], (VOCAB, D), PARAMS ** -0.5, 0.0009765625, ((0, 8),), jnp.float32),
        "qkv_m": normal_values(streams_of[11], (D, 3, D), PARAMS ** -0.5, 0.0009765625, ((0, 8), (2, 4)), jnp.float32),
        "out_m": normal_values(streams_of[12], (D, D), PARAMS ** -0.5, 0.0009765625, ((0, 4), (1, 8)), jnp.float32),
        "gate_up_m": normal_values(streams_of[13], (D, 2, FF), PARAMS ** -0.5, 0.0009765625, ((0, 8), (2, 4)), jnp.float32),
        "down_m": normal_values(streams_of[14], (FF, D), PARAMS ** -0.5, 0.0009765625, ((0, 4), (1, 8)), jnp.float32),
        "gains_m": normal_values(streams_of[15], (2, D), PARAMS ** -0.5, 0.0009765625, ((1, 8),), jnp.float32),
        "table_v": jnp.clip(jnp.exp(math.log(1.216388767488752e-07) - 1.3862944 * jax.random.uniform(streams_of[16], (VOCAB, D), jnp.float32) ** level_of(streams_of[16], (VOCAB, D), ((0, 8),), -0.2, 0.2)), 3.04097191872188e-08, 1.216388767488752e-07),
        "qkv_v": jnp.clip(jnp.exp(math.log(1.216388767488752e-07) - 1.3862944 * jax.random.uniform(streams_of[17], (D, 3, D), jnp.float32) ** level_of(streams_of[17], (D, 3, D), ((0, 8), (2, 4)), -0.2, 0.2)), 3.04097191872188e-08, 1.216388767488752e-07),
        "out_v": jnp.clip(jnp.exp(math.log(1.216388767488752e-07) - 1.3862944 * jax.random.uniform(streams_of[18], (D, D), jnp.float32) ** level_of(streams_of[18], (D, D), ((0, 4), (1, 8)), -0.2, 0.2)), 3.04097191872188e-08, 1.216388767488752e-07),
        "gate_up_v": jnp.clip(jnp.exp(math.log(1.216388767488752e-07) - 1.3862944 * jax.random.uniform(streams_of[19], (D, 2, FF), jnp.float32) ** level_of(streams_of[19], (D, 2, FF), ((0, 8), (2, 4)), -0.2, 0.2)), 3.04097191872188e-08, 1.216388767488752e-07),
        "down_v": jnp.clip(jnp.exp(math.log(1.216388767488752e-07) - 1.3862944 * jax.random.uniform(streams_of[20], (FF, D), jnp.float32) ** level_of(streams_of[20], (FF, D), ((0, 4), (1, 8)), -0.2, 0.2)), 3.04097191872188e-08, 1.216388767488752e-07),
        "gains_v": jnp.clip(jnp.exp(math.log(1.216388767488752e-07) - 1.3862944 * jax.random.uniform(streams_of[21], (2, D), jnp.float32) ** level_of(streams_of[21], (2, D), ((1, 8),), -0.2, 0.2)), 3.04097191872188e-08, 1.216388767488752e-07),
    }


peak_affinity = lax.Precision.HIGHEST
sharpness_divisor = 0.05
clip_limit = 1.0
step_number = 3.0
rates = (0.3, 0.02, 0.02, 0.02, 0.02, 0.3)

@jax.custom_vjp
def low(v):
    return lax.optimization_barrier(v.astype(jnp.bfloat16)).astype(jnp.float32)

@jax.custom_vjp
def low_back(v):
    return v

def low_keep(v):
    return (low(v), None)

def low_pass(kept, grad):
    return (grad,)

def back_keep(v):
    return (v, None)

def back_low(kept, grad):
    return (low(grad),)
low.defvjp(low_keep, low_pass)
low_back.defvjp(back_keep, back_low)

def positions(segment_row, segment_count):
    labels = jnp.arange(segment_count + 1, dtype=jnp.int32)
    member = (segment_row[:, None] == labels[None, :]).astype(jnp.int32)
    counts = lax.optimization_barrier(jnp.sum(member, 0))
    starts = jnp.cumsum(counts) - counts
    first_index = lax.optimization_barrier(jnp.sum(member * starts[None, :], 1))
    return (jnp.arange(segment_row.shape[0], dtype=jnp.int32) - first_index).astype(jnp.float32)

def rotate(values, places):
    half_dim = values.shape[-1] // 2
    freqs = jnp.power(1000.0, -2.0 * jnp.arange(half_dim, dtype=jnp.float32) / values.shape[-1])
    angles = places[:, None] * freqs[None, :]
    cosine = jnp.cos(angles)[:, None, :]
    sine = jnp.sin(angles)[:, None, :]
    former = values[..., :half_dim]
    latter = values[..., half_dim:]
    return jnp.concatenate([former * cosine - latter * sine, latter * cosine + former * sine], -1)

def layer_norm(values, gain):
    centred = values - lax.optimization_barrier(jnp.mean(values, -1, keepdims=True))
    spread = lax.optimization_barrier(jnp.mean(centred * centred, -1, keepdims=True))
    return centred * lax.rsqrt(spread + 1e-05) * gain

def swiglu(gate_up):
    return jax.nn.silu(gate_up[:, 0]) * gate_up[:, 1]

def row_pass(weights, x_zero, segment_row):
    w_qkv, w_out, w_gu, w_down, gain = weights
    length = x_zero.shape[0]
    places = positions(segment_row, SEGS)
    qkv = low_back(jnp.dot(x_zero, w_qkv.reshape(D, 3 * D), precision=peak_affinity)).reshape(length, 3, HEADS, HEAD_DIM)
    query = low(rotate(qkv[:, 0], places))
    keys = low(rotate(qkv[:, 1], places))
    values = low(qkv[:, 2])
    scores = low_back(jnp.einsum('qhd,khd->hqk', query, keys, precision=peak_affinity) * HEAD_DIM ** (-0.5))
    same = segment_row[:, None] == segment_row[None, :]
    scores = jnp.where(same[None], scores, -1e+30)
    probs = low(jax.nn.softmax(scores, axis=-1))
    attended = low_back(low(jnp.einsum('hqk,khd->qhd', probs, values, precision=peak_affinity).reshape(length, D)))
    attn = low_back(jnp.dot(attended, w_out, precision=peak_affinity))
    hidden_one = layer_norm(x_zero + attn, gain[0])
    gate_up = low_back(jnp.dot(low(hidden_one), w_gu.reshape(D, 2 * FF), precision=peak_affinity)).reshape(length, 2, FF)
    active = low(swiglu(gate_up))
    mlp = low_back(jnp.dot(active, w_down, precision=peak_affinity))
    hidden_two = layer_norm(hidden_one + mlp, gain[1])
    labels = jnp.arange(SEGS, dtype=jnp.int32)
    member = (segment_row[None, :] == labels[:, None]).astype(jnp.float32)
    return jnp.dot(member, hidden_two, precision=peak_affinity) / lax.optimization_barrier(jnp.sum(member, -1, keepdims=True))

def forward(table, w_qkv, w_out, w_gu, w_down, gains, token_ids, segment_ids, row_of, query_count):
    weights = (low(w_qkv), low(w_out), low(w_gu), low(w_down), low(gains))
    x_zero = low(table)[row_of[token_ids]]
    row_step = jax.checkpoint(partial(row_pass, weights))
    pooled = lax.map(lambda pair: row_step(pair[0], pair[1]), (x_zero, segment_ids))
    flat = pooled.reshape(2 * QUERIES, D)
    embed = flat * lax.rsqrt(lax.optimization_barrier(jnp.sum(flat * flat, -1, keepdims=True)) + 1e-06)
    question_vectors = embed[:QUERIES]
    passage_vectors = embed[QUERIES:]
    affinity_scores = jnp.dot(question_vectors, passage_vectors.T, precision=peak_affinity) / sharpness_divisor
    limit = query_count[0].astype(jnp.float32)
    valid = (jnp.arange(QUERIES, dtype=jnp.int32) < query_count[0]).astype(jnp.float32)
    positive_couples = lax.optimization_barrier(jnp.sum(question_vectors * passage_vectors, -1)) / sharpness_divisor
    return jnp.sum(valid * (jax.nn.logsumexp(affinity_scores, -1) - positive_couples)) / limit

def adam_update(weight, grad, first, second, rate):
    first = 0.5 * first + 0.5 * grad
    second = 0.5 * second + 0.5 * grad * grad
    correction = 1.0 - 0.5 ** step_number
    weight = weight - rate * (first / correction / (jnp.sqrt(second / correction) + 1e-08) + 0.01 * weight)
    return (weight, first, second)

def reference(token_ids, segment_ids, row_of, query_count, table, qkv_weight, out_weight, gate_up_weight, down_weight, gains, table_m, qkv_m, out_m, gate_up_m, down_m, gains_m, table_v, qkv_v, out_v, gate_up_v, down_v, gains_v):
    params = (table, qkv_weight, out_weight, gate_up_weight, down_weight, gains)
    loss, pullback = jax.vjp(lambda *weights: forward(*weights, token_ids, segment_ids, row_of, query_count), *params)
    grads = pullback(jnp.ones((), jnp.float32))
    total = sum((jnp.sum(part * part) for part in grads))
    grad_norm = jnp.sqrt(total)
    scale = clip_limit / jnp.maximum(grad_norm, clip_limit)
    firsts = (table_m, qkv_m, out_m, gate_up_m, down_m, gains_m)
    seconds = (table_v, qkv_v, out_v, gate_up_v, down_v, gains_v)
    updated = [adam_update(weight_old, grad_part * scale, first_old, second_old, rate) for weight_old, grad_part, first_old, second_old, rate in zip(params, grads, firsts, seconds, rates)]
    clipped_table = grads[0] * scale
    return (loss.reshape(1), grad_norm.reshape(1), updated[0][0], updated[1][0], updated[2][0], updated[3][0], updated[4][0], updated[5][0], clipped_table, updated[1][1], updated[2][1], updated[3][1], updated[4][1], updated[5][1], updated[0][2], updated[1][2], updated[2][2], updated[3][2], updated[4][2], updated[5][2])
```

```python
from functools import partial

import jax
import jax.numpy as jnp
from jax import lax
from jax.experimental import pallas as pl
from jax.experimental.pallas import tpu as pltpu
from jax.sharding import Mesh, PartitionSpec as P

HEAD_DIM = 64
SEGS = 8

peak_affinity = lax.Precision.HIGHEST
sharpness_divisor = 0.05
clip_limit = 1.0
step_number = 3.0
rates = (0.3, 0.02, 0.02, 0.02, 0.02, 0.3)
negative = -1e30
GROUP = ("x", "c")
ALL = ("h", "x", "c", "z")
f32 = jnp.float32
bf16 = jnp.bfloat16


def angles_of(places, head_dim):
    half_dim = head_dim // 2
    freqs = jnp.power(1000.0, -2.0 * jnp.arange(half_dim, dtype=f32) / head_dim)
    angles = places[:, None] * freqs[None, :]
    return jnp.cos(angles)[:, None, :], jnp.sin(angles)[:, None, :]


def rotate(values, cosine, sine):
    half_dim = values.shape[-1] // 2
    former = values[..., :half_dim]
    latter = values[..., half_dim:]
    return jnp.concatenate([former * cosine - latter * sine, latter * cosine + former * sine], -1)


def layer_norm(values, gain):
    centred = values - jnp.mean(values, -1, keepdims=True)
    spread = jnp.mean(centred * centred, -1, keepdims=True)
    return centred * lax.rsqrt(spread + 1e-05) * gain


def swiglu(gate, up):
    return jax.nn.silu(gate) * up


def dot(left, right, left_dims, right_dims, precision=None):
    return lax.dot_general(
        left, right, ((left_dims, right_dims), ((), ())), preferred_element_type=f32, precision=precision
    )


def attend_kernel(q_ref, k_ref, v_ref, segq_ref, segk_ref, o_ref):
    same = segq_ref[...] == segk_ref[...]
    query, keys, values = q_ref[...], k_ref[...], v_ref[...]
    width = query.shape[1]
    lane = lax.broadcasted_iota(jnp.int32, query.shape, 1) // HEAD_DIM
    result = jnp.zeros(query.shape, f32)
    for head in range(width // HEAD_DIM):
        own = jnp.where(lane == head, query, jnp.zeros_like(query))
        scores = dot(own, keys, (1,), (1,)) * HEAD_DIM ** (-0.5)
        scores = jnp.where(same, scores, negative)
        weights = jnp.exp(scores - jnp.max(scores, 1, keepdims=True))
        probs = (weights * (1.0 / jnp.sum(weights, 1, keepdims=True))).astype(bf16)
        result = jnp.where(lane == head, dot(probs, values, (1,), (0,)), result)
    o_ref[...] = result.astype(bf16)


def attend_back_kernel(q_ref, g_ref, k_ref, v_ref, segq_ref, segk_ref, dq_ref, dk_ref, dv_ref):
    @pl.when(pl.program_id(0) == 0)
    def _():
        dk_ref[...] = jnp.zeros_like(dk_ref)
        dv_ref[...] = jnp.zeros_like(dv_ref)

    same = segk_ref[...] == segq_ref[...]
    query, grad, keys, values = q_ref[...], g_ref[...], k_ref[...], v_ref[...]
    width = query.shape[1]
    factor = HEAD_DIM ** (-0.5)
    lane = lax.broadcasted_iota(jnp.int32, query.shape, 1) // HEAD_DIM
    result = jnp.zeros(query.shape, f32)
    for head in range(width // HEAD_DIM):
        own = jnp.where(lane == head, query, jnp.zeros_like(query))
        own_grad = jnp.where(lane == head, grad, jnp.zeros_like(grad))
        scores = dot(keys, own, (1,), (1,)) * factor
        scores = jnp.where(same, scores, negative)
        weights = jnp.exp(scores - jnp.max(scores, 0, keepdims=True))
        probs = weights * (1.0 / jnp.sum(weights, 0, keepdims=True))
        grad_probs = dot(values, own_grad, (1,), (1,))
        inner = jnp.sum(probs * grad_probs, 0, keepdims=True)
        grad_scores = (probs * (grad_probs - inner)).astype(bf16)
        dk_ref[...] += dot(grad_scores, own, (1,), (0,)) * factor
        dv_ref[...] += dot(probs.astype(bf16), own_grad, (1,), (0,))
        result = jnp.where(lane == head, dot(grad_scores, keys, (0,), (0,)) * factor, result)
    dq_ref[...] = result


def attend(query, keys, values, segment_row):
    length, width = query.shape
    block = min(256, length)
    whole = pl.BlockSpec((length, width), lambda i: (0, 0))
    part = pl.BlockSpec((block, width), lambda i: (i, 0))
    return pl.pallas_call(
        attend_kernel,
        grid=(length // block,),
        in_specs=[
            part,
            whole,
            whole,
            pl.BlockSpec((block, 1), lambda i: (i, 0)),
            pl.BlockSpec((1, length), lambda i: (0, 0)),
        ],
        out_specs=part,
        out_shape=jax.ShapeDtypeStruct((length, width), bf16),
    )(query, keys, values, segment_row[:, None], segment_row[None, :])


def attend_back(query, grad, keys, values, segment_row):
    length, width = query.shape
    block = min(256, length)
    whole = pl.BlockSpec((length, width), lambda i: (0, 0))
    part = pl.BlockSpec((block, width), lambda i: (i, 0))
    full = jax.ShapeDtypeStruct((length, width), f32)
    return pl.pallas_call(
        attend_back_kernel,
        grid=(length // block,),
        in_specs=[
            part,
            part,
            whole,
            whole,
            pl.BlockSpec((1, block), lambda i: (0, i)),
            pl.BlockSpec((length, 1), lambda i: (0, 0)),
        ],
        out_specs=[part, whole, whole],
        out_shape=[full, full, full],
    )(query, grad, keys, values, segment_row[None, :], segment_row[:, None])


MESH = pl.DeviceIdType.MESH
anywhere = pl.BlockSpec(memory_space=pl.ANY)
on_chip = pl.BlockSpec(memory_space=pltpu.VMEM)


def guarded(when, action):
    if when is None:
        action()
    else:
        pl.when(when)(action)


def both(first, second):
    return second if first is None else first if second is None else first & second


class Wires:
    def __init__(self, send_sem):
        self.at = {name: lax.axis_index(name) for name in ALL}
        self.send_sem = send_sem
        self.pending = []

    def peer(self, **moved):
        return tuple(moved.get(name, self.at[name]) for name in ALL)

    def greet(self, peers):
        barrier = pltpu.get_barrier_semaphore()
        expected = 0
        for when, target in peers:
            guarded(
                when,
                lambda target=target: pl.semaphore_signal(
                    barrier, inc=1, device_id=target, device_id_type=MESH
                ),
            )
            expected = expected + (1 if when is None else when.astype(jnp.int32))
        pl.semaphore_wait(barrier, expected)

    def send(self, source, goal, recv_sem, target, when=None):
        number = len(self.pending)

        def copy():
            return pltpu.make_async_remote_copy(
                src_ref=source,
                dst_ref=goal,
                send_sem=self.send_sem.at[number],
                recv_sem=recv_sem,
                device_id=target,
                device_id_type=MESH,
            )

        guarded(when, lambda: copy().start())
        self.pending.append((when, lambda: copy().wait_send()))

    def arrived(self, goal, recv_sem, when=None):
        guarded(when, lambda: pltpu.make_async_copy(goal, goal, recv_sem).wait())

    def drain(self):
        for when, wait in self.pending:
            guarded(when, wait)


def call(kernel, arguments, outs, out_specs, scratch, number, in_specs=None, vmem=None):
    return pl.pallas_call(
        kernel,
        in_specs=in_specs or [on_chip] * len(arguments),
        out_specs=out_specs,
        out_shape=outs,
        scratch_shapes=scratch,
        compiler_params=pltpu.CompilerParams(
            collective_id=number, has_side_effects=True, vmem_limit_bytes=vmem
        ),
    )(*arguments)


def everyone_kernel(dims, x_ref, o_ref, send_sem, recv_sem):
    wires = Wires(send_sem)
    H, X, C, Z = dims
    total = H * X * C * Z
    at = wires.at
    me = ((at["h"] * X + at["x"]) * C + at["c"]) * Z + at["z"]

    def coordinates(flat):
        return (flat // (X * C * Z), flat // (C * Z) % X, flat // Z % C, flat % Z)

    wires.greet([(None, coordinates((me + k) % total)) for k in range(1, total)])
    for k in range(1, total):
        wires.send(x_ref, o_ref.at[me], recv_sem.at[k], coordinates((me + k) % total))
    o_ref[me] = x_ref[...]
    for k in range(1, total):
        wires.arrived(o_ref.at[(me + total - k) % total], recv_sem.at[k])
    wires.drain()


def gather_everyone(x, dims, number):
    total = dims[0] * dims[1] * dims[2] * dims[3]
    if dims[0] > 2:
        return lax.all_gather(x, ALL, axis=0, tiled=False)
    return call(
        partial(everyone_kernel, dims),
        (x,),
        jax.ShapeDtypeStruct((total,) + x.shape, x.dtype),
        on_chip,
        [pltpu.SemaphoreType.DMA((total,)), pltpu.SemaphoreType.DMA((total,))],
        number,
    )


def team_kernel(dims, split_in, x_ref, o_ref, send_sem, recv_sem):
    H, X, C, Z = dims
    wires = Wires(send_sem)
    at = wires.at
    me = at["x"] * C + at["c"]
    others = [(1 - at["x"], at["c"]), (1 - at["x"], 1 - at["c"]), (at["x"], 1 - at["c"])]
    wires.greet([(None, wires.peer(x=x, c=c)) for x, c in others])
    for x, c in others:
        wires.send(x_ref.at[x * C + c], o_ref.at[me], recv_sem.at[me], wires.peer(x=x, c=c))
    o_ref[me] = x_ref[me]
    for x, c in others:
        wires.arrived(o_ref.at[x * C + c], recv_sem.at[x * C + c])
    wires.drain()


def team_swap(x, dims, number):
    if dims[0] > 2:
        return lax.all_to_all(x, GROUP, split_axis=0, concat_axis=0, tiled=True)
    return call(
        partial(team_kernel, dims, 0),
        (x,),
        jax.ShapeDtypeStruct(x.shape, x.dtype),
        on_chip,
        [pltpu.SemaphoreType.DMA((3,)), pltpu.SemaphoreType.DMA((4,))],
        number,
    )


def contrast(total, counts, queries):
    exact = partial(dot, precision=peak_affinity)
    pooled = total / counts
    scale = lax.rsqrt(jnp.sum(pooled * pooled, -1, keepdims=True) + 1e-06)
    embed = pooled * scale
    half = total.shape[0] // 2
    question, passage = embed[:half], embed[half:]
    scores = exact(question, passage, (1,), (1,)) / sharpness_divisor
    order = lax.broadcasted_iota(jnp.int32, scores.shape, 0)
    target = (order == lax.broadcasted_iota(jnp.int32, scores.shape, 1)).astype(f32)
    weight = (order < queries).astype(f32) / jnp.full(scores.shape, queries).astype(f32)
    peak = jnp.max(scores, -1, keepdims=True)
    shares = jnp.exp(scores - peak)
    mass = jnp.sum(shares, -1, keepdims=True)
    each = peak + jnp.log(mass) - jnp.sum(scores * target, -1, keepdims=True)
    loss = jnp.sum(weight[:, :1] * each)
    slope = (shares / mass - target) * weight
    grad = jnp.concatenate(
        [exact(slope, passage, (1,), (0,)), exact(slope, question, (0,), (0,))], 0
    ) / sharpness_divisor
    grad = scale * (grad - embed * jnp.sum(grad * embed, -1, keepdims=True))
    return loss, grad / counts


def contrast_kernel(dims, queries_ref, hidden_ref, seg_ref, counts_ref, loss_ref, grad_ref, sums_ref, team_ref, all_ref, send_sem, team_sem, recv_sem):
    H, X, C, Z = dims
    wires = Wires(send_sem)
    at = wires.at
    me = at["x"] * C + at["c"]
    row = at["h"] * Z + at["z"]
    rows = H * Z
    others = [(1 - at["x"], at["c"]), (1 - at["x"], 1 - at["c"]), (at["x"], 1 - at["c"])]
    far = [(row + k) % rows for k in range(1, rows)]
    wires.greet(
        [(None, wires.peer(x=x, c=c)) for x, c in others]
        + [(None, wires.peer(h=r // Z, z=r % Z)) for r in far]
    )
    texts, own_len = sums_ref.shape[0], seg_ref.shape[1]
    label = lax.broadcasted_iota(jnp.int32, (texts, own_len), 0)
    member = (label == seg_ref[...]).astype(f32)
    sums_ref[...] = dot(member, hidden_ref[...], (1,), (0,), peak_affinity)
    for x, c in others:
        wires.send(sums_ref, team_ref.at[me], team_sem.at[me], wires.peer(x=x, c=c))
    team_ref[me] = sums_ref[...]
    for x, c in others:
        wires.arrived(team_ref.at[x * C + c], team_sem.at[x * C + c])
    all_ref[row] = (team_ref[0] + team_ref[1]) + (team_ref[2] + team_ref[3])
    for r in far:
        wires.send(all_ref.at[row], all_ref.at[row], recv_sem.at[row], wires.peer(h=r // Z, z=r % Z))
    for r in far:
        wires.arrived(all_ref.at[r], recv_sem.at[r])
    wires.drain()
    width = all_ref.shape[2]
    loss, grad = contrast(all_ref[...].reshape(rows * texts, width), counts_ref[...], queries_ref[0])
    loss_ref[...] = jnp.full(loss_ref.shape, loss)
    all_ref[...] = grad.reshape(rows, texts, width)
    grad_ref[...] = dot(member, all_ref[row], (0,), (0,), peak_affinity)


def contrast_all(hidden, seg_own, counts, queries, dims, number):
    H, X, C, Z = dims
    rows, team = H * Z, X * C
    own_len, width = hidden.shape
    labels = jnp.arange(SEGS, dtype=jnp.int32)
    if H > 2:
        member = (seg_own[None, :] == labels[:, None]).astype(f32)
        sums = jnp.dot(member, hidden, precision=peak_affinity)
        total = lax.all_gather(lax.psum(sums, GROUP), ("h", "z"), axis=0, tiled=True)
        loss, grad = contrast(total, counts, queries[0])
        row = lax.axis_index("h") * Z + lax.axis_index("z")
        grad = lax.dynamic_slice_in_dim(grad, row * SEGS, SEGS, 0)
        return loss, dot(member, grad, (0,), (0,), peak_affinity)
    loss, grad = call(
        partial(contrast_kernel, dims),
        (queries, hidden, seg_own[None, :], counts),
        [jax.ShapeDtypeStruct((8, 128), f32), jax.ShapeDtypeStruct(hidden.shape, f32)],
        [on_chip] * 2,
        [
            pltpu.VMEM((SEGS, width), f32),
            pltpu.VMEM((team, SEGS, width), f32),
            pltpu.VMEM((rows, SEGS, width), f32),
            pltpu.SemaphoreType.DMA((3 + rows,)),
            pltpu.SemaphoreType.DMA((team,)),
            pltpu.SemaphoreType.DMA((rows,)),
        ],
        number,
        in_specs=[pl.BlockSpec(memory_space=pltpu.SMEM)] + [on_chip] * 3,
        vmem=12 * 2**20,
    )
    return loss[0, 0], grad


def fetch_kernel(dims, x_ref, o_ref, send_sem, recv_sem):
    H, X, C, Z = dims
    wires = Wires(send_sem)
    at = wires.at
    h, x, c = at["h"], at["x"], at["c"]
    across, beside = wires.peer(x=1 - x), wires.peer(c=1 - c)
    away = [(h + k) % H for k in range(1, H)]
    wires.greet([(None, across), (None, beside)] + [(None, wires.peer(h=g)) for g in away])
    for g in away:
        wires.send(x_ref.at[g], o_ref.at[x, c, h], recv_sem.at[x, c, h], wires.peer(h=g))
    mine = (o_ref.at[x, c, h], recv_sem.at[x, c, h])
    wires.send(x_ref.at[h], *mine, across)
    wires.send(x_ref.at[h], *mine, beside)
    o_ref[x, c, h] = x_ref[h]
    for g in away:
        place = (o_ref.at[x, c, g], recv_sem.at[x, c, g])
        wires.arrived(*place)
        wires.send(place[0], *place, across)
        wires.send(place[0], *place, beside)
    for g in [h] + away:
        place = (o_ref.at[1 - x, c, g], recv_sem.at[1 - x, c, g])
        wires.arrived(*place)
        wires.send(place[0], *place, beside)
    for y in (x, 1 - x):
        for g in [h] + away:
            wires.arrived(o_ref.at[y, 1 - c, g], recv_sem.at[y, 1 - c, g])
    wires.drain()


def fetch_rows(rows, dims, number):
    H, X, C, Z = dims
    if H > 2:
        got = lax.all_to_all(rows, "h", split_axis=0, concat_axis=0, tiled=True)
        return lax.all_gather(got, GROUP, axis=0, tiled=False)
    return call(
        partial(fetch_kernel, dims),
        (rows,),
        jax.ShapeDtypeStruct((X, C) + rows.shape, rows.dtype),
        on_chip,
        [pltpu.SemaphoreType.DMA((4 * H,)), pltpu.SemaphoreType.DMA((X, C, H))],
        number,
    )


def along_line(wires, piece, recv_sem, extra=None):
    z, Z = wires.at["z"], wires.size_z
    right, left = wires.peer(z=z + 1), wires.peer(z=z - 1)
    for far in range(0, Z):
        for sign, onward, more in ((-1, right, z + 1 < Z), (1, left, z >= 1)):
            spot = z + sign * far
            there = None if far == 0 else (spot >= 0 if sign < 0 else spot < Z)
            for view, sem in zip(piece(spot), recv_sem(spot)):
                if far:
                    wires.arrived(view, sem, there)
                wires.send(view, view, sem, onward, both(there, more))
            if extra is not None and (far or sign < 0):
                extra(spot, there)


def settle_kernel(dims, x_ref, o_ref, beside_ref, across_ref, ready_ref, send_sem, beside_sem, across_sem, recv_sem):
    H, X, C, Z = dims
    wires = Wires(send_sem)
    wires.size_z = Z
    at = wires.at
    h, x, c, z = at["h"], at["x"], at["c"], at["z"]
    across, beside = wires.peer(x=1 - x), wires.peer(c=1 - c)
    away = [(h + k) % H for k in range(1, H)]
    wires.greet(
        [(None, across), (None, beside)]
        + [(None, wires.peer(h=g)) for g in away]
        + [(z + 1 < Z, wires.peer(z=z + 1)), (z >= 1, wires.peer(z=z - 1))]
    )
    for y in (1 - x, x):
        wires.send(x_ref.at[y, 1 - c], beside_ref.at[y], beside_sem.at[y], beside)
    wires.arrived(beside_ref.at[1 - x], beside_sem.at[1 - x])
    for g in away + [h]:
        total = x_ref[1 - x, c, g].astype(f32) + beside_ref[1 - x, g].astype(f32)
        ready_ref[g] = total.astype(ready_ref.dtype)
        wires.send(ready_ref.at[g], across_ref.at[g], across_sem.at[g], across)
    wires.arrived(beside_ref.at[x], beside_sem.at[x])
    for g in away + [h]:
        wires.arrived(across_ref.at[g], across_sem.at[g])
        total = x_ref[x, c, g].astype(f32) + beside_ref[x, g].astype(f32)
        total = (total + across_ref[g].astype(f32)).astype(o_ref.dtype)
        if g is h:
            o_ref[z, h] = total
        else:
            ready_ref[H + g] = total
            wires.send(ready_ref.at[H + g], o_ref.at[z, h], recv_sem.at[z, h], wires.peer(h=g))
    for g in away:
        wires.arrived(o_ref.at[z, g], recv_sem.at[z, g])
    along_line(wires, lambda s: [o_ref.at[s]], lambda s: [recv_sem.at[s, H]])
    wires.drain()


def settle_rows(terms, dims, number):
    H, X, C, Z = dims
    block = terms.shape[3:]
    if H > 2:
        terms = terms.reshape((X * C,) + (H,) + block)
        terms = lax.psum_scatter(terms, GROUP, scatter_dimension=0, tiled=True)[0]
        terms = lax.all_to_all(terms, "h", split_axis=0, concat_axis=0, tiled=True)
        return lax.all_gather(terms, "z", axis=0, tiled=False)
    return call(
        partial(settle_kernel, dims),
        (terms,),
        jax.ShapeDtypeStruct((Z, H) + block, terms.dtype),
        on_chip,
        [
            pltpu.VMEM((X, H) + block, terms.dtype),
            pltpu.VMEM((H,) + block, terms.dtype),
            pltpu.VMEM((2 * H,) + block, terms.dtype),
            pltpu.SemaphoreType.DMA((2 + 2 * H + 2 * Z,)),
            pltpu.SemaphoreType.DMA((X,)),
            pltpu.SemaphoreType.DMA((H,)),
            pltpu.SemaphoreType.DMA((Z, H + 1)),
        ],
        number,
    )


def gather_weights(pieces, dims):
    H, X, C, Z = dims
    rows = pieces[0].shape[0]
    outs = [lax.all_gather(piece, ALL, axis=0, tiled=False) for piece in pieces]
    outs = [whole.reshape(H * X * C, Z, rows, -1).transpose(1, 0, 2, 3) for whole in outs]
    return [whole.reshape(Z, H * X * C * rows, -1) for whole in outs]


def reduce_weights(pieces, dims):
    H, X, C, Z = dims
    batch = H * X * C
    rows = pieces[0].shape[1] // batch
    sums = []
    for piece in pieces:
        piece = piece.reshape(Z, batch, rows, -1).transpose(1, 0, 2, 3)
        piece = piece.reshape(batch * Z, rows, -1)
        sums.append(lax.psum_scatter(piece, ALL, scatter_dimension=0, tiled=True)[0].astype(f32))
    return sums


class Spread:
    def __init__(self, wires, dims, kinds, stages, outs, send_sem, recv_sem):
        self.wires, self.kinds, self.stages, self.outs = wires, kinds, stages, outs
        self.send_sem, self.recv_sem = send_sem, recv_sem
        self.Z = dims[3]
        self.spots = 2 * self.Z - 1

    def where(self, i):
        z = self.wires.at["z"]
        if isinstance(i, int) and i == 0:
            return z, 0, None
        sign = 1 - 2 * (i % 2)
        s = z + sign * ((i + 1) // 2)
        return s, sign, (s >= 0) & (s < self.Z)

    def place(self, a, s, h, x, c):
        return self.outs[a].at[s, h, x, c], self.recv_sem.at[a, s, (h * 2 + x) * 2 + c]

    def moves(self, phase, i):
        at, peer = self.wires.at, self.wires.peer
        h, x, c, z = at["h"], at["x"], at["c"], at["z"]
        s, sign, there = self.where(i)
        beside = peer(c=1 - c)
        moves = []

        def add(a, block, kind, target, when=there):
            view, sem = self.place(a, s, *block)
            fresh = isinstance(i, int) and i == 0 and phase < 2
            source = self.stages[a] if fresh else view
            moves.append((when, source, view, sem, self.send_sem.at[a, kind, i], target))

        for a, kind in enumerate(self.kinds):
            hops = [peer(h=1 - h), peer(x=1 - x)]
            if phase == 0:
                if isinstance(i, int) and i == 0:
                    add(a, (h, x, c), 0, peer(z=z + 1), z + 1 < self.Z)
                    add(a, (h, x, c), 1, peer(z=z - 1), z >= 1)
                else:
                    onward = z - sign
                    add(a, (h, x, c), 0, peer(z=onward), there & (onward >= 0) & (onward < self.Z))
            if phase == 1:
                add(a, (h, x, c), 2, hops[kind])
                add(a, (h, x, c), 3, hops[1 - kind])
                add(a, (h, x, c), 4, beside)
            if phase == 2:
                block = (1 - h, x, c) if kind == 0 else (h, 1 - x, c)
                add(a, block, 5, hops[1 - kind])
                add(a, block, 6, beside)
            if phase == 3:
                add(a, (h, 1 - x, c) if kind == 0 else (1 - h, x, c), 7, beside)
                add(a, (1 - h, 1 - x, c), 8, beside)
        return moves

    def copy(self, move):
        return pltpu.make_async_remote_copy(
            src_ref=move[1],
            dst_ref=move[2],
            send_sem=move[4],
            recv_sem=move[3],
            device_id=move[5],
            device_id_type=MESH,
        )

    def wait(self, phase, i):
        at = self.wires.at
        h, x, c = at["h"], at["x"], at["c"]
        s, _, there = self.where(i)
        for a, kind in enumerate(self.kinds):
            if phase == 0:
                blocks = [] if isinstance(i, int) and i == 0 else [(h, x, c)]
            elif phase == 1:
                blocks = []
            elif phase == 2:
                blocks = [(1 - h, x, c) if kind == 0 else (h, 1 - x, c)]
            elif phase == 3:
                blocks = [(h, 1 - x, c) if kind == 0 else (1 - h, x, c), (1 - h, 1 - x, c)]
            else:
                blocks = [(g, y, 1 - c) for g in range(2) for y in range(2)]
            for block in blocks:
                self.wires.arrived(*self.place(a, s, *block), there)

    def step(self, phase, i):
        self.wait(phase, i)
        if phase < 4:
            for move in self.moves(phase, i):
                guarded(move[0], lambda move=move: self.copy(move).start())

    def run(self, phases, first, last):
        if first == 0:
            for phase in phases:
                self.step(phase, 0)
        low = max(first, 1)
        if low < last:

            @pl.loop(low, last)
            def _(i):
                for phase in phases:
                    self.step(phase, i)

    def settle(self):
        def sent(i):
            for phase in (0, 1, 2, 3):
                for move in self.moves(phase, i):
                    guarded(move[0], lambda move=move: self.copy(move).wait_send())

        sent(0)

        @pl.loop(1, self.spots)
        def _(i):
            sent(i)


class Late:
    def __init__(self, wires, dims, stage, out, send_sem, recv_sem):
        self.wires, self.stage, self.out = wires, stage, out
        self.send_sem, self.recv_sem, self.Z = send_sem, recv_sem, dims[3]
        self.spots = 2 * self.Z - 1

    def where(self, i):
        z = self.wires.at["z"]
        if isinstance(i, int) and i == 0:
            return z, 0, None
        sign = 1 - 2 * (i % 2)
        s = z + sign * ((i + 1) // 2)
        return s, sign, (s >= 0) & (s < self.Z)

    def line(self, s, c):
        return self.out.at[s, :, :, c]

    def moves(self, i):
        at, peer = self.wires.at, self.wires.peer
        h, x, c, z = at["h"], at["x"], at["c"], at["z"]
        sent, got = self.send_sem, self.recv_sem
        if isinstance(i, str) and i == "across":
            view = self.out.at[z, h, x, c]
            return [(None, self.stage, view, sent.at[0, 0], got.at[0, 0], peer(x=1 - x))]
        if isinstance(i, str) and i == "away":
            view = self.out.at[z, h, :, c]
            return [(None, view, view, sent.at[0, 1], got.at[0, 1], peer(h=1 - h))]
        s, sign, there = self.where(i)
        view = self.line(s, c)
        if isinstance(i, int) and i == 0:
            moves = [
                (z + 1 < self.Z, view, view, sent.at[1, 0], got.at[1, s], peer(z=z + 1)),
                (z >= 1, view, view, sent.at[0, 2], got.at[1, s], peer(z=z - 1)),
            ]
        else:
            onward = z - sign
            when = there & (onward >= 0) & (onward < self.Z)
            moves = [(when, view, view, sent.at[1, i], got.at[1, s], peer(z=onward))]
        return moves + [(there, view, view, sent.at[2, i], got.at[2, s], peer(c=1 - c))]

    def copy(self, move):
        return pltpu.make_async_remote_copy(
            src_ref=move[1],
            dst_ref=move[2],
            send_sem=move[3],
            recv_sem=move[4],
            device_id=move[5],
            device_id_type=MESH,
        )

    def step(self, i):
        at = self.wires.at
        h, x, c, z = at["h"], at["x"], at["c"], at["z"]
        if isinstance(i, str) and i == "away":
            self.wires.arrived(self.out.at[z, h, 1 - x, c], self.recv_sem.at[0, 0])
        elif isinstance(i, int) and i == 0:
            self.wires.arrived(self.out.at[z, 1 - h, :, c], self.recv_sem.at[0, 1])
        elif not isinstance(i, str):
            s, _, there = self.where(i)
            self.wires.arrived(self.line(s, c), self.recv_sem.at[1, s], there)
        for move in self.moves(i):
            guarded(move[0], lambda move=move: self.copy(move).start())

    def settle(self):
        def sent(i):
            for move in self.moves(i):
                guarded(move[0], lambda move=move: self.copy(move).wait_send())

        for i in ("across", "away", 0):
            sent(i)

        @pl.loop(1, self.spots)
        def _(i):
            sent(i)

        @pl.loop(0, self.Z)
        def _(s):
            self.wires.arrived(self.line(s, 1 - self.wires.at["c"]), self.recv_sem.at[2, s])


def selection(rows, columns, shift):
    row = lax.broadcasted_iota(jnp.int32, (rows, columns), 0)
    column = lax.broadcasted_iota(jnp.int32, (rows, columns), 1)
    return (column == row + shift).astype(bf16)


def turned(values, cosine, sine):
    half = HEAD_DIM // 2
    lanes = values.shape[1]
    lane = lax.broadcasted_iota(jnp.int32, values.shape, 1) % HEAD_DIM
    after = pltpu.roll(values, lanes - half, 1)
    before = pltpu.roll(values, half, 1)
    wide = lambda t: jnp.concatenate([t] * (lanes // t.shape[1]), 1)
    return values * wide(cosine) + jnp.where(lane < half, -after, before) * wide(sine)


def attend_block(query, keys, values, same, heads):
    lane = lax.broadcasted_iota(jnp.int32, query.shape, 1) // HEAD_DIM
    result = jnp.zeros(query.shape, f32)
    for head in range(heads):
        own = jnp.where(lane == head, query, jnp.zeros_like(query))
        scores = dot(own, keys, (1,), (1,)) * HEAD_DIM ** (-0.5)
        scores = jnp.where(same, scores, negative)
        weights = jnp.exp(scores - jnp.max(scores, 1, keepdims=True))
        probs = (weights * (1.0 / jnp.sum(weights, 1, keepdims=True))).astype(bf16)
        result = jnp.where(lane == head, dot(probs, values, (1,), (0,)), result)
    return result.astype(bf16)


def front_kernel(
    dims,
    rows_ref,
    slot_ref,
    more_ref,
    cos_ref,
    sin_ref,
    segq_ref,
    segk_ref,
    *refs,
):
    ins, outs, (x_ref, q_ref, k_ref, v_ref, swap_ref), stages = refs[:5], refs[5:10], refs[10:15], refs[15:20]
    (
        got_ref,
        heads_ref,
        pick_ref,
        send_ref,
        load_sem,
        store_sem,
        main_send,
        main_recv,
        small_send,
        small_recv,
        late_send,
        late_recv,
        row_send,
        row_recv,
        heads_sem,
        swap_send,
        swap_recv,
    ) = refs[20:]
    H, X, C, Z = dims
    wires = Wires(row_send)
    at = wires.at
    h, x, c, z = at["h"], at["x"], at["c"], at["z"]
    across, beside, away = wires.peer(x=1 - x), wires.peer(c=1 - c), wires.peer(h=1 - h)
    team = x * C + c
    wires.greet(
        [(None, across), (None, beside), (None, away), (None, wires.peer(x=1 - x, c=1 - c))]
        + [(z + 1 < Z, wires.peer(z=z + 1)), (z >= 1, wires.peer(z=z - 1))]
    )
    loads = [pltpu.make_async_copy(ins[i], stages[i], load_sem.at[i]) for i in range(5)]
    stores = [
        pltpu.make_async_copy(stages[i], outs[i].at[z, h, x, c], store_sem.at[i]) for i in range(5)
    ]
    for load in loads:
        load.start()

    def owner_rows(y, d, g):
        return got_ref.at[y, d, g], row_recv.at[y, d, g]

    wires.send(rows_ref.at[1 - h], *owner_rows(x, c, h), away)
    wires.send(rows_ref.at[h], *owner_rows(x, c, h), across)
    wires.send(rows_ref.at[h], *owner_rows(x, c, h), beside)
    got_ref[x, c, h] = rows_ref[h]
    for load, store in zip(loads, stores):
        load.wait()
        store.start()
    small = Spread(wires, dims, [1], stages[:1], outs[:1], small_send, small_recv)
    main = Spread(wires, dims, [0, 0, 1], stages[1:4], outs[1:4], main_send, main_recv)
    late = Late(wires, dims, stages[4], outs[4], late_send, late_recv)
    spots = main.spots
    small.run((0, 1), 0, 1)
    late.step("across")
    main.run((0,), 0, 1)
    small.run((0, 1), 1, 3)
    place = owner_rows(x, c, 1 - h)
    wires.arrived(*place)
    wires.send(place[0], *place, across)
    wires.send(place[0], *place, beside)
    small.run((2,), 0, 1)
    main.run((0,), 1, 3)
    stores[4].wait()
    late.step("away")
    small.run((0, 1), 3, 5)
    small.run((2,), 1, 3)
    for g in (h, 1 - h):
        place = owner_rows(1 - x, c, g)
        wires.arrived(*place)
        wires.send(place[0], *place, beside)
    small.run((3,), 0, 1)
    small.run((0, 1), 5, spots)
    main.run((0,), 3, 5)
    small.run((2,), 3, 5)
    small.run((3,), 1, 3)
    late.step(0)
    small.run((2,), 5, spots)
    main.run((1,), 0, 3)
    main.run((0,), 5, spots)
    main.run((1,), 3, spots)
    small.run((3,), 3, spots)
    stores[0].wait()
    small.run((4,), 0, spots)
    heads = pltpu.make_async_copy(outs[0].at[team], heads_ref, heads_sem)
    heads.start()
    for y in (x, 1 - x):
        for g in (h, 1 - h):
            wires.arrived(*owner_rows(y, 1 - c, g))
    heads.wait()

    length, width = x_ref.shape
    heads_width = send_ref.shape[1]
    lanes = q_ref.shape[1]
    merged = heads_ref[...].reshape(width, heads_ref.shape[-1])
    for part in range(3):
        choose = selection(lanes, 3 * heads_width, part * heads_width)
        row = lax.broadcasted_iota(jnp.int32, choose.shape, 0)
        choose = jnp.where(row < heads_width, choose, jnp.zeros_like(choose))
        pick_ref[part] = dot(merged, choose, (1,), (1,)).astype(bf16)
    block = min(256, length)
    blocks = length // block
    slots = got_ref.shape[0] * got_ref.shape[1] * got_ref.shape[2] * got_ref.shape[3]

    @pl.loop(0, blocks)
    def _(i):
        here = pl.ds(pl.multiple_of(i * block, block), block)
        slot = lax.broadcasted_iota(jnp.int32, (block, slots), 1)
        chosen = (slot_ref[here, :] == slot).astype(bf16)
        full = dot(chosen, got_ref[...].reshape(slots, width), (1,), (0,))
        low = (full + more_ref[here, :].astype(f32)).astype(bf16)
        x_ref[here, :] = low
        cosine, sine = cos_ref[here, :], sin_ref[here, :]
        q_ref[here, :] = turned(dot(low, pick_ref[0], (1,), (0,)), cosine, sine).astype(bf16)
        k_ref[here, :] = turned(dot(low, pick_ref[1], (1,), (0,)), cosine, sine).astype(bf16)
        v_ref[here, :] = dot(low, pick_ref[2], (1,), (0,)).astype(bf16)

        @pl.when(i == 2)
        def _():
            late.step(1)
            late.step(2)

    main.run((2,), 0, 3)
    own_len = length // (X * C)

    @pl.loop(0, blocks)
    def _(i):
        here = pl.ds(pl.multiple_of(i * block, block), block)
        same = segq_ref[here, :] == segk_ref[...]
        heads = heads_width // HEAD_DIM
        result = attend_block(q_ref[here, :], k_ref[...], v_ref[...], same, heads)
        send_ref[here, :] = result[:, :heads_width]

        @pl.when((i == 0) | (i == 2))
        def _():
            main.step(2, i + 3)
            main.step(2, i + 4)

        @pl.when(i == 1)
        def _():
            late.step(3)
            late.step(4)

        pl.when(i == 3)(lambda: main.step(3, 0))
        pl.when(i == 4)(lambda: main.step(3, 1))

    others = [(1 - x, c), (1 - x, 1 - c), (x, 1 - c)]

    def part_of(y, d):
        return send_ref.at[pl.ds(pl.multiple_of((y * C + d) * own_len, 128), own_len), :]

    swaps = [
        pltpu.make_async_remote_copy(
            src_ref=part_of(y, d),
            dst_ref=swap_ref.at[team],
            send_sem=swap_send.at[k],
            recv_sem=swap_recv.at[team],
            device_id=wires.peer(x=y, c=d),
            device_id_type=MESH,
        )
        for k, (y, d) in enumerate(others)
    ]
    for swap in swaps:
        swap.start()
    swap_ref[team] = send_ref[pl.ds(pl.multiple_of(team * own_len, 128), own_len), :]
    late.step(5)
    late.step(6)
    main.run((3,), 2, spots)
    main.run((4,), 0, spots)
    for y, d in others:
        wires.arrived(swap_ref.at[y * C + d], swap_recv.at[y * C + d])
    for swap in swaps:
        swap.wait_send()
    for store in stores[1:4]:
        store.wait()
    late.settle()
    main.settle()
    small.settle()
    wires.drain()


def front(rows, slot, more, cosine, sine, segments, pieces, heads_width, dims, number):
    H, X, C, Z = dims
    length, width = more.shape
    team = X * C
    spots = 2 * Z - 1
    batch = H * team
    rows_in = pieces[0].shape[0]
    lanes = -(-heads_width // 128) * 128
    vmem = lambda shape, dtype=bf16: pltpu.VMEM(shape, dtype)
    dma = lambda *shape: pltpu.SemaphoreType.DMA(shape)
    outs = call(
        partial(front_kernel, dims),
        (rows, slot[:, None], more, cosine, sine, segments[:, None], segments[None, :], *pieces),
        [jax.ShapeDtypeStruct((Z, H, X, C) + piece.shape, bf16) for piece in pieces]
        + [jax.ShapeDtypeStruct((length, width), bf16)]
        + [jax.ShapeDtypeStruct((length, lanes), bf16)] * 3
        + [jax.ShapeDtypeStruct((team, length // team, heads_width), bf16)],
        [anywhere] * 5 + [on_chip] * 5,
        [vmem(piece.shape) for piece in pieces]
        + [
            vmem((X, C) + rows.shape),
            vmem((H, X, C) + pieces[0].shape),
            vmem((3, width, lanes)),
            vmem((length, heads_width)),
            dma(5),
            dma(5),
            dma(3, 9, spots),
            dma(3, Z, batch),
            dma(1, 9, spots),
            dma(1, Z, batch),
            dma(3, spots),
            dma(3, Z),
            dma(7),
            dma(X, C, H),
            pltpu.SemaphoreType.DMA,
            dma(3),
            dma(team),
        ],
        number,
        in_specs=[on_chip] * 7 + [anywhere] * 5,
        vmem=60 * 2**20,
    )
    weights = [whole.reshape(Z, batch * rows_in, -1) for whole in outs[:5]]
    return weights, outs[5:]


def sum_rows(goal, sources):
    rows = goal.shape[0]
    step = 16 if rows % 16 == 0 else rows

    @pl.loop(0, rows // step)
    def _(i):
        part = pl.ds(pl.multiple_of(i * step, step), step)
        value = sources[0][part, :].astype(f32)
        for source in sources[1:]:
            value += source[part, :].astype(f32)
        goal[part, :] = value.astype(goal.dtype)


class Line:
    def __init__(self, wires, Z, buffers, send_sem, recv_sem):
        self.wires, self.Z, self.buffers = wires, Z, buffers
        self.send_sem, self.recv_sem = send_sem, recv_sem

    def onward(self, a, s, source):
        z = self.wires.at["z"]
        upward = z < s
        goal = jnp.where(upward, z + 1, z - 1)
        index = jnp.where((s < goal) | upward, s, self.Z)
        return pltpu.make_async_remote_copy(
            src_ref=source,
            dst_ref=self.buffers[a].at[index],
            send_sem=self.send_sem.at[a, s],
            recv_sem=self.recv_sem.at[a, index],
            device_id=self.wires.peer(z=goal),
            device_id_type=MESH,
        )

    def step(self, a, s, sources, running, final):
        z, Z = self.wires.at["z"], self.Z

        def took(index):
            view = self.buffers[a].at[index]
            self.wires.arrived(view, self.recv_sem.at[a, index])
            return view

        passing = z != s
        edge = ((z < s) & (z == 0)) | ((z > s) & (z == Z - 1))

        @pl.when(passing & edge)
        def _():
            sum_rows(running, sources)

        @pl.when(passing & ~edge)
        def _():
            sum_rows(running, sources + [took(s)])

        @pl.when(passing)
        def _():
            self.onward(a, s, running).start()

        @pl.when((z == s) & (z == 0))
        def _():
            sum_rows(final, sources + [took(Z)])

        @pl.when((z == s) & (z == Z - 1))
        def _():
            sum_rows(final, sources + [took(s)])

        @pl.when((z == s) & (z > 0) & (z < Z - 1))
        def _():
            sum_rows(final, sources + [took(s), took(Z)])

    def settle(self, a, s, running):
        @pl.when(self.wires.at["z"] != s)
        def _():
            self.onward(a, s, running).wait_send()


class Gathering:
    def __init__(self, wires, dims, kinds, ins, outs, own, near, first, second, lines, sems):
        self.wires, self.kinds, self.Z = wires, kinds, dims[3]
        self.ins, self.outs, self.own, self.near = ins, outs, own, near
        self.first, self.second = first, second
        self.load_sem, self.near_sem, self.first_sem, self.second_sem = sems[:4]
        self.near_send, self.first_send, self.second_send = sems[4:7]
        self.line = Line(wires, dims[3], lines, sems[7], sems[8])
        at = wires.at
        self.x, self.h, self.c, self.z = at["x"], at["h"], at["c"], at["z"]
        self.across, self.beside = wires.peer(x=1 - self.x), wires.peer(c=1 - self.c)
        self.away = wires.peer(h=1 - self.h)

    def turn(self, i):
        Z = self.Z
        low = self.z < Z // 2
        side = jnp.where(low, self.z, Z - 1 - self.z)
        s = jnp.where(i < Z - 1 - side, Z - 1 - i, jnp.where(i < Z - 1, i - (Z - 1 - side), side))
        return jnp.where(low, s, Z - 1 - s)

    def remote(self, source, goal, send_sem, recv_sem, target):
        return pltpu.make_async_remote_copy(
            src_ref=source,
            dst_ref=goal,
            send_sem=send_sem,
            recv_sem=recv_sem,
            device_id=target,
            device_id_type=MESH,
        )

    def load(self, a, s):
        return pltpu.make_async_copy(
            self.ins[a].at[s, :, :, self.c], self.own[a].at[s], self.load_sem.at[a, s]
        )

    def near_copy(self, a, s):
        return self.remote(
            self.ins[a].at[s, :, :, 1 - self.c],
            self.near[a].at[s],
            self.near_send.at[a, s],
            self.near_sem.at[a, s],
            self.beside,
        )

    def axes(self, a):
        return (self.x, self.h) if self.kinds[a] == 0 else (self.h, self.x)

    def spot(self, a, s, f, g):
        return (s, g, f) if self.kinds[a] == 0 else (s, f, g)

    def first_copy(self, a, s, g):
        f, _ = self.axes(a)
        return self.remote(
            self.own[a].at[self.spot(a, s, 1 - f, g)],
            self.first[a].at[s, g],
            self.first_send.at[a, s, g],
            self.first_sem.at[a, s, g],
            self.across if self.kinds[a] == 0 else self.away,
        )

    def second_copy(self, a, s):
        f, g = self.axes(a)
        return self.remote(
            self.own[a].at[self.spot(a, s, f, 1 - g)],
            self.second[a].at[s],
            self.second_send.at[a, s],
            self.second_sem.at[a, s],
            self.away if self.kinds[a] == 0 else self.across,
        )

    def begin(self):
        @pl.loop(0, self.Z)
        def _(i):
            s = self.turn(i)
            for a in range(len(self.kinds)):
                self.near_copy(a, s).start()
                self.load(a, s).start()

    def one(self, i):
        s = self.turn(i)
        for a in range(len(self.kinds)):
            self.wires.arrived(self.near[a].at[s], self.near_sem.at[a, s])
            self.load(a, s).wait()
            f, g = self.axes(a)
            for k in (1 - g, g):
                place = self.spot(a, s, 1 - f, k)
                sum_rows(self.own[a].at[place], [self.own[a].at[place], self.near[a].at[place]])
                self.first_copy(a, s, k).start()

    def two(self, i):
        s = self.turn(i)
        for a in range(len(self.kinds)):
            f, g = self.axes(a)
            for k in (1 - g, g):
                self.wires.arrived(self.first[a].at[s, k], self.first_sem.at[a, s, k])
            place = self.spot(a, s, f, 1 - g)
            sum_rows(
                self.own[a].at[place],
                [self.own[a].at[place], self.near[a].at[place], self.first[a].at[s, 1 - g]],
            )
            self.second_copy(a, s).start()

    def three(self, i):
        s = self.turn(i)
        for a in range(len(self.kinds)):
            f, g = self.axes(a)
            self.wires.arrived(self.second[a].at[s], self.second_sem.at[a, s])
            place = self.spot(a, s, f, g)
            own = self.own[a].at[place]
            sources = [own, self.near[a].at[place], self.first[a].at[s, g], self.second[a].at[s]]
            self.line.step(a, s, sources, own, self.outs[a])

    def settle(self):
        @pl.loop(0, self.Z)
        def _(s):
            for a in range(len(self.kinds)):
                self.near_copy(a, s).wait_send()
                for k in range(2):
                    self.first_copy(a, s, k).wait_send()
                self.second_copy(a, s).wait_send()
                f, g = self.axes(a)
                self.line.settle(a, s, self.own[a].at[self.spot(a, s, f, g)])


def attend_back_block(query, grad, keys, values, same, heads, dk_ref, dv_ref):
    factor = HEAD_DIM ** (-0.5)
    lane = lax.broadcasted_iota(jnp.int32, query.shape, 1) // HEAD_DIM
    result = jnp.zeros(query.shape, f32)
    for head in range(heads):
        own = jnp.where(lane == head, query, jnp.zeros_like(query))
        own_grad = jnp.where(lane == head, grad, jnp.zeros_like(grad))
        scores = dot(keys, own, (1,), (1,)) * factor
        scores = jnp.where(same, scores, negative)
        weights = jnp.exp(scores - jnp.max(scores, 0, keepdims=True))
        probs = weights * (1.0 / jnp.sum(weights, 0, keepdims=True))
        grad_probs = dot(values, own_grad, (1,), (1,))
        inner = jnp.sum(probs * grad_probs, 0, keepdims=True)
        grad_scores = (probs * (grad_probs - inner)).astype(bf16)
        dk_ref[...] += dot(grad_scores, own, (1,), (0,)) * factor
        dv_ref[...] += dot(probs.astype(bf16), own_grad, (1,), (0,))
        result = jnp.where(lane == head, dot(grad_scores, keys, (0,), (0,)) * factor, result)
    return result


def back_kernel(
    dims,
    heads,
    swap_ref,
    q_ref,
    k_ref,
    v_ref,
    x_ref,
    cos_ref,
    sin_ref,
    segq_ref,
    segk_ref,
    slot_ref,
    first_ref,
    listq_ref,
    listk_ref,
    heads_ref,
    in_gate,
    in_up,
    in_down,
    in_misc,
    out_gate,
    out_up,
    out_down,
    out_misc,
    out_qkv,
    spread_ref,
    zero_ref,
    total_ref,
    *scratch,
):
    H, X, C, Z = dims
    scratch = list(scratch)
    take = lambda n: [scratch.pop(0) for _ in range(n)]
    own, near, first, second, lines = (take(4) for _ in range(5))
    (got_ref, grad_ref, dk_ref, dv_ref, low_ref, matrix_ref, heads_v) = take(7)
    (qsrc, qnear, qx, qh, qtot, qline) = take(6)
    (slots_ref, beside_ref, across_ref, ready_ref) = take(4)
    sems = take(9)
    (swap_send, swap_recv, heads_sem, qsend, qrecv, qline_send, qline_recv) = take(7)
    (row_send, beside_sem, across_sem, row_recv, norm_ref, norm_send, norm_recv) = take(7)
    wires = Wires(row_send)
    wires.size_z = Z
    at = wires.at
    h, x, c, z = at["h"], at["x"], at["c"], at["z"]
    across, beside, away = wires.peer(x=1 - x), wires.peer(c=1 - c), wires.peer(h=1 - h)
    team = x * C + c
    devices = H * X * C * Z
    me = (team + h * X * C) * Z + z

    def coordinates(flat):
        return (flat // (X * C * Z), flat // (C * Z) % X, flat // Z % C, flat % Z)

    wires.greet([(None, coordinates((me + k) % devices)) for k in range(1, devices)])
    others = [(1 - x, c), (1 - x, 1 - c), (x, 1 - c)]
    swaps = [
        pltpu.make_async_remote_copy(
            src_ref=swap_ref.at[y * C + d],
            dst_ref=got_ref.at[team],
            send_sem=swap_send.at[k],
            recv_sem=swap_recv.at[team],
            device_id=wires.peer(x=y, c=d),
            device_id_type=MESH,
        )
        for k, (y, d) in enumerate(others)
    ]
    for swap in swaps:
        swap.start()
    fetch = pltpu.make_async_copy(heads_ref.at[team], heads_v, heads_sem)
    fetch.start()
    job = Gathering(
        wires,
        dims,
        [1, 1, 0, 0],
        [in_gate, in_up, in_down, in_misc],
        [out_gate, out_up, out_down, out_misc],
        own,
        near,
        first,
        second,
        lines,
        sems,
    )
    job.begin()
    got_ref[team] = swap_ref[team]
    dk_ref[...] = jnp.zeros_like(dk_ref)
    dv_ref[...] = jnp.zeros_like(dv_ref)
    matrix_ref[...] = jnp.zeros_like(matrix_ref)
    length, lanes = q_ref.shape
    heads_width = got_ref.shape[2]
    own_len = got_ref.shape[1]
    width = x_ref.shape[1]
    edge = (z == 0) | (z == Z - 1)
    job.one(0)
    widen = selection(heads_width, lanes, 0)
    for y, d in others:
        wires.arrived(got_ref.at[y * C + d], swap_recv.at[y * C + d])
    job.one(1)

    @pl.loop(0, X * C)
    def _(k):
        part = pl.ds(pl.multiple_of(k * own_len, 128), own_len)
        grad_ref[part, :] = dot(got_ref[k], widen, (1,), (0,)).astype(bf16)

    block = min(256, length)
    blocks = length // block

    def narrow(values, part):
        choose = selection(lanes, 3 * heads_width, part * heads_width)
        row = lax.broadcasted_iota(jnp.int32, choose.shape, 0)
        choose = jnp.where(row < heads_width, choose, jnp.zeros_like(choose))
        return dot(values.astype(bf16), choose, (1,), (0,))

    @pl.loop(0, blocks)
    def _(i):
        here = pl.ds(pl.multiple_of(i * block, block), block)
        same = segk_ref[...] == segq_ref[:, here]
        grad_query = attend_back_block(
            q_ref[here, :], grad_ref[here, :], k_ref[...], v_ref[...], same, heads, dk_ref, dv_ref
        )
        low_ref[here, :] = narrow(turned(grad_query, cos_ref[here, :], -sin_ref[here, :]), 0).astype(bf16)

        pl.when((i == 1) | (i == 3))(lambda: job.two(i // 2))
        pl.when((i == 2) | (i == 5))(lambda: job.one(2 + i // 5))
        pl.when((i == 4) & edge)(lambda: job.three(0))

    fetch.wait()

    @pl.loop(0, X * C)
    def _(k):
        part = pl.ds(pl.multiple_of(k * own_len, 128), own_len)
        grad_keys = turned(dk_ref[part, :], cos_ref[part, :], -sin_ref[part, :])
        low = low_ref[part, :].astype(f32) + narrow(grad_keys, 1) + narrow(dv_ref[part, :], 2)
        low = low.astype(bf16)
        zero = dot(low, heads_v[...], (1,), (1,))
        zero_ref[part, :] = (zero + (k == team).astype(f32) * first_ref[...]).astype(bf16)
        matrix_ref[...] += dot(x_ref[part, :], low, (0,), (0,))
        pl.when(k == 1)(lambda: job.two(2))
        pl.when(k == 2)(lambda: job.three(edge.astype(jnp.int32)))

    capacity = slots_ref.shape[3]

    def fill(y, d):
        for g in range(H):
            slot = lax.broadcasted_iota(jnp.int32, (capacity, length), 0)
            slot += ((y * C + d) * H + g) * capacity
            chosen = (slot_ref[...] == slot).astype(bf16)
            slots_ref[y, d, g] = dot(chosen, zero_ref[...], (1,), (0,)).astype(bf16)

    def row_copy(y):
        wires.send(slots_ref.at[y, 1 - c], beside_ref.at[y], beside_sem.at[y], beside)

    fill(1 - x, 1 - c)
    row_copy(1 - x)
    fill(x, 1 - c)
    row_copy(x)
    fill(1 - x, c)
    wires.arrived(beside_ref.at[1 - x], beside_sem.at[1 - x])
    for g in (1 - h, h):
        total = slots_ref[1 - x, c, g].astype(f32) + beside_ref[1 - x, g].astype(f32)
        ready_ref[g] = total.astype(bf16)
        wires.send(ready_ref.at[g], across_ref.at[g], across_sem.at[g], across)
    fill(x, c)
    rows_in, wide = qsrc.shape[3], qsrc.shape[4]
    qsrc[...] = matrix_ref[...].astype(bf16).reshape(qsrc.shape)

    def qcopy(source, goal, k, target):
        return pltpu.make_async_remote_copy(
            src_ref=source,
            dst_ref=goal,
            send_sem=qsend.at[k],
            recv_sem=qrecv.at[k],
            device_id=target,
            device_id_type=MESH,
        )

    qcopies = [
        qcopy(qsrc.at[:, :, 1 - c], qnear, 0, beside),
        qcopy(qsrc.at[:, 1 - x, c], qx.at[0], 1, across),
        qcopy(qnear.at[:, 1 - x], qx.at[1], 2, across),
        qcopy(qsrc.at[1 - h, x, c], qh.at[0], 3, away),
        qcopy(qnear.at[1 - h, x], qh.at[1], 4, away),
        qcopy(qx.at[0, 1 - h], qh.at[2], 5, away),
        qcopy(qx.at[1, 1 - h], qh.at[3], 6, away),
    ]
    qcopies[0].start()
    wires.arrived(beside_ref.at[x], beside_sem.at[x])
    job.three(2)
    pl.when(~edge)(lambda: job.three(1))
    for g in (1 - h, h):
        wires.arrived(across_ref.at[g], across_sem.at[g])
        total = slots_ref[x, c, g].astype(f32) + beside_ref[x, g].astype(f32)
        total = (total + across_ref[g].astype(f32)).astype(bf16)
        if g is h:
            spread_ref[z, h] = total
        else:
            ready_ref[2 + g] = total
            wires.send(ready_ref.at[2 + g], spread_ref.at[z, h], row_recv.at[z, h], away)
    wires.arrived(qnear, qrecv.at[0])
    for k in range(1, 5):
        qcopies[k].start()
    job.two(3)
    wires.arrived(spread_ref.at[z, 1 - h], row_recv.at[z, 1 - h])

    def row_line(far):
        for sign in (-1, 1):
            spot = z + sign * far
            onward = z - sign
            more = (onward >= 0) & (onward < Z)
            there = None if far == 0 else (spot >= 0) & (spot < Z)
            if far:
                wires.arrived(spread_ref.at[spot], row_recv.at[spot, H], there)
            wires.send(
                spread_ref.at[spot], spread_ref.at[spot], row_recv.at[spot, H], wires.peer(z=onward), both(there, more)
            )

    row_line(0)
    for k in (1, 2):
        wires.arrived(qx.at[k - 1], qrecv.at[k])
    qcopies[5].start()
    qcopies[6].start()
    row_line(1)
    for k in range(4):
        wires.arrived(qh.at[k], qrecv.at[3 + k])
    terms = [qsrc.at[h, x, c], qnear.at[h, x], qx.at[0, h], qx.at[1, h]]
    pair = (team, x * C + 1 - c, (1 - x) * C + c, (1 - x) * C + 1 - c)
    for k in range(4):
        sum_rows(qtot.at[pair[k]], [terms[k], qh.at[k]])
    line = Line(wires, Z, [qline], qline_send, qline_recv)

    def heads_line(i):
        s = job.turn(i)
        line.step(0, s, [qtot.at[s]], qtot.at[s], out_qkv)

    pl.loop(0, 2)(heads_line)
    for far in range(2, Z - 1):
        row_line(far)
    pl.loop(2, Z - 1)(heads_line)
    row_line(Z - 1)
    heads_line(Z - 1)
    job.three(3)
    quarter = H * capacity
    mine = pl.ds(pl.multiple_of(z * quarter, 8), quarter)
    products = dot(
        spread_ref[z].reshape(quarter, width), spread_ref[...].reshape(Z * quarter, width), (1,), (1,)
    )
    squares = jnp.sum(jnp.where(listq_ref[mine, :] == listk_ref[...], products, 0.0))
    for ref in (out_gate, out_up, out_down, out_qkv):
        squares += jnp.sum(ref[...] * ref[...])
    lane = lax.broadcasted_iota(jnp.int32, out_misc.shape, 1)
    squares += jnp.sum(out_misc[...] * out_misc[...] * jnp.where(lane < heads_width, 1.0, 1.0 / Z))
    norm_ref[me] = jnp.full(norm_ref.shape[1:], squares)

    @pl.loop(0, Z)
    def _(s):
        line.settle(0, s, qtot.at[s])

    for copy in qcopies:
        copy.wait_send()
    for swap in swaps:
        swap.wait_send()
    job.settle()
    wires.drain()
    tell = [
        pltpu.make_async_remote_copy(
            src_ref=norm_ref.at[me],
            dst_ref=norm_ref.at[me],
            send_sem=norm_send.at[k],
            recv_sem=norm_recv.at[k],
            device_id=coordinates((me + k) % devices),
            device_id_type=MESH,
        )
        for k in range(1, devices)
    ]
    for copy in tell:
        copy.start()
    for k in range(1, devices):
        wires.arrived(norm_ref.at[(me + devices - k) % devices], norm_recv.at[k])
    total_ref[...] = jnp.sum(norm_ref[...], 0)
    for copy in tell:
        copy.wait_send()


def back(swap, q, k, v, x_low, cosine, sine, segments, slot, listed, grad_first, w_heads, terms, heads, capacity, dims, number):
    H, X, C, Z = dims
    length, width = x_low.shape
    lanes = q.shape[1]
    team, own_len, heads_width = swap.shape
    batch = H * team
    rows = width // batch
    widths = [term.shape[2] for term in terms]
    wide = 3 * heads_width
    vmem = lambda shape, dtype=bf16: pltpu.VMEM(shape, dtype)
    dma = lambda *shape: pltpu.SemaphoreType.DMA(shape)
    shapes = [(Z, H, X), (Z, H, X), (Z, 2), (Z,), (Z + 1,)]
    n = len(terms)
    return call(
        partial(back_kernel, dims, heads),
        (
            swap,
            q,
            k,
            v,
            x_low,
            cosine,
            sine,
            segments[None, :],
            segments[:, None],
            slot[None, :],
            grad_first,
            listed[:, None],
            listed[None, :],
            w_heads,
            *(term.reshape(Z, H, X, C, rows, -1) for term in terms),
        ),
        [jax.ShapeDtypeStruct((rows, w), f32) for w in widths + [wide]]
        + [
            jax.ShapeDtypeStruct((Z, H, capacity, width), bf16),
            jax.ShapeDtypeStruct((length, width), bf16),
            jax.ShapeDtypeStruct((8, 128), f32),
        ],
        [on_chip] * 8,
        [vmem(shape + (rows, w)) for shape in shapes for w in widths]
        + [
            vmem(swap.shape),
            vmem((length, lanes)),
            vmem((length, lanes), f32),
            vmem((length, lanes), f32),
            vmem((length, wide)),
            vmem((width, wide), f32),
            vmem(w_heads.shape[1:]),
            vmem((H, X, C, rows, wide)),
            vmem((H, X, rows, wide)),
            vmem((2, H, rows, wide)),
            vmem((4, rows, wide)),
            vmem((Z, rows, wide)),
            vmem((Z + 1, rows, wide)),
            vmem((X, C, H, capacity, width)),
            vmem((X, H, capacity, width)),
            vmem((H, capacity, width)),
            vmem((2 * H, capacity, width)),
            dma(n, Z),
            dma(n, Z),
            dma(n, Z, 2),
            dma(n, Z),
            dma(n, Z),
            dma(n, Z, 2),
            dma(n, Z),
            dma(n, Z),
            dma(n, Z + 1),
            dma(3),
            dma(team),
            pltpu.SemaphoreType.DMA,
            dma(7),
            dma(7),
            dma(1, Z),
            dma(1, Z + 1),
            dma(2 + 2 + 1 + 2 * Z),
            dma(X),
            dma(H),
            dma(Z, H + 1),
            vmem((batch * Z, 8, 128), f32),
            dma(batch * Z),
            dma(batch * Z),
        ],
        number,
        in_specs=[on_chip] * 13 + [anywhere] * 5,
        vmem=67_000_000,
    )


def adam_update(weight, grad, first, second, rate):
    first = 0.5 * first + 0.5 * grad
    second = 0.5 * second + 0.5 * grad * grad
    correction = 1.0 - 0.5**step_number
    weight = weight - rate * (
        first / correction / (jnp.sqrt(second / correction) + 1e-08) + 0.01 * weight
    )
    return (weight, first, second)


def blank(shape, dtype):
    return pl.pallas_call(
        lambda o_ref: None, out_specs=anywhere, out_shape=jax.ShapeDtypeStruct(shape, dtype)
    )()


def rows_kernel(list_ref, table_ref, o_ref, hold_ref, sem):
    count = o_ref.shape[0]

    @pl.loop(0, count)
    def _(i):
        row = pl.ds(list_ref[i], 1)
        pltpu.make_async_copy(table_ref.at[row, :], hold_ref.at[pl.ds(i, 1), :], sem).start()

    pltpu.make_async_copy(hold_ref, hold_ref, sem).wait()
    o_ref[...] = hold_ref[...].astype(bf16)


def low_rows(table, listed):
    shape = (listed.shape[0], table.shape[1])
    return pl.pallas_call(
        rows_kernel,
        in_specs=[pl.BlockSpec(memory_space=pltpu.SMEM), anywhere],
        out_specs=on_chip,
        out_shape=jax.ShapeDtypeStruct(shape, bf16),
        scratch_shapes=[pltpu.VMEM(shape, f32), pltpu.SemaphoreType.DMA],
    )(listed, table)


def table_kernel(rate, rounds_ref, scale_ref, list_ref, rows_ref, more_ref, w_ref, m_ref, v_ref, nw_ref, g_ref, nv_ref, far_ref, sem):
    block, width = w_ref.shape
    count = list_ref.shape[1]
    start = pl.program_id(0) * block

    def placed(turn, rows):
        row = lax.broadcasted_iota(jnp.int32, (block, count), 0) + start
        pick = (row == list_ref[pl.ds(turn, 1), :]).astype(bf16)
        return dot(pick, rows, (1,), (0,))

    g_ref[...] = placed(0, rows_ref[...])

    @pl.loop(1, rounds_ref[0])
    def _(turn):
        copy = pltpu.make_async_copy(more_ref.at[turn - 1], far_ref, sem)
        copy.start()
        copy.wait()
        g_ref[...] += placed(turn, far_ref[...])

    grad = g_ref[...] * scale_ref[0]
    new_w, _, new_v = adam_update(w_ref[...], grad, m_ref[...], v_ref[...], rate)
    g_ref[...] = grad
    nw_ref[...] = new_w
    nv_ref[...] = new_v


def update_table(rounds, scale, lists, rows, more, table, first, second, rate):
    height, width = table.shape
    sizes = [n for n in range(8, 513, 8) if height % n == 0]
    block = max(sizes) if sizes else height
    part = pl.BlockSpec((block, width), lambda i: (i, 0))
    whole = lambda a: pl.BlockSpec(a.shape, lambda i: (0,) * a.ndim)
    single = pl.BlockSpec(memory_space=pltpu.SMEM)
    return pl.pallas_call(
        partial(table_kernel, rate),
        grid=(height // block,),
        in_specs=[single, single, whole(lists), whole(rows), anywhere, part, part, part],
        out_specs=[part] * 3,
        out_shape=[jax.ShapeDtypeStruct(table.shape, f32)] * 3,
        scratch_shapes=[pltpu.VMEM(rows.shape, bf16), pltpu.SemaphoreType.DMA],
        compiler_params=pltpu.CompilerParams(vmem_limit_bytes=56 * 2**20),
    )(rounds.reshape(1), scale.reshape(1), lists, rows, more, table, first, second)


def small_kernel(scale_ref, qkv_ref, misc_ref, gate_ref, up_ref, down_ref, *refs):
    ins, outs = refs[:15], refs[15:]
    scale = scale_ref[0]
    heads_width = ins[0].shape[2]
    turned_misc = misc_ref[...].T

    def update(k, grad, where):
        old, first, second = (ins[3 * k + n][where] for n in range(3))
        for n, value in enumerate(adam_update(old, grad * scale, first, second, rates[1 + k])):
            outs[3 * k + n][where] = value

    for part in range(3):
        grad = qkv_ref[:, part * heads_width : (part + 1) * heads_width]
        update(0, grad, (slice(None), part, slice(None)))
    update(1, turned_misc[:heads_width], (slice(None), slice(None)))
    update(2, gate_ref[...], (slice(None), 0, slice(None)))
    update(2, up_ref[...], (slice(None), 1, slice(None)))
    update(3, down_ref[...].T, (slice(None), slice(None)))
    count = ins[12].shape[0]
    update(4, turned_misc[heads_width : heads_width + count], (slice(None), slice(None)))


def update_small(scale, sums, olds, firsts, seconds):
    values = [value for group in zip(olds, firsts, seconds) for value in group]
    whole = lambda a: pl.BlockSpec(a.shape, lambda i: (0,) * a.ndim)
    outs = pl.pallas_call(
        small_kernel,
        grid=(1,),
        in_specs=[pl.BlockSpec(memory_space=pltpu.SMEM)] + [whole(a) for a in (*sums, *values)],
        out_specs=[whole(a) for a in values],
        out_shape=[jax.ShapeDtypeStruct(value.shape, f32) for value in values],
        compiler_params=pltpu.CompilerParams(vmem_limit_bytes=50 * 2**20),
    )(scale.reshape(1), *sums, *values)
    return [tuple(outs[3 * k : 3 * k + 3]) for k in range(len(olds))]


def local(
    dims,
    token_ids,
    segment_ids,
    row_of,
    query_count,
    table,
    qkv_weight,
    out_weight,
    gate_up_weight,
    down_weight,
    gains,
    table_m,
    qkv_m,
    out_m,
    gate_up_m,
    down_m,
    gains_m,
    table_v,
    qkv_v,
    out_v,
    gate_up_v,
    down_v,
    gains_v,
):
    H, X, C, Z = dims
    G = X * C
    batch = H * G
    at = {name: lax.axis_index(name) for name in ALL}
    team = at["x"] * C + at["c"]
    owner = at["h"] * G + team
    length = token_ids.shape[1]
    own_len = length // G
    part_len = length // Z
    shard_rows, width = table.shape
    rows_in = width // batch
    heads_width = qkv_weight.shape[2]
    ff_part = down_weight.shape[0]
    capacity = -(-3 * length // (64 * batch)) * 16

    position = jnp.arange(length, dtype=jnp.int32)
    start = at["z"] * part_len
    mine = lax.dynamic_slice_in_dim(token_ids[0], start, part_len, 0)
    mine_seg = lax.dynamic_slice_in_dim(segment_ids[0], start, part_len, 0)
    earlier = position[None, :] < (start + position[:part_len])[:, None]
    seen = jnp.any((mine[:, None] == token_ids[0][None, :]) & earlier, 1)
    tags = jnp.stack([row_of[mine] * 2 + seen.astype(jnp.int32), mine_seg])
    everyone = gather_everyone(tags, dims, 0)
    tags_all = everyone[:, 0].reshape(batch, length)
    segs_all = everyone[:, 1].reshape(batch, length)
    ids_all, fresh_all = tags_all // 2, tags_all % 2 == 0
    row = at["h"] * Z + at["z"]
    seg_row = lax.dynamic_index_in_dim(segs_all, row, 0, keepdims=False)
    ids_row = lax.dynamic_index_in_dim(ids_all, row, 0, keepdims=False)
    fresh_row = lax.dynamic_index_in_dim(fresh_all, row, 0, keepdims=False)

    def counted(flags):
        lanes = 128 if length % 128 == 0 else length
        steps = flags.astype(f32).reshape(-1, length // lanes, lanes)
        upto = jnp.arange(lanes)[:, None] <= jnp.arange(lanes)[None, :]
        inner = jnp.einsum("rgl,lk->rgk", steps, upto.astype(f32))
        sums = inner[:, :, -1]
        groups = jnp.arange(length // lanes)
        before = (groups[:, None] < groups[None, :]).astype(f32)
        outer = jnp.dot(sums, before, precision=peak_affinity)
        return (inner + outer[:, :, None]).reshape(-1, length).astype(jnp.int32)

    owned = fresh_all & (ids_all // shard_rows == owner)
    number = counted(owned)
    shares = (ids_all // shard_rows)[:, None, :] == jnp.arange(batch, dtype=jnp.int32)[None, :, None]
    shares = jnp.sum((shares & fresh_all[:, None, :]).astype(jnp.int32), 2)
    rounds = (jnp.max(shares) + capacity - 1) // capacity
    offset = jnp.where(owned, number, 0)
    spot = jnp.arange(1, capacity + 1, dtype=jnp.int32)

    def owned_list(turn, rows):
        ids = lax.dynamic_slice_in_dim(ids_all, rows[0], rows[1], 0) if rows else ids_all
        places = lax.dynamic_slice_in_dim(offset, rows[0], rows[1], 0) if rows else offset
        hit = (spot + turn * capacity)[None, :, None] == places[:, None, :]
        return jnp.sum(jnp.where(hit, (ids - owner * shard_rows + 1)[:, None, :], 0), 2) - 1

    holder_row = ids_row // shard_rows
    holders = jnp.arange(batch, dtype=jnp.int32)
    split = fresh_row[None, :] & (holder_row[None, :] == holders[:, None])
    number_row = jnp.sum(jnp.where(split, counted(split), 0), 0)
    same_row = ids_row[:, None] == ids_row[None, :]
    rank_row = jnp.sum(jnp.where(same_row, number_row[None, :], 0), 1) - 1
    slots = batch * capacity

    def listed_for(turn):
        return owned_list(turn, None).reshape(H, Z, capacity).transpose(1, 0, 2).reshape(-1)

    def slot_of(turn):
        rank = rank_row - turn * capacity
        slot = ((holder_row % G) * H + holder_row // G) * capacity + rank
        return jnp.where((rank >= 0) & (rank < capacity), slot, -1)

    def expander(turn):
        slot = slot_of(turn)
        return (slot[:, None] == jnp.arange(slots, dtype=jnp.int32)[None, :]).astype(bf16)

    labels = jnp.arange(SEGS, dtype=jnp.int32)
    marks = jnp.arange(SEGS + 1, dtype=jnp.int32)
    member_row = (seg_row[:, None] == marks[None, :]).astype(jnp.int32)
    counts_row = jnp.sum(member_row, 0)
    starts = jnp.cumsum(counts_row) - counts_row
    places = (position - jnp.sum(member_row * starts[None, :], 1)).astype(f32)
    cosine, sine = angles_of(places, HEAD_DIM)
    heads = heads_width // HEAD_DIM

    def rows_for(turn):
        listed = jnp.concatenate([owned_list(turn, (h * Z + at["z"], 1)) for h in range(H)])
        return low_rows(table, jnp.maximum(listed, 0).reshape(-1)).reshape(H, capacity, width)

    def fetch(turn):
        got = fetch_rows(rows_for(turn), dims, 1).reshape(slots, width)
        return jnp.dot(expander(turn), got, preferred_element_type=f32).astype(bf16)

    _, x_more = lax.while_loop(
        lambda s: s[0] < rounds,
        lambda s: (s[0] + 1, s[1] + fetch(s[0])),
        (jnp.int32(1), jnp.zeros((length, width), bf16)),
    )

    pad = -(-(heads_width + 2) // 128) * 128 - heads_width
    misc = jnp.concatenate([out_weight.T, gains.T, jnp.zeros((rows_in, pad - 2), f32)], 1)
    pieces = [
        qkv_weight.reshape(rows_in, -1).astype(bf16),
        misc.astype(bf16),
        gate_up_weight[:, 0].astype(bf16),
        gate_up_weight[:, 1].astype(bf16),
        down_weight.T.astype(bf16),
    ]
    if H == 2:
        tables = [jnp.concatenate([t[:, 0]] * 4, 1) for t in (cosine, sine)]
        weights, (x_low, query, keys, values, attended) = front(
            rows_for(0), slot_of(0), x_more, *tables, seg_row, pieces, heads_width, dims, 2
        )
    else:
        weights = gather_weights(pieces, dims)
    w_qkv, w_misc, w_gate, w_up, w_down = weights
    w_out = w_misc[:, :, :heads_width]
    gain = w_misc[0, :, heads_width : heads_width + 2].T.astype(f32)
    if H != 2:
        w_heads = lax.dynamic_index_in_dim(w_qkv, team, 0, keepdims=False)
        x_low = x_more + fetch(0)
        qkv = jnp.dot(x_low, w_heads, preferred_element_type=f32).reshape(length, 3, heads, HEAD_DIM)
        query = rotate(qkv[:, 0], cosine, sine).astype(bf16).reshape(length, -1)
        keys = rotate(qkv[:, 1], cosine, sine).astype(bf16).reshape(length, -1)
        values = qkv[:, 2].astype(bf16).reshape(length, -1)
        attended_heads = attend(query, keys, values, seg_row)
        attended = team_swap(attended_heads.reshape(G, own_len, heads_width), dims, 3)
    attended = attended.transpose(1, 0, 2)
    x_own = lax.dynamic_slice_in_dim(x_low, team * own_len, own_len, 0)

    attn = dot(attended, w_out, (1, 2), (0, 2))
    hidden_one, first_back = jax.vjp(layer_norm, x_own.astype(f32) + attn, gain[0])
    hidden_low = hidden_one.astype(bf16)
    gate = jnp.einsum("td,zdf->ztf", hidden_low, w_gate, preferred_element_type=f32)
    up = jnp.einsum("td,zdf->ztf", hidden_low, w_up, preferred_element_type=f32)
    active, swiglu_back = jax.vjp(swiglu, gate, up)
    active_low = active.astype(bf16)
    mlp = dot(active_low, w_down, (0, 2), (0, 2))
    hidden_two, second_back = jax.vjp(layer_norm, hidden_one + mlp, gain[1])

    seg_own = lax.dynamic_slice_in_dim(seg_row, team * own_len, own_len, 0)
    counts_all = jnp.sum((segs_all[:, None, :] == labels[None, :, None]).astype(f32), -1)
    loss_value, grad_two = contrast_all(
        hidden_two, seg_own, counts_all.reshape(-1, 1), query_count, dims, 4
    )

    grad_second, grad_gain_two = second_back(grad_two)
    grad_mlp_low = grad_second.astype(bf16)
    grad_active = jnp.einsum("tn,znf->ztf", grad_mlp_low, w_down, preferred_element_type=f32)
    grad_down = jnp.einsum("tn,ztf->znf", grad_mlp_low, active_low, preferred_element_type=f32)
    grad_gate, grad_up = swiglu_back(grad_active)
    grad_gate_low, grad_up_low = grad_gate.astype(bf16), grad_up.astype(bf16)
    grad_one = grad_second + dot(grad_gate_low, w_gate, (0, 2), (0, 2))
    grad_one = grad_one + dot(grad_up_low, w_up, (0, 2), (0, 2))
    grad_first, grad_gain_one = first_back(grad_one)
    weight_grad = partial(jnp.einsum, "td,ztf->zdf", preferred_element_type=f32)
    grad_gate = weight_grad(hidden_low, grad_gate_low).astype(bf16)
    grad_up = weight_grad(hidden_low, grad_up_low).astype(bf16)
    grad_attn_low = grad_first.astype(bf16)
    grad_attended = jnp.einsum("tn,znk->tzk", grad_attn_low, w_out, preferred_element_type=f32)
    grad_attended = grad_attended.astype(bf16).transpose(1, 0, 2)
    grad_out = jnp.einsum("tn,tzk->znk", grad_attn_low, attended, preferred_element_type=f32)
    grad_gains = jnp.stack([grad_gain_one, grad_gain_two], 1)
    grad_misc = jnp.concatenate(
        [
            grad_out.astype(bf16),
            jnp.broadcast_to(grad_gains.astype(bf16)[None], (Z, width, 2)),
            jnp.zeros((Z, width, pad - 2), bf16),
        ],
        2,
    )
    terms = [grad_gate, grad_up, grad_down.astype(bf16), grad_misc]
    most_rounds = -(-length // capacity)
    listed = listed_for(0)
    _, lists = lax.while_loop(
        lambda s: s[0] < rounds,
        lambda s: (
            s[0] + 1,
            lax.dynamic_update_slice_in_dim(s[1], listed_for(s[0])[None], s[0], 0),
        ),
        (jnp.int32(1), jnp.broadcast_to(listed[None], (most_rounds,) + listed.shape)),
    )
    if H == 2:
        sum_gate, sum_up, sum_down, sum_misc, sum_qkv, spread, grad_zero_low, total = back(
            grad_attended,
            query,
            keys,
            values,
            x_low,
            *tables,
            seg_row,
            slot_of(0),
            listed,
            grad_first,
            w_qkv,
            terms,
            heads,
            capacity,
            dims,
            5,
        )
    else:
        grad_heads = team_swap(grad_attended, dims, 5).reshape(length, heads_width)
        grad_query, grad_keys, grad_values = attend_back(query, grad_heads, keys, values, seg_row)
        back_turn = lambda g: rotate(g.reshape(length, heads, HEAD_DIM), cosine, -sine).reshape(length, -1)
        grad_qkv_low = jnp.concatenate([back_turn(grad_query), back_turn(grad_keys), grad_values], 1)
        grad_qkv_low = grad_qkv_low.astype(bf16)
        grad_heads_w = dot(x_low, grad_qkv_low, (0,), (0,)).astype(bf16)
        grad_zero = dot(grad_qkv_low, w_heads, (1,), (1,))
        own_term = lax.dynamic_update_slice_in_dim(
            jnp.zeros_like(grad_zero), grad_first, team * own_len, 0
        )
        grad_zero_low = (grad_zero + own_term).astype(bf16)
        heads_grad = lax.dynamic_update_slice_in_dim(
            jnp.zeros((Z,) + grad_heads_w.shape, bf16), grad_heads_w[None], team, 0
        )
        sum_gate, sum_up, sum_down, sum_misc, sum_qkv = reduce_weights(terms + [heads_grad], dims)

    def collect(turn):
        terms = dot(expander(turn), grad_zero_low, (0,), (0,)).astype(bf16)
        terms = terms.reshape(X, C, H, capacity, width)
        return settle_rows(terms, dims, 6)

    flat = lambda rows: rows.reshape(Z * H * capacity, width)
    spread = flat(spread if H == 2 else collect(0))

    def between(left, left_list, right, right_list):
        same = left_list[:, None] == right_list[None, :]
        return jnp.sum(jnp.where(same, dot(left, right, (1,), (1,)), 0.0))

    def summed(squares):
        return jnp.sum(gather_everyone(jnp.full((8, 128), squares), dims, 8), 0)

    def further(state):
        turn, more, total = state
        rows = flat(collect(turn))
        listed = lists[turn]
        squares = between(rows, listed, rows, listed) + 2 * between(rows, listed, spread, lists[0])
        squares += 2 * lax.fori_loop(
            1, turn, lambda k, held: held + between(rows, listed, more[k - 1], lists[k]), jnp.zeros((), f32)
        )
        more = lax.dynamic_update_slice_in_dim(more, rows[None], turn - 1, 0)
        return turn + 1, more, total + summed(squares / Z)

    if H != 2:
        squares = between(spread, listed, spread, listed) + jnp.sum(sum_misc[:, heads_width:] ** 2)
        squares = squares / Z + jnp.sum(sum_misc[:, :heads_width] ** 2)
        for part in (sum_qkv, sum_gate, sum_up, sum_down):
            squares += jnp.sum(part * part)
        total = summed(squares)
    blank_rows = blank((max(most_rounds - 1, 1),) + spread.shape, bf16)
    _, more, total = lax.while_loop(
        lambda s: s[0] < rounds, further, (jnp.int32(1), blank_rows, total)
    )
    grad_norm = jnp.sqrt(total[0, 0])
    scale = clip_limit / jnp.maximum(grad_norm, clip_limit)
    new_table, clipped_table, new_table_v = update_table(
        rounds, scale, lists, spread, more, table, table_m, table_v, rates[0]
    )
    updated = update_small(
        scale,
        (sum_qkv, sum_misc, sum_gate, sum_up, sum_down),
        (qkv_weight, out_weight, gate_up_weight, down_weight, gains),
        (qkv_m, out_m, gate_up_m, down_m, gains_m),
        (qkv_v, out_v, gate_up_v, down_v, gains_v),
    )
    return (
        loss_value.reshape(1),
        grad_norm.reshape(1),
        new_table,
        *(new[0] for new in updated),
        clipped_table,
        *(new[1] for new in updated),
        new_table_v,
        *(new[2] for new in updated),
    )


def solution(mesh):
    batch, mp = mesh.shape["batch"], mesh.shape["mp"]
    dims = (batch // mp, mp // 2, 2, mp)
    split = Mesh(mesh.devices.reshape(dims), ALL)
    rows = ("h", "x", "c")
    weights = (
        P(rows, None),
        P(rows, None, "z"),
        P("z", rows),
        P(rows, None, "z"),
        P("z", rows),
        P(None, rows),
    )
    return jax.shard_map(
        partial(local, dims),
        mesh=split,
        in_specs=(P(rows, None), P(rows, None), P(), P()) + weights * 3,
        out_specs=(P(), P()) + weights + weights + weights,
        check_vma=False,
    )
```

```python
from functools import partial

import jax
import jax.numpy as jnp
from jax import lax
from jax.experimental import pallas as pl
from jax.experimental.pallas import tpu as pltpu
from jax.sharding import Mesh, PartitionSpec as P

HEAD_DIM = 64
SEGS = 8

peak_affinity = lax.Precision.HIGHEST
sharpness_divisor = 0.05
clip_limit = 1.0
step_number = 3.0
rates = (0.3, 0.02, 0.02, 0.02, 0.02, 0.3)
negative = -1e30
GROUP = ("x", "c")
ALL = ("h", "x", "c", "z")
f32 = jnp.float32
bf16 = jnp.bfloat16


def angles_of(places, head_dim):
    half_dim = head_dim // 2
    freqs = jnp.power(1000.0, -2.0 * jnp.arange(half_dim, dtype=f32) / head_dim)
    angles = places[:, None] * freqs[None, :]
    return jnp.cos(angles)[:, None, :], jnp.sin(angles)[:, None, :]


def rotate(values, cosine, sine):
    half_dim = values.shape[-1] // 2
    former = values[..., :half_dim]
    latter = values[..., half_dim:]
    return jnp.concatenate([former * cosine - latter * sine, latter * cosine + former * sine], -1)


def layer_norm(values, gain):
    centred = values - jnp.mean(values, -1, keepdims=True)
    spread = jnp.mean(centred * centred, -1, keepdims=True)
    return centred * lax.rsqrt(spread + 1e-05) * gain


def swiglu(gate, up):
    return jax.nn.silu(gate) * up


def dot(left, right, left_dims, right_dims, precision=None):
    return lax.dot_general(
        left, right, ((left_dims, right_dims), ((), ())), preferred_element_type=f32, precision=precision
    )


def attend_kernel(q_ref, k_ref, v_ref, segq_ref, segk_ref, o_ref):
    same = segq_ref[...] == segk_ref[...]
    query, keys, values = q_ref[...], k_ref[...], v_ref[...]
    width = query.shape[1]
    lane = lax.broadcasted_iota(jnp.int32, query.shape, 1) // HEAD_DIM
    result = jnp.zeros(query.shape, f32)
    for head in range(width // HEAD_DIM):
        own = jnp.where(lane == head, query, jnp.zeros_like(query))
        scores = dot(own, keys, (1,), (1,)) * HEAD_DIM ** (-0.5)
        scores = jnp.where(same, scores, negative)
        weights = jnp.exp(scores - jnp.max(scores, 1, keepdims=True))
        probs = (weights * (1.0 / jnp.sum(weights, 1, keepdims=True))).astype(bf16)
        result = jnp.where(lane == head, dot(probs, values, (1,), (0,)), result)
    o_ref[...] = result.astype(bf16)


def attend_back_kernel(q_ref, g_ref, k_ref, v_ref, segq_ref, segk_ref, dq_ref, dk_ref, dv_ref):
    @pl.when(pl.program_id(0) == 0)
    def _():
        dk_ref[...] = jnp.zeros_like(dk_ref)
        dv_ref[...] = jnp.zeros_like(dv_ref)

    same = segk_ref[...] == segq_ref[...]
    query, grad, keys, values = q_ref[...], g_ref[...], k_ref[...], v_ref[...]
    width = query.shape[1]
    factor = HEAD_DIM ** (-0.5)
    lane = lax.broadcasted_iota(jnp.int32, query.shape, 1) // HEAD_DIM
    result = jnp.zeros(query.shape, f32)
    for head in range(width // HEAD_DIM):
        own = jnp.where(lane == head, query, jnp.zeros_like(query))
        own_grad = jnp.where(lane == head, grad, jnp.zeros_like(grad))
        scores = dot(keys, own, (1,), (1,)) * factor
        scores = jnp.where(same, scores, negative)
        weights = jnp.exp(scores - jnp.max(scores, 0, keepdims=True))
        probs = weights * (1.0 / jnp.sum(weights, 0, keepdims=True))
        grad_probs = dot(values, own_grad, (1,), (1,))
        inner = jnp.sum(probs * grad_probs, 0, keepdims=True)
        grad_scores = (probs * (grad_probs - inner)).astype(bf16)
        dk_ref[...] += dot(grad_scores, own, (1,), (0,)) * factor
        dv_ref[...] += dot(probs.astype(bf16), own_grad, (1,), (0,))
        result = jnp.where(lane == head, dot(grad_scores, keys, (0,), (0,)) * factor, result)
    dq_ref[...] = result


def attend(query, keys, values, segment_row):
    length, width = query.shape
    block = min(256, length)
    whole = pl.BlockSpec((length, width), lambda i: (0, 0))
    part = pl.BlockSpec((block, width), lambda i: (i, 0))
    return pl.pallas_call(
        attend_kernel,
        grid=(length // block,),
        in_specs=[
            part,
            whole,
            whole,
            pl.BlockSpec((block, 1), lambda i: (i, 0)),
            pl.BlockSpec((1, length), lambda i: (0, 0)),
        ],
        out_specs=part,
        out_shape=jax.ShapeDtypeStruct((length, width), bf16),
    )(query, keys, values, segment_row[:, None], segment_row[None, :])


def attend_back(query, grad, keys, values, segment_row):
    length, width = query.shape
    block = min(256, length)
    whole = pl.BlockSpec((length, width), lambda i: (0, 0))
    part = pl.BlockSpec((block, width), lambda i: (i, 0))
    full = jax.ShapeDtypeStruct((length, width), f32)
    return pl.pallas_call(
        attend_back_kernel,
        grid=(length // block,),
        in_specs=[
            part,
            part,
            whole,
            whole,
            pl.BlockSpec((1, block), lambda i: (0, i)),
            pl.BlockSpec((length, 1), lambda i: (0, 0)),
        ],
        out_specs=[part, whole, whole],
        out_shape=[full, full, full],
    )(query, grad, keys, values, segment_row[None, :], segment_row[:, None])


MESH = pl.DeviceIdType.MESH
anywhere = pl.BlockSpec(memory_space=pl.ANY)
on_chip = pl.BlockSpec(memory_space=pltpu.VMEM)


def guarded(when, action):
    if when is None:
        action()
    else:
        pl.when(when)(action)


def both(first, second):
    return second if first is None else first if second is None else first & second


class Wires:
    def __init__(self, send_sem):
        self.at = {name: lax.axis_index(name) for name in ALL}
        self.send_sem = send_sem
        self.pending = []

    def peer(self, **moved):
        return tuple(moved.get(name, self.at[name]) for name in ALL)

    def greet(self, peers):
        barrier = pltpu.get_barrier_semaphore()
        expected = 0
        for when, target in peers:
            guarded(
                when,
                lambda target=target: pl.semaphore_signal(
                    barrier, inc=1, device_id=target, device_id_type=MESH
                ),
            )
            expected = expected + (1 if when is None else when.astype(jnp.int32))
        pl.semaphore_wait(barrier, expected)

    def send(self, source, goal, recv_sem, target, when=None):
        number = len(self.pending)

        def copy():
            return pltpu.make_async_remote_copy(
                src_ref=source,
                dst_ref=goal,
                send_sem=self.send_sem.at[number],
                recv_sem=recv_sem,
                device_id=target,
                device_id_type=MESH,
            )

        guarded(when, lambda: copy().start())
        self.pending.append((when, lambda: copy().wait_send()))

    def arrived(self, goal, recv_sem, when=None):
        guarded(when, lambda: pltpu.make_async_copy(goal, goal, recv_sem).wait())

    def drain(self):
        for when, wait in self.pending:
            guarded(when, wait)


def call(kernel, arguments, outs, out_specs, scratch, number, in_specs=None, vmem=None):
    return pl.pallas_call(
        kernel,
        in_specs=in_specs or [on_chip] * len(arguments),
        out_specs=out_specs,
        out_shape=outs,
        scratch_shapes=scratch,
        compiler_params=pltpu.CompilerParams(
            collective_id=number, has_side_effects=True, vmem_limit_bytes=vmem
        ),
    )(*arguments)


def everyone_kernel(dims, x_ref, o_ref, send_sem, recv_sem):
    wires = Wires(send_sem)
    H, X, C, Z = dims
    total = H * X * C * Z
    at = wires.at
    me = ((at["h"] * X + at["x"]) * C + at["c"]) * Z + at["z"]

    def coordinates(flat):
        return (flat // (X * C * Z), flat // (C * Z) % X, flat // Z % C, flat % Z)

    wires.greet([(None, coordinates((me + k) % total)) for k in range(1, total)])
    for k in range(1, total):
        wires.send(x_ref, o_ref.at[me], recv_sem.at[k], coordinates((me + k) % total))
    o_ref[me] = x_ref[...]
    for k in range(1, total):
        wires.arrived(o_ref.at[(me + total - k) % total], recv_sem.at[k])
    wires.drain()


def gather_everyone(x, dims, number):
    total = dims[0] * dims[1] * dims[2] * dims[3]
    if dims[0] > 2:
        return lax.all_gather(x, ALL, axis=0, tiled=False)
    return call(
        partial(everyone_kernel, dims),
        (x,),
        jax.ShapeDtypeStruct((total,) + x.shape, x.dtype),
        on_chip,
        [pltpu.SemaphoreType.DMA((total,)), pltpu.SemaphoreType.DMA((total,))],
        number,
    )


def team_kernel(dims, split_in, x_ref, o_ref, send_sem, recv_sem):
    H, X, C, Z = dims
    wires = Wires(send_sem)
    at = wires.at
    me = at["x"] * C + at["c"]
    others = [(1 - at["x"], at["c"]), (1 - at["x"], 1 - at["c"]), (at["x"], 1 - at["c"])]
    wires.greet([(None, wires.peer(x=x, c=c)) for x, c in others])
    for x, c in others:
        wires.send(x_ref.at[x * C + c], o_ref.at[me], recv_sem.at[me], wires.peer(x=x, c=c))
    o_ref[me] = x_ref[me]
    for x, c in others:
        wires.arrived(o_ref.at[x * C + c], recv_sem.at[x * C + c])
    wires.drain()


def team_swap(x, dims, number):
    if dims[0] > 2:
        return lax.all_to_all(x, GROUP, split_axis=0, concat_axis=0, tiled=True)
    return call(
        partial(team_kernel, dims, 0),
        (x,),
        jax.ShapeDtypeStruct(x.shape, x.dtype),
        on_chip,
        [pltpu.SemaphoreType.DMA((3,)), pltpu.SemaphoreType.DMA((4,))],
        number,
    )


def contrast(total, counts, queries):
    exact = partial(dot, precision=peak_affinity)
    pooled = total / counts
    scale = lax.rsqrt(jnp.sum(pooled * pooled, -1, keepdims=True) + 1e-06)
    embed = pooled * scale
    half = total.shape[0] // 2
    question, passage = embed[:half], embed[half:]
    scores = exact(question, passage, (1,), (1,)) / sharpness_divisor
    order = lax.broadcasted_iota(jnp.int32, scores.shape, 0)
    target = (order == lax.broadcasted_iota(jnp.int32, scores.shape, 1)).astype(f32)
    weight = (order < queries).astype(f32) / jnp.full(scores.shape, queries).astype(f32)
    peak = jnp.max(scores, -1, keepdims=True)
    shares = jnp.exp(scores - peak)
    mass = jnp.sum(shares, -1, keepdims=True)
    each = peak + jnp.log(mass) - jnp.sum(scores * target, -1, keepdims=True)
    loss = jnp.sum(weight[:, :1] * each)
    slope = (shares / mass - target) * weight
    grad = jnp.concatenate(
        [exact(slope, passage, (1,), (0,)), exact(slope, question, (0,), (0,))], 0
    ) / sharpness_divisor
    grad = scale * (grad - embed * jnp.sum(grad * embed, -1, keepdims=True))
    return loss, grad / counts


def normed(values):
    centred = values - jnp.mean(values, -1, keepdims=True)
    scale = lax.rsqrt(jnp.mean(centred * centred, -1, keepdims=True) + 1e-05)
    return centred * scale, scale


def normed_back(grad, unit, scale):
    shared = jnp.mean(grad * unit, -1, keepdims=True)
    return (grad - jnp.mean(grad, -1, keepdims=True) - unit * shared) * scale


def middle_kernel(
    dims,
    queries_ref,
    att_ref,
    x_ref,
    gain_ref,
    seg_ref,
    counts_ref,
    *refs,
):
    H, X, C, Z = dims
    ins, (loss_ref, swap_ref, first_ref), terms, weights = refs[:4], refs[4:7], refs[7:11], refs[11:15]
    (
        gate_ref,
        up_ref,
        act_ref,
        one_ref,
        low_ref,
        unit_ref,
        work_ref,
        grad_ref,
        stage_ref,
        misc_ref,
        sums_ref,
        team_ref,
        all_ref,
        load_sem,
        store_sem,
        misc_sem,
        send_sem,
        team_sem,
        recv_sem,
    ) = refs[15:]
    wires = Wires(send_sem)
    at = wires.at
    me = at["x"] * C + at["c"]
    row = at["h"] * Z + at["z"]
    rows = H * Z
    others = [(1 - at["x"], at["c"]), (1 - at["x"], 1 - at["c"]), (at["x"], 1 - at["c"])]
    far = [(row + k) % rows for k in range(1, rows)]
    loads = lambda n, k: pltpu.make_async_copy(ins[n].at[k], weights[n].at[k], load_sem.at[n, k])
    for n in (3, 0, 1, 2):
        for k in range(Z):
            loads(n, k).start()
    wires.greet(
        [(None, wires.peer(x=x, c=c)) for x, c in others]
        + [(None, wires.peer(h=r // Z, z=r % Z)) for r in far]
    )
    w_gate, w_up, w_down, w_misc = weights
    heads_width = att_ref.shape[2]
    own_len, width = x_ref.shape
    attn = x_ref[...].astype(f32)
    for k in range(Z):
        loads(3, k).wait()
        attn = attn + dot(att_ref[k], w_misc[k, :, :heads_width], (1,), (1,))
    unit_one, scale_one = normed(attn)
    unit_ref[...] = unit_one
    one_ref[...] = unit_one * gain_ref[0:1, :]
    low_ref[...] = one_ref[...].astype(bf16)
    work_ref[...] = one_ref[...]

    @pl.loop(0, Z)
    def _(k):
        for n in range(3):
            loads(n, k).wait()
        gate = dot(low_ref[...], w_gate[k], (1,), (0,))
        up = dot(low_ref[...], w_up[k], (1,), (0,))
        gate_ref[k] = gate
        up_ref[k] = up
        act_ref[k] = (gate / (1.0 + jnp.exp(-gate)) * up).astype(bf16)
        work_ref[...] += dot(act_ref[k], w_down[k], (1,), (1,))

    unit_two, scale_two = normed(work_ref[...])
    texts = sums_ref.shape[0]
    label = lax.broadcasted_iota(jnp.int32, (texts, own_len), 0)
    member = (label == seg_ref[...]).astype(f32)
    sums_ref[...] = dot(member, unit_two * gain_ref[1:2, :], (1,), (0,), peak_affinity)
    for x, c in others:
        wires.send(sums_ref, team_ref.at[me], team_sem.at[me], wires.peer(x=x, c=c))
    team_ref[me] = sums_ref[...]
    for x, c in others:
        wires.arrived(team_ref.at[x * C + c], team_sem.at[x * C + c])
    all_ref[row] = (team_ref[0] + team_ref[1]) + (team_ref[2] + team_ref[3])
    for r in far:
        wires.send(all_ref.at[row], all_ref.at[row], recv_sem.at[row], wires.peer(h=r // Z, z=r % Z))
    for r in far:
        wires.arrived(all_ref.at[r], recv_sem.at[r])
    wires.drain()
    loss, grad = contrast(all_ref[...].reshape(rows * texts, width), counts_ref[...], queries_ref[0])
    loss_ref[...] = jnp.full(loss_ref.shape, loss)
    all_ref[...] = grad.reshape(rows, texts, width)
    grad_two = dot(member, all_ref[row], (0,), (0,), peak_affinity)
    lanes = misc_ref.shape[2]
    gain_two = jnp.sum(grad_two * unit_two, 0, keepdims=True)
    grad_ref[...] = normed_back(grad_two * gain_ref[1:2, :], unit_two, scale_two)
    low_back = grad_ref[...].astype(bf16)

    def store(n, k):
        return pltpu.make_async_copy(stage_ref.at[n, k % 2], terms[n].at[k], store_sem.at[n, k % 2])

    @pl.loop(0, Z)
    def _(k):
        @pl.when(k >= 2)
        def _():
            for n in range(3):
                store(n, k - 2).wait()

        grad_act = dot(low_back, w_down[k], (1,), (0,))
        stage_ref[2, k % 2] = dot(low_back, act_ref[k], (0,), (0,)).astype(bf16)
        gate, up = gate_ref[k], up_ref[k]
        share = 1.0 / (1.0 + jnp.exp(-gate))
        grad_gate = (grad_act * up * (share * (1.0 + gate * (1.0 - share)))).astype(bf16)
        grad_up = (grad_act * (gate * share)).astype(bf16)
        grad_ref[...] += dot(grad_gate, w_gate[k], (1,), (1,)) + dot(grad_up, w_up[k], (1,), (1,))
        stage_ref[0, k % 2] = dot(low_ref[...], grad_gate, (0,), (0,)).astype(bf16)
        stage_ref[1, k % 2] = dot(low_ref[...], grad_up, (0,), (0,)).astype(bf16)
        for n in range(3):
            store(n, k).start()

    gain_one = jnp.sum(grad_ref[...] * unit_ref[...], 0, keepdims=True)
    line = lax.broadcasted_iota(jnp.int32, (16, width), 0)
    lines = jnp.where(line == 0, gain_one, jnp.where(line == 1, gain_two, 0.0)).astype(bf16)
    gain_terms = dot(lines, selection(16, lanes, heads_width), (0,), (0,))
    first_ref[...] = normed_back(grad_ref[...] * gain_ref[0:1, :], unit_ref[...], scale_one)
    low_first = first_ref[...].astype(bf16)
    widen = selection(heads_width, lanes, 0)
    kept = lambda k: pltpu.make_async_copy(misc_ref.at[k], terms[3].at[k], misc_sem.at[k])
    for k in range(Z):
        swap_ref[k] = dot(low_first, w_misc[k, :, :heads_width], (1,), (0,)).astype(bf16)
        wide = dot(att_ref[k], widen, (1,), (0,)).astype(bf16)
        misc_ref[k] = (dot(low_first, wide, (0,), (0,)) + gain_terms).astype(bf16)
        kept(k).start()
    for k in range(Z):
        kept(k).wait()
    for k in (Z - 2, Z - 1):
        for n in range(3):
            store(n, k).wait()


def middle(queries, attended, x_own, gain, seg_own, counts, weights, dims, number):
    H, X, C, Z = dims
    rows, team = H * Z, X * C
    own_len, width = x_own.shape
    part = weights[0].shape[2]
    vmem = lambda shape, dtype=bf16: pltpu.VMEM(shape, dtype)
    dma = lambda *shape: pltpu.SemaphoreType.DMA(shape)
    outs = call(
        partial(middle_kernel, dims),
        (queries, attended, x_own, gain, seg_own[None, :], counts, *weights),
        [
            jax.ShapeDtypeStruct((8, 128), f32),
            jax.ShapeDtypeStruct(attended.shape, bf16),
            jax.ShapeDtypeStruct(x_own.shape, f32),
        ]
        + [jax.ShapeDtypeStruct(weight.shape, bf16) for weight in weights],
        [on_chip] * 3 + [anywhere] * 4,
        [vmem(weight.shape) for weight in weights]
        + [
            vmem((Z, own_len, part), f32),
            vmem((Z, own_len, part), f32),
            vmem((Z, own_len, part)),
            vmem((own_len, width), f32),
            vmem((own_len, width)),
            vmem((own_len, width), f32),
            vmem((own_len, width), f32),
            vmem((own_len, width), f32),
            vmem((3, 2, width, part)),
            vmem(weights[3].shape),
            vmem((SEGS, width), f32),
            vmem((team, SEGS, width), f32),
            vmem((rows, SEGS, width), f32),
            dma(4, Z),
            dma(3, 2),
            dma(Z),
            dma(3 + rows),
            dma(team),
            dma(rows),
        ],
        number,
        in_specs=[pl.BlockSpec(memory_space=pltpu.SMEM)] + [on_chip] * 5 + [anywhere] * 4,
        vmem=62 * 2**20,
    )
    return outs[0][0, 0], outs[1], outs[2], list(outs[3:])


def contrast_all(hidden, seg_own, counts, queries, dims):
    H, X, C, Z = dims
    labels = jnp.arange(SEGS, dtype=jnp.int32)
    member = (seg_own[None, :] == labels[:, None]).astype(f32)
    sums = jnp.dot(member, hidden, precision=peak_affinity)
    total = lax.all_gather(lax.psum(sums, GROUP), ("h", "z"), axis=0, tiled=True)
    loss, grad = contrast(total, counts, queries[0])
    row = lax.axis_index("h") * Z + lax.axis_index("z")
    grad = lax.dynamic_slice_in_dim(grad, row * SEGS, SEGS, 0)
    return loss, dot(member, grad, (0,), (0,), peak_affinity)


def fetch_kernel(dims, x_ref, o_ref, send_sem, recv_sem):
    H, X, C, Z = dims
    wires = Wires(send_sem)
    at = wires.at
    h, x, c = at["h"], at["x"], at["c"]
    across, beside = wires.peer(x=1 - x), wires.peer(c=1 - c)
    away = [(h + k) % H for k in range(1, H)]
    wires.greet([(None, across), (None, beside)] + [(None, wires.peer(h=g)) for g in away])
    for g in away:
        wires.send(x_ref.at[g], o_ref.at[x, c, h], recv_sem.at[x, c, h], wires.peer(h=g))
    mine = (o_ref.at[x, c, h], recv_sem.at[x, c, h])
    wires.send(x_ref.at[h], *mine, across)
    wires.send(x_ref.at[h], *mine, beside)
    o_ref[x, c, h] = x_ref[h]
    for g in away:
        place = (o_ref.at[x, c, g], recv_sem.at[x, c, g])
        wires.arrived(*place)
        wires.send(place[0], *place, across)
        wires.send(place[0], *place, beside)
    for g in [h] + away:
        place = (o_ref.at[1 - x, c, g], recv_sem.at[1 - x, c, g])
        wires.arrived(*place)
        wires.send(place[0], *place, beside)
    for y in (x, 1 - x):
        for g in [h] + away:
            wires.arrived(o_ref.at[y, 1 - c, g], recv_sem.at[y, 1 - c, g])
    wires.drain()


def fetch_rows(rows, dims, number):
    H, X, C, Z = dims
    if H > 2:
        got = lax.all_to_all(rows, "h", split_axis=0, concat_axis=0, tiled=True)
        return lax.all_gather(got, GROUP, axis=0, tiled=False)
    return call(
        partial(fetch_kernel, dims),
        (rows,),
        jax.ShapeDtypeStruct((X, C) + rows.shape, rows.dtype),
        on_chip,
        [pltpu.SemaphoreType.DMA((4 * H,)), pltpu.SemaphoreType.DMA((X, C, H))],
        number,
    )


def along_line(wires, piece, recv_sem, extra=None):
    z, Z = wires.at["z"], wires.size_z
    right, left = wires.peer(z=z + 1), wires.peer(z=z - 1)
    for far in range(0, Z):
        for sign, onward, more in ((-1, right, z + 1 < Z), (1, left, z >= 1)):
            spot = z + sign * far
            there = None if far == 0 else (spot >= 0 if sign < 0 else spot < Z)
            for view, sem in zip(piece(spot), recv_sem(spot)):
                if far:
                    wires.arrived(view, sem, there)
                wires.send(view, view, sem, onward, both(there, more))
            if extra is not None and (far or sign < 0):
                extra(spot, there)


def settle_kernel(dims, x_ref, o_ref, beside_ref, across_ref, ready_ref, send_sem, beside_sem, across_sem, recv_sem):
    H, X, C, Z = dims
    wires = Wires(send_sem)
    wires.size_z = Z
    at = wires.at
    h, x, c, z = at["h"], at["x"], at["c"], at["z"]
    across, beside = wires.peer(x=1 - x), wires.peer(c=1 - c)
    away = [(h + k) % H for k in range(1, H)]
    wires.greet(
        [(None, across), (None, beside)]
        + [(None, wires.peer(h=g)) for g in away]
        + [(z + 1 < Z, wires.peer(z=z + 1)), (z >= 1, wires.peer(z=z - 1))]
    )
    for y in (1 - x, x):
        wires.send(x_ref.at[y, 1 - c], beside_ref.at[y], beside_sem.at[y], beside)
    wires.arrived(beside_ref.at[1 - x], beside_sem.at[1 - x])
    for g in away + [h]:
        total = x_ref[1 - x, c, g].astype(f32) + beside_ref[1 - x, g].astype(f32)
        ready_ref[g] = total.astype(ready_ref.dtype)
        wires.send(ready_ref.at[g], across_ref.at[g], across_sem.at[g], across)
    wires.arrived(beside_ref.at[x], beside_sem.at[x])
    for g in away + [h]:
        wires.arrived(across_ref.at[g], across_sem.at[g])
        total = x_ref[x, c, g].astype(f32) + beside_ref[x, g].astype(f32)
        total = (total + across_ref[g].astype(f32)).astype(o_ref.dtype)
        if g is h:
            o_ref[z, h] = total
        else:
            ready_ref[H + g] = total
            wires.send(ready_ref.at[H + g], o_ref.at[z, h], recv_sem.at[z, h], wires.peer(h=g))
    for g in away:
        wires.arrived(o_ref.at[z, g], recv_sem.at[z, g])
    along_line(wires, lambda s: [o_ref.at[s]], lambda s: [recv_sem.at[s, H]])
    wires.drain()


def settle_rows(terms, dims, number):
    H, X, C, Z = dims
    block = terms.shape[3:]
    if H > 2:
        terms = terms.reshape((X * C,) + (H,) + block)
        terms = lax.psum_scatter(terms, GROUP, scatter_dimension=0, tiled=True)[0]
        terms = lax.all_to_all(terms, "h", split_axis=0, concat_axis=0, tiled=True)
        return lax.all_gather(terms, "z", axis=0, tiled=False)
    return call(
        partial(settle_kernel, dims),
        (terms,),
        jax.ShapeDtypeStruct((Z, H) + block, terms.dtype),
        on_chip,
        [
            pltpu.VMEM((X, H) + block, terms.dtype),
            pltpu.VMEM((H,) + block, terms.dtype),
            pltpu.VMEM((2 * H,) + block, terms.dtype),
            pltpu.SemaphoreType.DMA((2 + 2 * H + 2 * Z,)),
            pltpu.SemaphoreType.DMA((X,)),
            pltpu.SemaphoreType.DMA((H,)),
            pltpu.SemaphoreType.DMA((Z, H + 1)),
        ],
        number,
    )


def gather_weights(pieces, dims):
    H, X, C, Z = dims
    rows = pieces[0].shape[0]
    outs = [lax.all_gather(piece, ALL, axis=0, tiled=False) for piece in pieces]
    outs = [whole.reshape(H * X * C, Z, rows, -1).transpose(1, 0, 2, 3) for whole in outs]
    return [whole.reshape(Z, H * X * C * rows, -1) for whole in outs]


def reduce_weights(pieces, dims):
    H, X, C, Z = dims
    batch = H * X * C
    rows = pieces[0].shape[1] // batch
    sums = []
    for piece in pieces:
        piece = piece.reshape(Z, batch, rows, -1).transpose(1, 0, 2, 3)
        piece = piece.reshape(batch * Z, rows, -1)
        sums.append(lax.psum_scatter(piece, ALL, scatter_dimension=0, tiled=True)[0].astype(f32))
    return sums


class Spread:
    def __init__(self, wires, dims, kinds, stages, outs, send_sem, recv_sem):
        self.wires, self.kinds, self.stages, self.outs = wires, kinds, stages, outs
        self.send_sem, self.recv_sem = send_sem, recv_sem
        self.Z = dims[3]
        self.spots = 2 * self.Z - 1

    def where(self, i):
        z = self.wires.at["z"]
        if isinstance(i, int) and i == 0:
            return z, 0, None
        sign = 1 - 2 * (i % 2)
        s = z + sign * ((i + 1) // 2)
        return s, sign, (s >= 0) & (s < self.Z)

    def place(self, a, s, h, x, c):
        return self.outs[a].at[s, h, x, c], self.recv_sem.at[a, s, (h * 2 + x) * 2 + c]

    def moves(self, phase, i):
        at, peer = self.wires.at, self.wires.peer
        h, x, c, z = at["h"], at["x"], at["c"], at["z"]
        s, sign, there = self.where(i)
        beside = peer(c=1 - c)
        moves = []

        def add(a, block, kind, target, when=there):
            view, sem = self.place(a, s, *block)
            fresh = isinstance(i, int) and i == 0 and phase < 2
            source = self.stages[a] if fresh else view
            moves.append((when, source, view, sem, self.send_sem.at[a, kind, i], target))

        for a, kind in enumerate(self.kinds):
            hops = [peer(h=1 - h), peer(x=1 - x)]
            if phase == 0:
                if isinstance(i, int) and i == 0:
                    add(a, (h, x, c), 0, peer(z=z + 1), z + 1 < self.Z)
                    add(a, (h, x, c), 1, peer(z=z - 1), z >= 1)
                else:
                    onward = z - sign
                    add(a, (h, x, c), 0, peer(z=onward), there & (onward >= 0) & (onward < self.Z))
            if phase == 1:
                add(a, (h, x, c), 2, hops[kind])
                add(a, (h, x, c), 3, hops[1 - kind])
                add(a, (h, x, c), 4, beside)
            if phase == 2:
                block = (1 - h, x, c) if kind == 0 else (h, 1 - x, c)
                add(a, block, 5, hops[1 - kind])
                add(a, block, 6, beside)
            if phase == 3:
                add(a, (h, 1 - x, c) if kind == 0 else (1 - h, x, c), 7, beside)
                add(a, (1 - h, 1 - x, c), 8, beside)
        return moves

    def copy(self, move):
        return pltpu.make_async_remote_copy(
            src_ref=move[1],
            dst_ref=move[2],
            send_sem=move[4],
            recv_sem=move[3],
            device_id=move[5],
            device_id_type=MESH,
        )

    def wait(self, phase, i):
        at = self.wires.at
        h, x, c = at["h"], at["x"], at["c"]
        s, _, there = self.where(i)
        for a, kind in enumerate(self.kinds):
            if phase == 0:
                blocks = [] if isinstance(i, int) and i == 0 else [(h, x, c)]
            elif phase == 1:
                blocks = []
            elif phase == 2:
                blocks = [(1 - h, x, c) if kind == 0 else (h, 1 - x, c)]
            elif phase == 3:
                blocks = [(h, 1 - x, c) if kind == 0 else (1 - h, x, c), (1 - h, 1 - x, c)]
            else:
                blocks = [(g, y, 1 - c) for g in range(2) for y in range(2)]
            for block in blocks:
                self.wires.arrived(*self.place(a, s, *block), there)

    def step(self, phase, i):
        self.wait(phase, i)
        if phase < 4:
            for move in self.moves(phase, i):
                guarded(move[0], lambda move=move: self.copy(move).start())

    def run(self, phases, first, last):
        if first == 0:
            for phase in phases:
                self.step(phase, 0)
        low = max(first, 1)
        if low < last:

            @pl.loop(low, last)
            def _(i):
                for phase in phases:
                    self.step(phase, i)

    def settle(self):
        def sent(i):
            for phase in (0, 1, 2, 3):
                for move in self.moves(phase, i):
                    guarded(move[0], lambda move=move: self.copy(move).wait_send())

        sent(0)

        @pl.loop(1, self.spots)
        def _(i):
            sent(i)


class Late:
    def __init__(self, wires, dims, stage, out, send_sem, recv_sem):
        self.wires, self.stage, self.out = wires, stage, out
        self.send_sem, self.recv_sem, self.Z = send_sem, recv_sem, dims[3]
        self.spots = 2 * self.Z - 1

    def where(self, i):
        z = self.wires.at["z"]
        if isinstance(i, int) and i == 0:
            return z, 0, None
        sign = 1 - 2 * (i % 2)
        s = z + sign * ((i + 1) // 2)
        return s, sign, (s >= 0) & (s < self.Z)

    def line(self, s, c):
        return self.out.at[s, :, :, c]

    def moves(self, i):
        at, peer = self.wires.at, self.wires.peer
        h, x, c, z = at["h"], at["x"], at["c"], at["z"]
        sent, got = self.send_sem, self.recv_sem
        if isinstance(i, str) and i == "across":
            view = self.out.at[z, h, x, c]
            return [(None, self.stage, view, sent.at[0, 0], got.at[0, 0], peer(x=1 - x))]
        if isinstance(i, str) and i == "away":
            view = self.out.at[z, h, :, c]
            return [(None, view, view, sent.at[0, 1], got.at[0, 1], peer(h=1 - h))]
        s, sign, there = self.where(i)
        view = self.line(s, c)
        if isinstance(i, int) and i == 0:
            moves = [
                (z + 1 < self.Z, view, view, sent.at[1, 0], got.at[1, s], peer(z=z + 1)),
                (z >= 1, view, view, sent.at[0, 2], got.at[1, s], peer(z=z - 1)),
            ]
        else:
            onward = z - sign
            when = there & (onward >= 0) & (onward < self.Z)
            moves = [(when, view, view, sent.at[1, i], got.at[1, s], peer(z=onward))]
        return moves + [(there, view, view, sent.at[2, i], got.at[2, s], peer(c=1 - c))]

    def copy(self, move):
        return pltpu.make_async_remote_copy(
            src_ref=move[1],
            dst_ref=move[2],
            send_sem=move[3],
            recv_sem=move[4],
            device_id=move[5],
            device_id_type=MESH,
        )

    def step(self, i):
        at = self.wires.at
        h, x, c, z = at["h"], at["x"], at["c"], at["z"]
        if isinstance(i, str) and i == "away":
            self.wires.arrived(self.out.at[z, h, 1 - x, c], self.recv_sem.at[0, 0])
        elif isinstance(i, int) and i == 0:
            self.wires.arrived(self.out.at[z, 1 - h, :, c], self.recv_sem.at[0, 1])
        elif not isinstance(i, str):
            s, _, there = self.where(i)
            self.wires.arrived(self.line(s, c), self.recv_sem.at[1, s], there)
        for move in self.moves(i):
            guarded(move[0], lambda move=move: self.copy(move).start())

    def settle(self):
        def sent(i):
            for move in self.moves(i):
                guarded(move[0], lambda move=move: self.copy(move).wait_send())

        for i in ("across", "away", 0):
            sent(i)

        @pl.loop(1, self.spots)
        def _(i):
            sent(i)

        @pl.loop(0, self.Z)
        def _(s):
            self.wires.arrived(self.line(s, 1 - self.wires.at["c"]), self.recv_sem.at[2, s])


def selection(rows, columns, shift):
    row = lax.broadcasted_iota(jnp.int32, (rows, columns), 0)
    column = lax.broadcasted_iota(jnp.int32, (rows, columns), 1)
    return (column == row + shift).astype(bf16)


def turned(values, cosine, sine):
    half = HEAD_DIM // 2
    lanes = values.shape[1]
    lane = lax.broadcasted_iota(jnp.int32, values.shape, 1) % HEAD_DIM
    after = pltpu.roll(values, lanes - half, 1)
    before = pltpu.roll(values, half, 1)
    wide = lambda t: jnp.concatenate([t] * (lanes // t.shape[1]), 1)
    return values * wide(cosine) + jnp.where(lane < half, -after, before) * wide(sine)


def attend_block(query, keys, values, same, heads):
    lane = lax.broadcasted_iota(jnp.int32, query.shape, 1) // HEAD_DIM
    result = jnp.zeros(query.shape, f32)
    for head in range(heads):
        own = jnp.where(lane == head, query, jnp.zeros_like(query))
        scores = dot(own, keys, (1,), (1,)) * HEAD_DIM ** (-0.5)
        scores = jnp.where(same, scores, negative)
        weights = jnp.exp(scores - jnp.max(scores, 1, keepdims=True))
        probs = (weights * (1.0 / jnp.sum(weights, 1, keepdims=True))).astype(bf16)
        result = jnp.where(lane == head, dot(probs, values, (1,), (0,)), result)
    return result.astype(bf16)


def front_kernel(
    dims,
    rows_ref,
    slot_ref,
    more_ref,
    cos_ref,
    sin_ref,
    segq_ref,
    segk_ref,
    *refs,
):
    ins, outs, (x_ref, q_ref, k_ref, v_ref, swap_ref), stages = refs[:5], refs[5:10], refs[10:15], refs[15:20]
    (
        got_ref,
        heads_ref,
        pick_ref,
        send_ref,
        load_sem,
        store_sem,
        main_send,
        main_recv,
        small_send,
        small_recv,
        late_send,
        late_recv,
        row_send,
        row_recv,
        heads_sem,
        swap_send,
        swap_recv,
    ) = refs[20:]
    H, X, C, Z = dims
    wires = Wires(row_send)
    at = wires.at
    h, x, c, z = at["h"], at["x"], at["c"], at["z"]
    across, beside, away = wires.peer(x=1 - x), wires.peer(c=1 - c), wires.peer(h=1 - h)
    team = x * C + c
    wires.greet(
        [(None, across), (None, beside), (None, away), (None, wires.peer(x=1 - x, c=1 - c))]
        + [(z + 1 < Z, wires.peer(z=z + 1)), (z >= 1, wires.peer(z=z - 1))]
    )
    loads = [pltpu.make_async_copy(ins[i], stages[i], load_sem.at[i]) for i in range(5)]
    stores = [
        pltpu.make_async_copy(stages[i], outs[i].at[z, h, x, c], store_sem.at[i]) for i in range(5)
    ]
    for load in loads:
        load.start()

    def owner_rows(y, d, g):
        return got_ref.at[y, d, g], row_recv.at[y, d, g]

    wires.send(rows_ref.at[1 - h], *owner_rows(x, c, h), away)
    wires.send(rows_ref.at[h], *owner_rows(x, c, h), across)
    wires.send(rows_ref.at[h], *owner_rows(x, c, h), beside)
    got_ref[x, c, h] = rows_ref[h]
    for load, store in zip(loads, stores):
        load.wait()
        store.start()
    small = Spread(wires, dims, [1], stages[:1], outs[:1], small_send, small_recv)
    main = Spread(wires, dims, [0, 0, 1], stages[1:4], outs[1:4], main_send, main_recv)
    late = Late(wires, dims, stages[4], outs[4], late_send, late_recv)
    spots = main.spots
    small.run((0, 1), 0, 1)
    late.step("across")
    main.run((0,), 0, 1)
    small.run((0, 1), 1, 3)
    place = owner_rows(x, c, 1 - h)
    wires.arrived(*place)
    wires.send(place[0], *place, across)
    wires.send(place[0], *place, beside)
    small.run((2,), 0, 1)
    main.run((0,), 1, 3)
    stores[4].wait()
    late.step("away")
    small.run((0, 1), 3, 5)
    small.run((2,), 1, 3)
    for g in (h, 1 - h):
        place = owner_rows(1 - x, c, g)
        wires.arrived(*place)
        wires.send(place[0], *place, beside)
    small.run((3,), 0, 1)
    small.run((0, 1), 5, spots)
    main.run((0,), 3, 5)
    small.run((2,), 3, 5)
    small.run((3,), 1, 3)
    late.step(0)
    small.run((2,), 5, spots)
    main.run((1,), 0, 3)
    main.run((0,), 5, spots)
    main.run((1,), 3, spots)
    small.run((3,), 3, spots)
    stores[0].wait()
    small.run((4,), 0, spots)
    heads = pltpu.make_async_copy(outs[0].at[team], heads_ref, heads_sem)
    heads.start()
    for y in (x, 1 - x):
        for g in (h, 1 - h):
            wires.arrived(*owner_rows(y, 1 - c, g))
    heads.wait()

    length, width = x_ref.shape
    heads_width = send_ref.shape[1]
    lanes = q_ref.shape[1]
    merged = heads_ref[...].reshape(width, heads_ref.shape[-1])
    for part in range(3):
        choose = selection(lanes, 3 * heads_width, part * heads_width)
        row = lax.broadcasted_iota(jnp.int32, choose.shape, 0)
        choose = jnp.where(row < heads_width, choose, jnp.zeros_like(choose))
        pick_ref[part] = dot(merged, choose, (1,), (1,)).astype(bf16)
    block = min(256, length)
    blocks = length // block
    slots = got_ref.shape[0] * got_ref.shape[1] * got_ref.shape[2] * got_ref.shape[3]

    @pl.loop(0, blocks)
    def _(i):
        here = pl.ds(pl.multiple_of(i * block, block), block)
        slot = lax.broadcasted_iota(jnp.int32, (block, slots), 1)
        chosen = (slot_ref[here, :] == slot).astype(bf16)
        full = dot(chosen, got_ref[...].reshape(slots, width), (1,), (0,))
        low = (full + more_ref[here, :].astype(f32)).astype(bf16)
        x_ref[here, :] = low
        cosine, sine = cos_ref[here, :], sin_ref[here, :]
        q_ref[here, :] = turned(dot(low, pick_ref[0], (1,), (0,)), cosine, sine).astype(bf16)
        k_ref[here, :] = turned(dot(low, pick_ref[1], (1,), (0,)), cosine, sine).astype(bf16)
        v_ref[here, :] = dot(low, pick_ref[2], (1,), (0,)).astype(bf16)

        @pl.when(i == 2)
        def _():
            late.step(1)
            late.step(2)

    main.run((2,), 0, 3)
    own_len = length // (X * C)

    @pl.loop(0, blocks)
    def _(i):
        here = pl.ds(pl.multiple_of(i * block, block), block)
        same = segq_ref[here, :] == segk_ref[...]
        heads = heads_width // HEAD_DIM
        result = attend_block(q_ref[here, :], k_ref[...], v_ref[...], same, heads)
        send_ref[here, :] = result[:, :heads_width]

        @pl.when((i == 0) | (i == 2))
        def _():
            main.step(2, i + 3)
            main.step(2, i + 4)

        @pl.when(i == 1)
        def _():
            late.step(3)
            late.step(4)

        pl.when(i == 3)(lambda: main.step(3, 0))
        pl.when(i == 4)(lambda: main.step(3, 1))

    others = [(1 - x, c), (1 - x, 1 - c), (x, 1 - c)]

    def part_of(y, d):
        return send_ref.at[pl.ds(pl.multiple_of((y * C + d) * own_len, 128), own_len), :]

    swaps = [
        pltpu.make_async_remote_copy(
            src_ref=part_of(y, d),
            dst_ref=swap_ref.at[team],
            send_sem=swap_send.at[k],
            recv_sem=swap_recv.at[team],
            device_id=wires.peer(x=y, c=d),
            device_id_type=MESH,
        )
        for k, (y, d) in enumerate(others)
    ]
    for swap in swaps:
        swap.start()
    swap_ref[team] = send_ref[pl.ds(pl.multiple_of(team * own_len, 128), own_len), :]
    late.step(5)
    late.step(6)
    main.run((3,), 2, spots)
    main.run((4,), 0, spots)
    for y, d in others:
        wires.arrived(swap_ref.at[y * C + d], swap_recv.at[y * C + d])
    for swap in swaps:
        swap.wait_send()
    for store in stores[1:4]:
        store.wait()
    late.settle()
    main.settle()
    small.settle()
    wires.drain()


def front(rows, slot, more, cosine, sine, segments, pieces, heads_width, dims, number):
    H, X, C, Z = dims
    length, width = more.shape
    team = X * C
    spots = 2 * Z - 1
    batch = H * team
    rows_in = pieces[0].shape[0]
    lanes = -(-heads_width // 128) * 128
    vmem = lambda shape, dtype=bf16: pltpu.VMEM(shape, dtype)
    dma = lambda *shape: pltpu.SemaphoreType.DMA(shape)
    outs = call(
        partial(front_kernel, dims),
        (rows, slot[:, None], more, cosine, sine, segments[:, None], segments[None, :], *pieces),
        [jax.ShapeDtypeStruct((Z, H, X, C) + piece.shape, bf16) for piece in pieces]
        + [jax.ShapeDtypeStruct((length, width), bf16)]
        + [jax.ShapeDtypeStruct((length, lanes), bf16)] * 3
        + [jax.ShapeDtypeStruct((team, length // team, heads_width), bf16)],
        [anywhere] * 5 + [on_chip] * 5,
        [vmem(piece.shape) for piece in pieces]
        + [
            vmem((X, C) + rows.shape),
            vmem((H, X, C) + pieces[0].shape),
            vmem((3, width, lanes)),
            vmem((length, heads_width)),
            dma(5),
            dma(5),
            dma(3, 9, spots),
            dma(3, Z, batch),
            dma(1, 9, spots),
            dma(1, Z, batch),
            dma(3, spots),
            dma(3, Z),
            dma(7),
            dma(X, C, H),
            pltpu.SemaphoreType.DMA,
            dma(3),
            dma(team),
        ],
        number,
        in_specs=[on_chip] * 7 + [anywhere] * 5,
        vmem=60 * 2**20,
    )
    weights = [whole.reshape(Z, batch * rows_in, -1) for whole in outs[:5]]
    return weights, outs[5:]


def sum_rows(goal, sources):
    rows = goal.shape[0]
    step = 16 if rows % 16 == 0 else rows

    @pl.loop(0, rows // step)
    def _(i):
        part = pl.ds(pl.multiple_of(i * step, step), step)
        value = sources[0][part, :].astype(f32)
        for source in sources[1:]:
            value += source[part, :].astype(f32)
        goal[part, :] = value.astype(goal.dtype)


class Line:
    def __init__(self, wires, Z, buffers, send_sem, recv_sem):
        self.wires, self.Z, self.buffers = wires, Z, buffers
        self.send_sem, self.recv_sem = send_sem, recv_sem

    def onward(self, a, s, source):
        z = self.wires.at["z"]
        upward = z < s
        goal = jnp.where(upward, z + 1, z - 1)
        index = jnp.where((s < goal) | upward, s, self.Z)
        return pltpu.make_async_remote_copy(
            src_ref=source,
            dst_ref=self.buffers[a].at[index],
            send_sem=self.send_sem.at[a, s],
            recv_sem=self.recv_sem.at[a, index],
            device_id=self.wires.peer(z=goal),
            device_id_type=MESH,
        )

    def step(self, a, s, sources, running, final):
        z, Z = self.wires.at["z"], self.Z

        def took(index):
            view = self.buffers[a].at[index]
            self.wires.arrived(view, self.recv_sem.at[a, index])
            return view

        passing = z != s
        edge = ((z < s) & (z == 0)) | ((z > s) & (z == Z - 1))

        @pl.when(passing & edge)
        def _():
            sum_rows(running, sources)

        @pl.when(passing & ~edge)
        def _():
            sum_rows(running, sources + [took(s)])

        @pl.when(passing)
        def _():
            self.onward(a, s, running).start()

        @pl.when((z == s) & (z == 0))
        def _():
            sum_rows(final, sources + [took(Z)])

        @pl.when((z == s) & (z == Z - 1))
        def _():
            sum_rows(final, sources + [took(s)])

        @pl.when((z == s) & (z > 0) & (z < Z - 1))
        def _():
            sum_rows(final, sources + [took(s), took(Z)])

    def settle(self, a, s, running):
        @pl.when(self.wires.at["z"] != s)
        def _():
            self.onward(a, s, running).wait_send()


class Gathering:
    def __init__(self, wires, dims, kinds, ins, outs, own, near, first, second, lines, sems):
        self.wires, self.kinds, self.Z = wires, kinds, dims[3]
        self.ins, self.outs, self.own, self.near = ins, outs, own, near
        self.first, self.second = first, second
        self.load_sem, self.near_sem, self.first_sem, self.second_sem = sems[:4]
        self.near_send, self.first_send, self.second_send = sems[4:7]
        self.line = Line(wires, dims[3], lines, sems[7], sems[8])
        at = wires.at
        self.x, self.h, self.c, self.z = at["x"], at["h"], at["c"], at["z"]
        self.across, self.beside = wires.peer(x=1 - self.x), wires.peer(c=1 - self.c)
        self.away = wires.peer(h=1 - self.h)

    def turn(self, i):
        Z = self.Z
        low = self.z < Z // 2
        side = jnp.where(low, self.z, Z - 1 - self.z)
        s = jnp.where(i < Z - 1 - side, Z - 1 - i, jnp.where(i < Z - 1, i - (Z - 1 - side), side))
        return jnp.where(low, s, Z - 1 - s)

    def remote(self, source, goal, send_sem, recv_sem, target):
        return pltpu.make_async_remote_copy(
            src_ref=source,
            dst_ref=goal,
            send_sem=send_sem,
            recv_sem=recv_sem,
            device_id=target,
            device_id_type=MESH,
        )

    def load(self, a, s):
        return pltpu.make_async_copy(
            self.ins[a].at[s, :, :, self.c], self.own[a].at[s], self.load_sem.at[a, s]
        )

    def near_copy(self, a, s):
        return self.remote(
            self.ins[a].at[s, :, :, 1 - self.c],
            self.near[a].at[s],
            self.near_send.at[a, s],
            self.near_sem.at[a, s],
            self.beside,
        )

    def axes(self, a):
        return (self.x, self.h) if self.kinds[a] == 0 else (self.h, self.x)

    def spot(self, a, s, f, g):
        return (s, g, f) if self.kinds[a] == 0 else (s, f, g)

    def first_copy(self, a, s, g):
        f, _ = self.axes(a)
        return self.remote(
            self.own[a].at[self.spot(a, s, 1 - f, g)],
            self.first[a].at[s, g],
            self.first_send.at[a, s, g],
            self.first_sem.at[a, s, g],
            self.across if self.kinds[a] == 0 else self.away,
        )

    def second_copy(self, a, s):
        f, g = self.axes(a)
        return self.remote(
            self.own[a].at[self.spot(a, s, f, 1 - g)],
            self.second[a].at[s],
            self.second_send.at[a, s],
            self.second_sem.at[a, s],
            self.away if self.kinds[a] == 0 else self.across,
        )

    def begin(self):
        @pl.loop(0, self.Z)
        def _(i):
            s = self.turn(i)
            for a in range(len(self.kinds)):
                self.near_copy(a, s).start()
                self.load(a, s).start()

    def one(self, i):
        s = self.turn(i)
        for a in range(len(self.kinds)):
            self.wires.arrived(self.near[a].at[s], self.near_sem.at[a, s])
            self.load(a, s).wait()
            f, g = self.axes(a)
            for k in (1 - g, g):
                place = self.spot(a, s, 1 - f, k)
                sum_rows(self.own[a].at[place], [self.own[a].at[place], self.near[a].at[place]])
                self.first_copy(a, s, k).start()

    def two(self, i):
        s = self.turn(i)
        for a in range(len(self.kinds)):
            f, g = self.axes(a)
            for k in (1 - g, g):
                self.wires.arrived(self.first[a].at[s, k], self.first_sem.at[a, s, k])
            place = self.spot(a, s, f, 1 - g)
            sum_rows(
                self.own[a].at[place],
                [self.own[a].at[place], self.near[a].at[place], self.first[a].at[s, 1 - g]],
            )
            self.second_copy(a, s).start()

    def three(self, i):
        s = self.turn(i)
        for a in range(len(self.kinds)):
            f, g = self.axes(a)
            self.wires.arrived(self.second[a].at[s], self.second_sem.at[a, s])
            place = self.spot(a, s, f, g)
            own = self.own[a].at[place]
            sources = [own, self.near[a].at[place], self.first[a].at[s, g], self.second[a].at[s]]
            self.line.step(a, s, sources, own, self.outs[a])

    def settle(self):
        @pl.loop(0, self.Z)
        def _(s):
            for a in range(len(self.kinds)):
                self.near_copy(a, s).wait_send()
                for k in range(2):
                    self.first_copy(a, s, k).wait_send()
                self.second_copy(a, s).wait_send()
                f, g = self.axes(a)
                self.line.settle(a, s, self.own[a].at[self.spot(a, s, f, g)])


def attend_back_block(query, grad, keys, values, same, heads, dk_ref, dv_ref):
    factor = HEAD_DIM ** (-0.5)
    lane = lax.broadcasted_iota(jnp.int32, query.shape, 1) // HEAD_DIM
    result = jnp.zeros(query.shape, f32)
    for head in range(heads):
        own = jnp.where(lane == head, query, jnp.zeros_like(query))
        own_grad = jnp.where(lane == head, grad, jnp.zeros_like(grad))
        scores = dot(keys, own, (1,), (1,)) * factor
        scores = jnp.where(same, scores, negative)
        weights = jnp.exp(scores - jnp.max(scores, 0, keepdims=True))
        probs = weights * (1.0 / jnp.sum(weights, 0, keepdims=True))
        grad_probs = dot(values, own_grad, (1,), (1,))
        inner = jnp.sum(probs * grad_probs, 0, keepdims=True)
        grad_scores = (probs * (grad_probs - inner)).astype(bf16)
        dk_ref[...] += dot(grad_scores, own, (1,), (0,)) * factor
        dv_ref[...] += dot(probs.astype(bf16), own_grad, (1,), (0,))
        result = jnp.where(lane == head, dot(grad_scores, keys, (0,), (0,)) * factor, result)
    return result


def back_kernel(
    dims,
    heads,
    swap_ref,
    q_ref,
    k_ref,
    v_ref,
    x_ref,
    cos_ref,
    sin_ref,
    segq_ref,
    segk_ref,
    slot_ref,
    first_ref,
    listq_ref,
    listk_ref,
    heads_ref,
    in_gate,
    in_up,
    in_down,
    in_misc,
    out_gate,
    out_up,
    out_down,
    out_misc,
    out_qkv,
    spread_ref,
    zero_ref,
    total_ref,
    *scratch,
):
    H, X, C, Z = dims
    scratch = list(scratch)
    take = lambda n: [scratch.pop(0) for _ in range(n)]
    own, near, first, second, lines = (take(4) for _ in range(5))
    (got_ref, grad_ref, dk_ref, dv_ref, low_ref, matrix_ref, heads_v) = take(7)
    (qsrc, qnear, qx, qh, qtot, qline) = take(6)
    (slots_ref, beside_ref, across_ref, ready_ref) = take(4)
    sems = take(9)
    (swap_send, swap_recv, heads_sem, qsend, qrecv, qline_send, qline_recv) = take(7)
    (row_send, beside_sem, across_sem, row_recv, norm_ref, norm_send, norm_recv) = take(7)
    wires = Wires(row_send)
    wires.size_z = Z
    at = wires.at
    h, x, c, z = at["h"], at["x"], at["c"], at["z"]
    across, beside, away = wires.peer(x=1 - x), wires.peer(c=1 - c), wires.peer(h=1 - h)
    team = x * C + c
    devices = H * X * C * Z
    me = (team + h * X * C) * Z + z

    def coordinates(flat):
        return (flat // (X * C * Z), flat // (C * Z) % X, flat // Z % C, flat % Z)

    wires.greet([(None, coordinates((me + k) % devices)) for k in range(1, devices)])
    others = [(1 - x, c), (1 - x, 1 - c), (x, 1 - c)]
    swaps = [
        pltpu.make_async_remote_copy(
            src_ref=swap_ref.at[y * C + d],
            dst_ref=got_ref.at[team],
            send_sem=swap_send.at[k],
            recv_sem=swap_recv.at[team],
            device_id=wires.peer(x=y, c=d),
            device_id_type=MESH,
        )
        for k, (y, d) in enumerate(others)
    ]
    for swap in swaps:
        swap.start()
    fetch = pltpu.make_async_copy(heads_ref.at[team], heads_v, heads_sem)
    fetch.start()
    job = Gathering(
        wires,
        dims,
        [1, 1, 0, 0],
        [in_gate, in_up, in_down, in_misc],
        [out_gate, out_up, out_down, out_misc],
        own,
        near,
        first,
        second,
        lines,
        sems,
    )
    job.begin()
    got_ref[team] = swap_ref[team]
    dk_ref[...] = jnp.zeros_like(dk_ref)
    dv_ref[...] = jnp.zeros_like(dv_ref)
    matrix_ref[...] = jnp.zeros_like(matrix_ref)
    length, lanes = q_ref.shape
    heads_width = got_ref.shape[2]
    own_len = got_ref.shape[1]
    width = x_ref.shape[1]
    edge = (z == 0) | (z == Z - 1)
    job.one(0)
    widen = selection(heads_width, lanes, 0)
    for y, d in others:
        wires.arrived(got_ref.at[y * C + d], swap_recv.at[y * C + d])
    job.one(1)

    @pl.loop(0, X * C)
    def _(k):
        part = pl.ds(pl.multiple_of(k * own_len, 128), own_len)
        grad_ref[part, :] = dot(got_ref[k], widen, (1,), (0,)).astype(bf16)

    block = min(256, length)
    blocks = length // block

    def narrow(values, part):
        choose = selection(lanes, 3 * heads_width, part * heads_width)
        row = lax.broadcasted_iota(jnp.int32, choose.shape, 0)
        choose = jnp.where(row < heads_width, choose, jnp.zeros_like(choose))
        return dot(values.astype(bf16), choose, (1,), (0,))

    @pl.loop(0, blocks)
    def _(i):
        here = pl.ds(pl.multiple_of(i * block, block), block)
        same = segk_ref[...] == segq_ref[:, here]
        grad_query = attend_back_block(
            q_ref[here, :], grad_ref[here, :], k_ref[...], v_ref[...], same, heads, dk_ref, dv_ref
        )
        low_ref[here, :] = narrow(turned(grad_query, cos_ref[here, :], -sin_ref[here, :]), 0).astype(bf16)

        pl.when((i == 1) | (i == 3))(lambda: job.two(i // 2))
        pl.when((i == 2) | (i == 5))(lambda: job.one(2 + i // 5))
        pl.when((i == 4) & edge)(lambda: job.three(0))

    fetch.wait()

    @pl.loop(0, X * C)
    def _(k):
        part = pl.ds(pl.multiple_of(k * own_len, 128), own_len)
        grad_keys = turned(dk_ref[part, :], cos_ref[part, :], -sin_ref[part, :])
        low = low_ref[part, :].astype(f32) + narrow(grad_keys, 1) + narrow(dv_ref[part, :], 2)
        low = low.astype(bf16)
        zero = dot(low, heads_v[...], (1,), (1,))
        zero_ref[part, :] = (zero + (k == team).astype(f32) * first_ref[...]).astype(bf16)
        matrix_ref[...] += dot(x_ref[part, :], low, (0,), (0,))
        pl.when(k == 1)(lambda: job.two(2))
        pl.when(k == 2)(lambda: job.three(edge.astype(jnp.int32)))

    capacity = slots_ref.shape[3]

    def fill(y, d):
        for g in range(H):
            slot = lax.broadcasted_iota(jnp.int32, (capacity, length), 0)
            slot += ((y * C + d) * H + g) * capacity
            chosen = (slot_ref[...] == slot).astype(bf16)
            slots_ref[y, d, g] = dot(chosen, zero_ref[...], (1,), (0,)).astype(bf16)

    def row_copy(y):
        wires.send(slots_ref.at[y, 1 - c], beside_ref.at[y], beside_sem.at[y], beside)

    fill(1 - x, 1 - c)
    row_copy(1 - x)
    fill(x, 1 - c)
    row_copy(x)
    fill(1 - x, c)
    wires.arrived(beside_ref.at[1 - x], beside_sem.at[1 - x])
    for g in (1 - h, h):
        total = slots_ref[1 - x, c, g].astype(f32) + beside_ref[1 - x, g].astype(f32)
        ready_ref[g] = total.astype(bf16)
        wires.send(ready_ref.at[g], across_ref.at[g], across_sem.at[g], across)
    fill(x, c)
    rows_in, wide = qsrc.shape[3], qsrc.shape[4]
    qsrc[...] = matrix_ref[...].astype(bf16).reshape(qsrc.shape)

    def qcopy(source, goal, k, target):
        return pltpu.make_async_remote_copy(
            src_ref=source,
            dst_ref=goal,
            send_sem=qsend.at[k],
            recv_sem=qrecv.at[k],
            device_id=target,
            device_id_type=MESH,
        )

    qcopies = [
        qcopy(qsrc.at[:, :, 1 - c], qnear, 0, beside),
        qcopy(qsrc.at[:, 1 - x, c], qx.at[0], 1, across),
        qcopy(qnear.at[:, 1 - x], qx.at[1], 2, across),
        qcopy(qsrc.at[1 - h, x, c], qh.at[0], 3, away),
        qcopy(qnear.at[1 - h, x], qh.at[1], 4, away),
        qcopy(qx.at[0, 1 - h], qh.at[2], 5, away),
        qcopy(qx.at[1, 1 - h], qh.at[3], 6, away),
    ]
    qcopies[0].start()
    wires.arrived(beside_ref.at[x], beside_sem.at[x])
    job.three(2)
    pl.when(~edge)(lambda: job.three(1))
    for g in (1 - h, h):
        wires.arrived(across_ref.at[g], across_sem.at[g])
        total = slots_ref[x, c, g].astype(f32) + beside_ref[x, g].astype(f32)
        total = (total + across_ref[g].astype(f32)).astype(bf16)
        if g is h:
            spread_ref[z, h] = total
        else:
            ready_ref[2 + g] = total
            wires.send(ready_ref.at[2 + g], spread_ref.at[z, h], row_recv.at[z, h], away)
    wires.arrived(qnear, qrecv.at[0])
    for k in range(1, 5):
        qcopies[k].start()
    job.two(3)
    wires.arrived(spread_ref.at[z, 1 - h], row_recv.at[z, 1 - h])

    def row_line(far):
        for sign in (-1, 1):
            spot = z + sign * far
            onward = z - sign
            more = (onward >= 0) & (onward < Z)
            there = None if far == 0 else (spot >= 0) & (spot < Z)
            if far:
                wires.arrived(spread_ref.at[spot], row_recv.at[spot, H], there)
            wires.send(
                spread_ref.at[spot], spread_ref.at[spot], row_recv.at[spot, H], wires.peer(z=onward), both(there, more)
            )

    row_line(0)
    for k in (1, 2):
        wires.arrived(qx.at[k - 1], qrecv.at[k])
    qcopies[5].start()
    qcopies[6].start()
    row_line(1)
    for k in range(4):
        wires.arrived(qh.at[k], qrecv.at[3 + k])
    terms = [qsrc.at[h, x, c], qnear.at[h, x], qx.at[0, h], qx.at[1, h]]
    pair = (team, x * C + 1 - c, (1 - x) * C + c, (1 - x) * C + 1 - c)
    for k in range(4):
        sum_rows(qtot.at[pair[k]], [terms[k], qh.at[k]])
    line = Line(wires, Z, [qline], qline_send, qline_recv)

    def heads_line(i):
        s = job.turn(i)
        line.step(0, s, [qtot.at[s]], qtot.at[s], out_qkv)

    pl.loop(0, 2)(heads_line)
    for far in range(2, Z - 1):
        row_line(far)
    pl.loop(2, Z - 1)(heads_line)
    row_line(Z - 1)
    heads_line(Z - 1)
    job.three(3)
    quarter = H * capacity
    mine = pl.ds(pl.multiple_of(z * quarter, 8), quarter)
    products = dot(
        spread_ref[z].reshape(quarter, width), spread_ref[...].reshape(Z * quarter, width), (1,), (1,)
    )
    squares = jnp.sum(jnp.where(listq_ref[mine, :] == listk_ref[...], products, 0.0))
    for ref in (out_gate, out_up, out_down, out_qkv):
        squares += jnp.sum(ref[...] * ref[...])
    lane = lax.broadcasted_iota(jnp.int32, out_misc.shape, 1)
    squares += jnp.sum(out_misc[...] * out_misc[...] * jnp.where(lane < heads_width, 1.0, 1.0 / Z))
    norm_ref[me] = jnp.full(norm_ref.shape[1:], squares)

    @pl.loop(0, Z)
    def _(s):
        line.settle(0, s, qtot.at[s])

    for copy in qcopies:
        copy.wait_send()
    for swap in swaps:
        swap.wait_send()
    job.settle()
    wires.drain()
    tell = [
        pltpu.make_async_remote_copy(
            src_ref=norm_ref.at[me],
            dst_ref=norm_ref.at[me],
            send_sem=norm_send.at[k],
            recv_sem=norm_recv.at[k],
            device_id=coordinates((me + k) % devices),
            device_id_type=MESH,
        )
        for k in range(1, devices)
    ]
    for copy in tell:
        copy.start()
    for k in range(1, devices):
        wires.arrived(norm_ref.at[(me + devices - k) % devices], norm_recv.at[k])
    total_ref[...] = jnp.sum(norm_ref[...], 0)
    for copy in tell:
        copy.wait_send()


def back(swap, q, k, v, x_low, cosine, sine, segments, slot, listed, grad_first, w_heads, terms, heads, capacity, dims, number):
    H, X, C, Z = dims
    length, width = x_low.shape
    lanes = q.shape[1]
    team, own_len, heads_width = swap.shape
    batch = H * team
    rows = width // batch
    widths = [term.shape[2] for term in terms]
    wide = 3 * heads_width
    vmem = lambda shape, dtype=bf16: pltpu.VMEM(shape, dtype)
    dma = lambda *shape: pltpu.SemaphoreType.DMA(shape)
    shapes = [(Z, H, X), (Z, H, X), (Z, 2), (Z,), (Z + 1,)]
    n = len(terms)
    return call(
        partial(back_kernel, dims, heads),
        (
            swap,
            q,
            k,
            v,
            x_low,
            cosine,
            sine,
            segments[None, :],
            segments[:, None],
            slot[None, :],
            grad_first,
            listed[:, None],
            listed[None, :],
            w_heads,
            *(term.reshape(Z, H, X, C, rows, -1) for term in terms),
        ),
        [jax.ShapeDtypeStruct((rows, w), f32) for w in widths + [wide]]
        + [
            jax.ShapeDtypeStruct((Z, H, capacity, width), bf16),
            jax.ShapeDtypeStruct((length, width), bf16),
            jax.ShapeDtypeStruct((8, 128), f32),
        ],
        [on_chip] * 8,
        [vmem(shape + (rows, w)) for shape in shapes for w in widths]
        + [
            vmem(swap.shape),
            vmem((length, lanes)),
            vmem((length, lanes), f32),
            vmem((length, lanes), f32),
            vmem((length, wide)),
            vmem((width, wide), f32),
            vmem(w_heads.shape[1:]),
            vmem((H, X, C, rows, wide)),
            vmem((H, X, rows, wide)),
            vmem((2, H, rows, wide)),
            vmem((4, rows, wide)),
            vmem((Z, rows, wide)),
            vmem((Z + 1, rows, wide)),
            vmem((X, C, H, capacity, width)),
            vmem((X, H, capacity, width)),
            vmem((H, capacity, width)),
            vmem((2 * H, capacity, width)),
            dma(n, Z),
            dma(n, Z),
            dma(n, Z, 2),
            dma(n, Z),
            dma(n, Z),
            dma(n, Z, 2),
            dma(n, Z),
            dma(n, Z),
            dma(n, Z + 1),
            dma(3),
            dma(team),
            pltpu.SemaphoreType.DMA,
            dma(7),
            dma(7),
            dma(1, Z),
            dma(1, Z + 1),
            dma(2 + 2 + 1 + 2 * Z),
            dma(X),
            dma(H),
            dma(Z, H + 1),
            vmem((batch * Z, 8, 128), f32),
            dma(batch * Z),
            dma(batch * Z),
        ],
        number,
        in_specs=[on_chip] * 13 + [anywhere] * 5,
        vmem=67_000_000,
    )


def adam_update(weight, grad, first, second, rate):
    first = 0.5 * first + 0.5 * grad
    second = 0.5 * second + 0.5 * grad * grad
    correction = 1.0 - 0.5**step_number
    weight = weight - rate * (
        first / correction / (jnp.sqrt(second / correction) + 1e-08) + 0.01 * weight
    )
    return (weight, first, second)


def blank(shape, dtype):
    return pl.pallas_call(
        lambda o_ref: None, out_specs=anywhere, out_shape=jax.ShapeDtypeStruct(shape, dtype)
    )()


def rows_kernel(list_ref, table_ref, o_ref, hold_ref, sem):
    count = o_ref.shape[0]

    @pl.loop(0, count)
    def _(i):
        row = pl.ds(list_ref[i], 1)
        pltpu.make_async_copy(table_ref.at[row, :], hold_ref.at[pl.ds(i, 1), :], sem).start()

    pltpu.make_async_copy(hold_ref, hold_ref, sem).wait()
    o_ref[...] = hold_ref[...].astype(bf16)


def low_rows(table, listed):
    shape = (listed.shape[0], table.shape[1])
    return pl.pallas_call(
        rows_kernel,
        in_specs=[pl.BlockSpec(memory_space=pltpu.SMEM), anywhere],
        out_specs=on_chip,
        out_shape=jax.ShapeDtypeStruct(shape, bf16),
        scratch_shapes=[pltpu.VMEM(shape, f32), pltpu.SemaphoreType.DMA],
    )(listed, table)


def table_kernel(rate, rounds_ref, scale_ref, list_ref, rows_ref, more_ref, w_ref, m_ref, v_ref, nw_ref, g_ref, nv_ref, far_ref, sem):
    block, width = w_ref.shape
    count = list_ref.shape[1]
    start = pl.program_id(0) * block

    def placed(turn, rows):
        row = lax.broadcasted_iota(jnp.int32, (block, count), 0) + start
        pick = (row == list_ref[pl.ds(turn, 1), :]).astype(bf16)
        return dot(pick, rows, (1,), (0,))

    g_ref[...] = placed(0, rows_ref[...])

    @pl.loop(1, rounds_ref[0])
    def _(turn):
        copy = pltpu.make_async_copy(more_ref.at[turn - 1], far_ref, sem)
        copy.start()
        copy.wait()
        g_ref[...] += placed(turn, far_ref[...])

    grad = g_ref[...] * scale_ref[0]
    new_w, _, new_v = adam_update(w_ref[...], grad, m_ref[...], v_ref[...], rate)
    g_ref[...] = grad
    nw_ref[...] = new_w
    nv_ref[...] = new_v


def update_table(rounds, scale, lists, rows, more, table, first, second, rate):
    height, width = table.shape
    sizes = [n for n in range(8, 513, 8) if height % n == 0]
    block = max(sizes) if sizes else height
    part = pl.BlockSpec((block, width), lambda i: (i, 0))
    whole = lambda a: pl.BlockSpec(a.shape, lambda i: (0,) * a.ndim)
    single = pl.BlockSpec(memory_space=pltpu.SMEM)
    return pl.pallas_call(
        partial(table_kernel, rate),
        grid=(height // block,),
        in_specs=[single, single, whole(lists), whole(rows), anywhere, part, part, part],
        out_specs=[part] * 3,
        out_shape=[jax.ShapeDtypeStruct(table.shape, f32)] * 3,
        scratch_shapes=[pltpu.VMEM(rows.shape, bf16), pltpu.SemaphoreType.DMA],
        compiler_params=pltpu.CompilerParams(vmem_limit_bytes=56 * 2**20),
    )(rounds.reshape(1), scale.reshape(1), lists, rows, more, table, first, second)


def small_kernel(scale_ref, qkv_ref, misc_ref, gate_ref, up_ref, down_ref, *refs):
    ins, outs = refs[:15], refs[15:]
    scale = scale_ref[0]
    heads_width = ins[0].shape[2]
    turned_misc = misc_ref[...].T

    def update(k, grad, where):
        old, first, second = (ins[3 * k + n][where] for n in range(3))
        for n, value in enumerate(adam_update(old, grad * scale, first, second, rates[1 + k])):
            outs[3 * k + n][where] = value

    for part in range(3):
        grad = qkv_ref[:, part * heads_width : (part + 1) * heads_width]
        update(0, grad, part)
    update(1, turned_misc[:heads_width], (slice(None), slice(None)))
    update(2, gate_ref[...], (slice(None), 0, slice(None)))
    update(2, up_ref[...], (slice(None), 1, slice(None)))
    update(3, down_ref[...], (slice(None), slice(None)))
    count = ins[12].shape[0]
    update(4, turned_misc[heads_width : heads_width + count], (slice(None), slice(None)))


def update_small(scale, sums, olds, firsts, seconds):
    views = (lambda a: a.transpose(1, 0, 2), lambda a: a, lambda a: a, lambda a: a.T, lambda a: a)
    groups = zip(views, zip(olds, firsts, seconds))
    values = [view(value) for view, group in groups for value in group]
    whole = lambda a: pl.BlockSpec(a.shape, lambda i: (0,) * a.ndim)
    outs = pl.pallas_call(
        small_kernel,
        grid=(1,),
        in_specs=[pl.BlockSpec(memory_space=pltpu.SMEM)] + [whole(a) for a in (*sums, *values)],
        out_specs=[whole(a) for a in values],
        out_shape=[jax.ShapeDtypeStruct(value.shape, f32) for value in values],
        compiler_params=pltpu.CompilerParams(vmem_limit_bytes=50 * 2**20),
    )(scale.reshape(1), *sums, *values)
    return [tuple(view(new) for new in outs[3 * k : 3 * k + 3]) for k, view in enumerate(views)]


def local(
    dims,
    token_ids,
    segment_ids,
    row_of,
    query_count,
    table,
    qkv_weight,
    out_weight,
    gate_up_weight,
    down_weight,
    gains,
    table_m,
    qkv_m,
    out_m,
    gate_up_m,
    down_m,
    gains_m,
    table_v,
    qkv_v,
    out_v,
    gate_up_v,
    down_v,
    gains_v,
):
    H, X, C, Z = dims
    G = X * C
    batch = H * G
    at = {name: lax.axis_index(name) for name in ALL}
    team = at["x"] * C + at["c"]
    owner = at["h"] * G + team
    length = token_ids.shape[1]
    own_len = length // G
    part_len = length // Z
    shard_rows, width = table.shape
    rows_in = width // batch
    heads_width = qkv_weight.shape[2]
    ff_part = down_weight.shape[0]
    capacity = -(-3 * length // (64 * batch)) * 16

    position = jnp.arange(length, dtype=jnp.int32)
    start = at["z"] * part_len
    mine = lax.dynamic_slice_in_dim(token_ids[0], start, part_len, 0)
    mine_seg = lax.dynamic_slice_in_dim(segment_ids[0], start, part_len, 0)
    earlier = position[None, :] < (start + position[:part_len])[:, None]
    seen = jnp.any((mine[:, None] == token_ids[0][None, :]) & earlier, 1)
    tags = jnp.stack([row_of[mine] * 2 + seen.astype(jnp.int32), mine_seg])
    everyone = gather_everyone(tags, dims, 0)
    tags_all = everyone[:, 0].reshape(batch, length)
    segs_all = everyone[:, 1].reshape(batch, length)
    ids_all, fresh_all = tags_all // 2, tags_all % 2 == 0
    row = at["h"] * Z + at["z"]
    seg_row = lax.dynamic_index_in_dim(segs_all, row, 0, keepdims=False)
    ids_row = lax.dynamic_index_in_dim(ids_all, row, 0, keepdims=False)
    fresh_row = lax.dynamic_index_in_dim(fresh_all, row, 0, keepdims=False)

    def counted(flags):
        lanes = 128 if length % 128 == 0 else length
        steps = flags.astype(f32).reshape(-1, length // lanes, lanes)
        upto = jnp.arange(lanes)[:, None] <= jnp.arange(lanes)[None, :]
        inner = jnp.einsum("rgl,lk->rgk", steps, upto.astype(f32))
        sums = inner[:, :, -1]
        groups = jnp.arange(length // lanes)
        before = (groups[:, None] < groups[None, :]).astype(f32)
        outer = jnp.dot(sums, before, precision=peak_affinity)
        return (inner + outer[:, :, None]).reshape(-1, length).astype(jnp.int32)

    owned = fresh_all & (ids_all // shard_rows == owner)
    number = counted(owned)
    shares = (ids_all // shard_rows)[:, None, :] == jnp.arange(batch, dtype=jnp.int32)[None, :, None]
    shares = jnp.sum((shares & fresh_all[:, None, :]).astype(jnp.int32), 2)
    rounds = (jnp.max(shares) + capacity - 1) // capacity
    offset = jnp.where(owned, number, 0)
    spot = jnp.arange(1, capacity + 1, dtype=jnp.int32)

    def owned_list(turn, rows):
        ids = lax.dynamic_slice_in_dim(ids_all, rows[0], rows[1], 0) if rows else ids_all
        places = lax.dynamic_slice_in_dim(offset, rows[0], rows[1], 0) if rows else offset
        hit = (spot + turn * capacity)[None, :, None] == places[:, None, :]
        return jnp.sum(jnp.where(hit, (ids - owner * shard_rows + 1)[:, None, :], 0), 2) - 1

    holder_row = ids_row // shard_rows
    holders = jnp.arange(batch, dtype=jnp.int32)
    split = fresh_row[None, :] & (holder_row[None, :] == holders[:, None])
    number_row = jnp.sum(jnp.where(split, counted(split), 0), 0)
    same_row = ids_row[:, None] == ids_row[None, :]
    rank_row = jnp.sum(jnp.where(same_row, number_row[None, :], 0), 1) - 1
    slots = batch * capacity

    def listed_for(turn):
        return owned_list(turn, None).reshape(H, Z, capacity).transpose(1, 0, 2).reshape(-1)

    def slot_of(turn):
        rank = rank_row - turn * capacity
        slot = ((holder_row % G) * H + holder_row // G) * capacity + rank
        return jnp.where((rank >= 0) & (rank < capacity), slot, -1)

    def expander(turn):
        slot = slot_of(turn)
        return (slot[:, None] == jnp.arange(slots, dtype=jnp.int32)[None, :]).astype(bf16)

    labels = jnp.arange(SEGS, dtype=jnp.int32)
    marks = jnp.arange(SEGS + 1, dtype=jnp.int32)
    member_row = (seg_row[:, None] == marks[None, :]).astype(jnp.int32)
    counts_row = jnp.sum(member_row, 0)
    starts = jnp.cumsum(counts_row) - counts_row
    places = (position - jnp.sum(member_row * starts[None, :], 1)).astype(f32)
    cosine, sine = angles_of(places, HEAD_DIM)
    heads = heads_width // HEAD_DIM

    def rows_for(turn):
        listed = jnp.concatenate([owned_list(turn, (h * Z + at["z"], 1)) for h in range(H)])
        return low_rows(table, jnp.maximum(listed, 0).reshape(-1)).reshape(H, capacity, width)

    def fetch(turn):
        got = fetch_rows(rows_for(turn), dims, 1).reshape(slots, width)
        return jnp.dot(expander(turn), got, preferred_element_type=f32).astype(bf16)

    _, x_more = lax.while_loop(
        lambda s: s[0] < rounds,
        lambda s: (s[0] + 1, s[1] + fetch(s[0])),
        (jnp.int32(1), jnp.zeros((length, width), bf16)),
    )

    pad = -(-(heads_width + 2) // 128) * 128 - heads_width
    misc = jnp.concatenate([out_weight.T, gains.T, jnp.zeros((rows_in, pad - 2), f32)], 1)
    pieces = [
        qkv_weight.reshape(rows_in, -1).astype(bf16),
        misc.astype(bf16),
        gate_up_weight[:, 0].astype(bf16),
        gate_up_weight[:, 1].astype(bf16),
        down_weight.T.astype(bf16),
    ]
    if H == 2:
        tables = [jnp.concatenate([t[:, 0]] * 4, 1) for t in (cosine, sine)]
        weights, (x_low, query, keys, values, attended) = front(
            rows_for(0), slot_of(0), x_more, *tables, seg_row, pieces, heads_width, dims, 2
        )
    else:
        weights = gather_weights(pieces, dims)
    w_qkv, w_misc, w_gate, w_up, w_down = weights
    w_out = w_misc[:, :, :heads_width]
    gain = w_misc[0, :, heads_width : heads_width + 2].T.astype(f32)
    if H != 2:
        w_heads = lax.dynamic_index_in_dim(w_qkv, team, 0, keepdims=False)
        x_low = x_more + fetch(0)
        qkv = jnp.dot(x_low, w_heads, preferred_element_type=f32).reshape(length, 3, heads, HEAD_DIM)
        query = rotate(qkv[:, 0], cosine, sine).astype(bf16).reshape(length, -1)
        keys = rotate(qkv[:, 1], cosine, sine).astype(bf16).reshape(length, -1)
        values = qkv[:, 2].astype(bf16).reshape(length, -1)
        attended_heads = attend(query, keys, values, seg_row)
        attended = team_swap(attended_heads.reshape(G, own_len, heads_width), dims, 3)
    x_own = lax.dynamic_slice_in_dim(x_low, team * own_len, own_len, 0)

    seg_own = lax.dynamic_slice_in_dim(seg_row, team * own_len, own_len, 0)
    counts_all = jnp.sum((segs_all[:, None, :] == labels[None, :, None]).astype(f32), -1).reshape(-1, 1)
    if H == 2:
        loss_value, grad_attended, grad_first, terms = middle(
            query_count, attended, x_own, gain, seg_own, counts_all, weights[2:] + [w_misc], dims, 4
        )
    else:
        attended = attended.transpose(1, 0, 2)
        attn = dot(attended, w_out, (1, 2), (0, 2))
        hidden_one, first_back = jax.vjp(layer_norm, x_own.astype(f32) + attn, gain[0])
        hidden_low = hidden_one.astype(bf16)
        gate = jnp.einsum("td,zdf->ztf", hidden_low, w_gate, preferred_element_type=f32)
        up = jnp.einsum("td,zdf->ztf", hidden_low, w_up, preferred_element_type=f32)
        active, swiglu_back = jax.vjp(swiglu, gate, up)
        active_low = active.astype(bf16)
        mlp = dot(active_low, w_down, (0, 2), (0, 2))
        hidden_two, second_back = jax.vjp(layer_norm, hidden_one + mlp, gain[1])

        loss_value, grad_two = contrast_all(hidden_two, seg_own, counts_all, query_count, dims)
        grad_second, grad_gain_two = second_back(grad_two)
        grad_mlp_low = grad_second.astype(bf16)
        grad_active = jnp.einsum("tn,znf->ztf", grad_mlp_low, w_down, preferred_element_type=f32)
        grad_down = jnp.einsum("tn,ztf->znf", grad_mlp_low, active_low, preferred_element_type=f32)
        grad_gate, grad_up = swiglu_back(grad_active)
        grad_gate_low, grad_up_low = grad_gate.astype(bf16), grad_up.astype(bf16)
        grad_one = grad_second + dot(grad_gate_low, w_gate, (0, 2), (0, 2))
        grad_one = grad_one + dot(grad_up_low, w_up, (0, 2), (0, 2))
        grad_first, grad_gain_one = first_back(grad_one)
        weight_grad = partial(jnp.einsum, "td,ztf->zdf", preferred_element_type=f32)
        grad_gate = weight_grad(hidden_low, grad_gate_low).astype(bf16)
        grad_up = weight_grad(hidden_low, grad_up_low).astype(bf16)
        grad_attn_low = grad_first.astype(bf16)
        grad_attended = jnp.einsum("tn,znk->tzk", grad_attn_low, w_out, preferred_element_type=f32)
        grad_attended = grad_attended.astype(bf16).transpose(1, 0, 2)
        grad_out = jnp.einsum("tn,tzk->znk", grad_attn_low, attended, preferred_element_type=f32)
        grad_gains = jnp.stack([grad_gain_one, grad_gain_two], 1)
        grad_misc = jnp.concatenate(
            [
                grad_out.astype(bf16),
                jnp.broadcast_to(grad_gains.astype(bf16)[None], (Z, width, 2)),
                jnp.zeros((Z, width, pad - 2), bf16),
            ],
            2,
        )
        terms = [grad_gate, grad_up, grad_down.astype(bf16), grad_misc]
    most_rounds = -(-length // capacity)
    listed = listed_for(0)
    _, lists = lax.while_loop(
        lambda s: s[0] < rounds,
        lambda s: (
            s[0] + 1,
            lax.dynamic_update_slice_in_dim(s[1], listed_for(s[0])[None], s[0], 0),
        ),
        (jnp.int32(1), jnp.broadcast_to(listed[None], (most_rounds,) + listed.shape)),
    )
    if H == 2:
        sum_gate, sum_up, sum_down, sum_misc, sum_qkv, spread, grad_zero_low, total = back(
            grad_attended,
            query,
            keys,
            values,
            x_low,
            *tables,
            seg_row,
            slot_of(0),
            listed,
            grad_first,
            w_qkv,
            terms,
            heads,
            capacity,
            dims,
            5,
        )
    else:
        grad_heads = team_swap(grad_attended, dims, 5).reshape(length, heads_width)
        grad_query, grad_keys, grad_values = attend_back(query, grad_heads, keys, values, seg_row)
        back_turn = lambda g: rotate(g.reshape(length, heads, HEAD_DIM), cosine, -sine).reshape(length, -1)
        grad_qkv_low = jnp.concatenate([back_turn(grad_query), back_turn(grad_keys), grad_values], 1)
        grad_qkv_low = grad_qkv_low.astype(bf16)
        grad_heads_w = dot(x_low, grad_qkv_low, (0,), (0,)).astype(bf16)
        grad_zero = dot(grad_qkv_low, w_heads, (1,), (1,))
        own_term = lax.dynamic_update_slice_in_dim(
            jnp.zeros_like(grad_zero), grad_first, team * own_len, 0
        )
        grad_zero_low = (grad_zero + own_term).astype(bf16)
        heads_grad = lax.dynamic_update_slice_in_dim(
            jnp.zeros((Z,) + grad_heads_w.shape, bf16), grad_heads_w[None], team, 0
        )
        sum_gate, sum_up, sum_down, sum_misc, sum_qkv = reduce_weights(terms + [heads_grad], dims)

    def collect(turn):
        terms = dot(expander(turn), grad_zero_low, (0,), (0,)).astype(bf16)
        terms = terms.reshape(X, C, H, capacity, width)
        return settle_rows(terms, dims, 6)

    flat = lambda rows: rows.reshape(Z * H * capacity, width)
    spread = flat(spread if H == 2 else collect(0))

    def between(left, left_list, right, right_list):
        same = left_list[:, None] == right_list[None, :]
        return jnp.sum(jnp.where(same, dot(left, right, (1,), (1,)), 0.0))

    def summed(squares):
        return jnp.sum(gather_everyone(jnp.full((8, 128), squares), dims, 8), 0)

    def further(state):
        turn, more, total = state
        rows = flat(collect(turn))
        listed = lists[turn]
        squares = between(rows, listed, rows, listed) + 2 * between(rows, listed, spread, lists[0])
        squares += 2 * lax.fori_loop(
            1, turn, lambda k, held: held + between(rows, listed, more[k - 1], lists[k]), jnp.zeros((), f32)
        )
        more = lax.dynamic_update_slice_in_dim(more, rows[None], turn - 1, 0)
        return turn + 1, more, total + summed(squares / Z)

    if H != 2:
        squares = between(spread, listed, spread, listed) + jnp.sum(sum_misc[:, heads_width:] ** 2)
        squares = squares / Z + jnp.sum(sum_misc[:, :heads_width] ** 2)
        for part in (sum_qkv, sum_gate, sum_up, sum_down):
            squares += jnp.sum(part * part)
        total = summed(squares)
    blank_rows = blank((max(most_rounds - 1, 1),) + spread.shape, bf16)
    _, more, total = lax.while_loop(
        lambda s: s[0] < rounds, further, (jnp.int32(1), blank_rows, total)
    )
    grad_norm = jnp.sqrt(total[0, 0])
    scale = clip_limit / jnp.maximum(grad_norm, clip_limit)
    new_table, clipped_table, new_table_v = update_table(
        rounds, scale, lists, spread, more, table, table_m, table_v, rates[0]
    )
    updated = update_small(
        scale,
        (sum_qkv, sum_misc, sum_gate, sum_up, sum_down),
        (qkv_weight, out_weight, gate_up_weight, down_weight, gains),
        (qkv_m, out_m, gate_up_m, down_m, gains_m),
        (qkv_v, out_v, gate_up_v, down_v, gains_v),
    )
    return (
        loss_value.reshape(1),
        grad_norm.reshape(1),
        new_table,
        *(new[0] for new in updated),
        clipped_table,
        *(new[1] for new in updated),
        new_table_v,
        *(new[2] for new in updated),
    )


def solution(mesh):
    batch, mp = mesh.shape["batch"], mesh.shape["mp"]
    dims = (batch // mp, mp // 2, 2, mp)
    split = Mesh(mesh.devices.reshape(dims), ALL)
    rows = ("h", "x", "c")
    weights = (
        P(rows, None),
        P(rows, None, "z"),
        P("z", rows),
        P(rows, None, "z"),
        P("z", rows),
        P(None, rows),
    )
    return jax.shard_map(
        partial(local, dims),
        mesh=split,
        in_specs=(P(rows, None), P(rows, None), P(), P()) + weights * 3,
        out_specs=(P(), P()) + weights + weights + weights,
        check_vma=False,
    )
```

```python
from functools import partial

import jax
import jax.numpy as jnp
from jax import lax
from jax.experimental import pallas as pl
from jax.experimental.pallas import tpu as pltpu
from jax.sharding import Mesh, PartitionSpec as P

HEAD_DIM = 64
SEGS = 8

peak_affinity = lax.Precision.HIGHEST
sharpness_divisor = 0.05
clip_limit = 1.0
step_number = 3.0
rates = (0.3, 0.02, 0.02, 0.02, 0.02, 0.3)
negative = -1e30
GROUP = ("x", "c")
ALL = ("h", "x", "c", "z")
f32 = jnp.float32
bf16 = jnp.bfloat16


def angles_of(places, head_dim):
    half_dim = head_dim // 2
    freqs = jnp.power(1000.0, -2.0 * jnp.arange(half_dim, dtype=f32) / head_dim)
    angles = places[:, None] * freqs[None, :]
    return jnp.cos(angles)[:, None, :], jnp.sin(angles)[:, None, :]


def rotate(values, cosine, sine):
    half_dim = values.shape[-1] // 2
    former = values[..., :half_dim]
    latter = values[..., half_dim:]
    return jnp.concatenate([former * cosine - latter * sine, latter * cosine + former * sine], -1)


def layer_norm(values, gain):
    centred = values - jnp.mean(values, -1, keepdims=True)
    spread = jnp.mean(centred * centred, -1, keepdims=True)
    return centred * lax.rsqrt(spread + 1e-05) * gain


def swiglu(gate, up):
    return jax.nn.silu(gate) * up


def dot(left, right, left_dims, right_dims, precision=None):
    return lax.dot_general(
        left, right, ((left_dims, right_dims), ((), ())), preferred_element_type=f32, precision=precision
    )


def attend_kernel(q_ref, k_ref, v_ref, segq_ref, segk_ref, o_ref):
    same = segq_ref[...] == segk_ref[...]
    query, keys, values = q_ref[...], k_ref[...], v_ref[...]
    width = query.shape[1]
    lane = lax.broadcasted_iota(jnp.int32, query.shape, 1) // HEAD_DIM
    result = jnp.zeros(query.shape, f32)
    for head in range(width // HEAD_DIM):
        own = jnp.where(lane == head, query, jnp.zeros_like(query))
        scores = dot(own, keys, (1,), (1,)) * HEAD_DIM ** (-0.5)
        scores = jnp.where(same, scores, negative)
        weights = jnp.exp(scores - jnp.max(scores, 1, keepdims=True))
        probs = (weights * (1.0 / jnp.sum(weights, 1, keepdims=True))).astype(bf16)
        result = jnp.where(lane == head, dot(probs, values, (1,), (0,)), result)
    o_ref[...] = result.astype(bf16)


def attend_back_kernel(q_ref, g_ref, k_ref, v_ref, segq_ref, segk_ref, dq_ref, dk_ref, dv_ref):
    @pl.when(pl.program_id(0) == 0)
    def _():
        dk_ref[...] = jnp.zeros_like(dk_ref)
        dv_ref[...] = jnp.zeros_like(dv_ref)

    same = segk_ref[...] == segq_ref[...]
    query, grad, keys, values = q_ref[...], g_ref[...], k_ref[...], v_ref[...]
    width = query.shape[1]
    factor = HEAD_DIM ** (-0.5)
    lane = lax.broadcasted_iota(jnp.int32, query.shape, 1) // HEAD_DIM
    result = jnp.zeros(query.shape, f32)
    for head in range(width // HEAD_DIM):
        own = jnp.where(lane == head, query, jnp.zeros_like(query))
        own_grad = jnp.where(lane == head, grad, jnp.zeros_like(grad))
        scores = dot(keys, own, (1,), (1,)) * factor
        scores = jnp.where(same, scores, negative)
        weights = jnp.exp(scores - jnp.max(scores, 0, keepdims=True))
        probs = weights * (1.0 / jnp.sum(weights, 0, keepdims=True))
        grad_probs = dot(values, own_grad, (1,), (1,))
        inner = jnp.sum(probs * grad_probs, 0, keepdims=True)
        grad_scores = (probs * (grad_probs - inner)).astype(bf16)
        dk_ref[...] += dot(grad_scores, own, (1,), (0,)) * factor
        dv_ref[...] += dot(probs.astype(bf16), own_grad, (1,), (0,))
        result = jnp.where(lane == head, dot(grad_scores, keys, (0,), (0,)) * factor, result)
    dq_ref[...] = result


def attend(query, keys, values, segment_row):
    length, width = query.shape
    block = min(256, length)
    whole = pl.BlockSpec((length, width), lambda i: (0, 0))
    part = pl.BlockSpec((block, width), lambda i: (i, 0))
    return pl.pallas_call(
        attend_kernel,
        grid=(length // block,),
        in_specs=[
            part,
            whole,
            whole,
            pl.BlockSpec((block, 1), lambda i: (i, 0)),
            pl.BlockSpec((1, length), lambda i: (0, 0)),
        ],
        out_specs=part,
        out_shape=jax.ShapeDtypeStruct((length, width), bf16),
    )(query, keys, values, segment_row[:, None], segment_row[None, :])


def attend_back(query, grad, keys, values, segment_row):
    length, width = query.shape
    block = min(256, length)
    whole = pl.BlockSpec((length, width), lambda i: (0, 0))
    part = pl.BlockSpec((block, width), lambda i: (i, 0))
    full = jax.ShapeDtypeStruct((length, width), f32)
    return pl.pallas_call(
        attend_back_kernel,
        grid=(length // block,),
        in_specs=[
            part,
            part,
            whole,
            whole,
            pl.BlockSpec((1, block), lambda i: (0, i)),
            pl.BlockSpec((length, 1), lambda i: (0, 0)),
        ],
        out_specs=[part, whole, whole],
        out_shape=[full, full, full],
    )(query, grad, keys, values, segment_row[None, :], segment_row[:, None])


MESH = pl.DeviceIdType.MESH
anywhere = pl.BlockSpec(memory_space=pl.ANY)
on_chip = pl.BlockSpec(memory_space=pltpu.VMEM)


def guarded(when, action):
    if when is None:
        action()
    else:
        pl.when(when)(action)


def both(first, second):
    return second if first is None else first if second is None else first & second


class Wires:
    def __init__(self, send_sem):
        self.at = {name: lax.axis_index(name) for name in ALL}
        self.send_sem = send_sem
        self.pending = []

    def peer(self, **moved):
        return tuple(moved.get(name, self.at[name]) for name in ALL)

    def greet(self, peers):
        barrier = pltpu.get_barrier_semaphore()
        expected = 0
        for when, target in peers:
            guarded(
                when,
                lambda target=target: pl.semaphore_signal(
                    barrier, inc=1, device_id=target, device_id_type=MESH
                ),
            )
            expected = expected + (1 if when is None else when.astype(jnp.int32))
        pl.semaphore_wait(barrier, expected)

    def send(self, source, goal, recv_sem, target, when=None):
        number = len(self.pending)

        def copy():
            return pltpu.make_async_remote_copy(
                src_ref=source,
                dst_ref=goal,
                send_sem=self.send_sem.at[number],
                recv_sem=recv_sem,
                device_id=target,
                device_id_type=MESH,
            )

        guarded(when, lambda: copy().start())
        self.pending.append((when, lambda: copy().wait_send()))

    def arrived(self, goal, recv_sem, when=None):
        guarded(when, lambda: pltpu.make_async_copy(goal, goal, recv_sem).wait())

    def drain(self):
        for when, wait in self.pending:
            guarded(when, wait)


def call(kernel, arguments, outs, out_specs, scratch, number, in_specs=None, vmem=None):
    return pl.pallas_call(
        kernel,
        in_specs=in_specs or [on_chip] * len(arguments),
        out_specs=out_specs,
        out_shape=outs,
        scratch_shapes=scratch,
        compiler_params=pltpu.CompilerParams(
            collective_id=number, has_side_effects=True, vmem_limit_bytes=vmem
        ),
    )(*arguments)


def everyone_kernel(dims, x_ref, o_ref, send_sem, recv_sem):
    wires = Wires(send_sem)
    H, X, C, Z = dims
    total = H * X * C * Z
    at = wires.at
    me = ((at["h"] * X + at["x"]) * C + at["c"]) * Z + at["z"]

    def coordinates(flat):
        return (flat // (X * C * Z), flat // (C * Z) % X, flat // Z % C, flat % Z)

    wires.greet([(None, coordinates((me + k) % total)) for k in range(1, total)])
    for k in range(1, total):
        wires.send(x_ref, o_ref.at[me], recv_sem.at[k], coordinates((me + k) % total))
    o_ref[me] = x_ref[...]
    for k in range(1, total):
        wires.arrived(o_ref.at[(me + total - k) % total], recv_sem.at[k])
    wires.drain()


def gather_everyone(x, dims, number):
    total = dims[0] * dims[1] * dims[2] * dims[3]
    if dims[0] > 2:
        return lax.all_gather(x, ALL, axis=0, tiled=False)
    return call(
        partial(everyone_kernel, dims),
        (x,),
        jax.ShapeDtypeStruct((total,) + x.shape, x.dtype),
        on_chip,
        [pltpu.SemaphoreType.DMA((total,)), pltpu.SemaphoreType.DMA((total,))],
        number,
    )


def team_kernel(dims, split_in, x_ref, o_ref, send_sem, recv_sem):
    H, X, C, Z = dims
    wires = Wires(send_sem)
    at = wires.at
    me = at["x"] * C + at["c"]
    others = [(1 - at["x"], at["c"]), (1 - at["x"], 1 - at["c"]), (at["x"], 1 - at["c"])]
    wires.greet([(None, wires.peer(x=x, c=c)) for x, c in others])
    for x, c in others:
        wires.send(x_ref.at[x * C + c], o_ref.at[me], recv_sem.at[me], wires.peer(x=x, c=c))
    o_ref[me] = x_ref[me]
    for x, c in others:
        wires.arrived(o_ref.at[x * C + c], recv_sem.at[x * C + c])
    wires.drain()


def team_swap(x, dims, number):
    if dims[0] > 2:
        return lax.all_to_all(x, GROUP, split_axis=0, concat_axis=0, tiled=True)
    return call(
        partial(team_kernel, dims, 0),
        (x,),
        jax.ShapeDtypeStruct(x.shape, x.dtype),
        on_chip,
        [pltpu.SemaphoreType.DMA((3,)), pltpu.SemaphoreType.DMA((4,))],
        number,
    )


def contrast(total, counts, queries):
    exact = partial(dot, precision=peak_affinity)
    pooled = total / counts
    scale = lax.rsqrt(jnp.sum(pooled * pooled, -1, keepdims=True) + 1e-06)
    embed = pooled * scale
    half = total.shape[0] // 2
    question, passage = embed[:half], embed[half:]
    scores = exact(question, passage, (1,), (1,)) / sharpness_divisor
    order = lax.broadcasted_iota(jnp.int32, scores.shape, 0)
    target = (order == lax.broadcasted_iota(jnp.int32, scores.shape, 1)).astype(f32)
    weight = (order < queries).astype(f32) / jnp.full(scores.shape, queries).astype(f32)
    peak = jnp.max(scores, -1, keepdims=True)
    shares = jnp.exp(scores - peak)
    mass = jnp.sum(shares, -1, keepdims=True)
    each = peak + jnp.log(mass) - jnp.sum(scores * target, -1, keepdims=True)
    loss = jnp.sum(weight[:, :1] * each)
    slope = (shares / mass - target) * weight
    grad = jnp.concatenate(
        [exact(slope, passage, (1,), (0,)), exact(slope, question, (0,), (0,))], 0
    ) / sharpness_divisor
    grad = scale * (grad - embed * jnp.sum(grad * embed, -1, keepdims=True))
    return loss, grad / counts


def normed(values):
    centred = values - jnp.mean(values, -1, keepdims=True)
    scale = lax.rsqrt(jnp.mean(centred * centred, -1, keepdims=True) + 1e-05)
    return centred * scale, scale


def normed_back(grad, unit, scale):
    shared = jnp.mean(grad * unit, -1, keepdims=True)
    return (grad - jnp.mean(grad, -1, keepdims=True) - unit * shared) * scale


def middle_kernel(
    dims,
    queries_ref,
    att_ref,
    x_ref,
    seg_ref,
    counts_ref,
    *refs,
):
    H, X, C, Z = dims
    ins, (loss_ref, swap_ref, first_ref), terms, weights = refs[:4], refs[4:7], refs[7:11], refs[11:15]
    (
        gate_ref,
        up_ref,
        act_ref,
        one_ref,
        low_ref,
        unit_ref,
        work_ref,
        grad_ref,
        stage_ref,
        misc_ref,
        sums_ref,
        team_ref,
        all_ref,
        gain_ref,
        load_sem,
        store_sem,
        misc_sem,
        send_sem,
        team_sem,
        recv_sem,
    ) = refs[15:]
    wires = Wires(send_sem)
    at = wires.at
    me = at["x"] * C + at["c"]
    row = at["h"] * Z + at["z"]
    rows = H * Z
    others = [(1 - at["x"], at["c"]), (1 - at["x"], 1 - at["c"]), (at["x"], 1 - at["c"])]
    far = [(row + k) % rows for k in range(1, rows)]
    loads = lambda n, k: pltpu.make_async_copy(ins[n].at[k], weights[n].at[k], load_sem.at[n, k])
    for n in (3, 0, 1, 2):
        for k in range(Z):
            loads(n, k).start()
    wires.greet(
        [(None, wires.peer(x=x, c=c)) for x, c in others]
        + [(None, wires.peer(h=r // Z, z=r % Z)) for r in far]
    )
    w_gate, w_up, w_down, w_misc = weights
    heads_width = att_ref.shape[2]
    own_len, width = x_ref.shape
    attn = x_ref[...].astype(f32)
    lanes = misc_ref.shape[2]
    for k in range(Z):
        loads(3, k).wait()
        if k == 0:
            gain_ref[...] = dot(selection(16, lanes, heads_width), w_misc[0], (1,), (1,))
        attn = attn + dot(att_ref[k], w_misc[k, :, :heads_width], (1,), (1,))
    unit_one, scale_one = normed(attn)
    unit_ref[...] = unit_one
    one_ref[...] = unit_one * gain_ref[0:1, :]
    low_ref[...] = one_ref[...].astype(bf16)
    work_ref[...] = one_ref[...]

    @pl.loop(0, Z)
    def _(k):
        for n in range(3):
            loads(n, k).wait()
        gate = dot(low_ref[...], w_gate[k], (1,), (0,))
        up = dot(low_ref[...], w_up[k], (1,), (0,))
        gate_ref[k] = gate
        up_ref[k] = up
        act_ref[k] = (gate / (1.0 + jnp.exp(-gate)) * up).astype(bf16)
        work_ref[...] += dot(act_ref[k], w_down[k], (1,), (1,))

    unit_two, scale_two = normed(work_ref[...])
    texts = sums_ref.shape[0]
    label = lax.broadcasted_iota(jnp.int32, (texts, own_len), 0)
    member = (label == seg_ref[...]).astype(f32)
    sums_ref[...] = dot(member, unit_two * gain_ref[1:2, :], (1,), (0,), peak_affinity)
    for x, c in others:
        wires.send(sums_ref, team_ref.at[me], team_sem.at[me], wires.peer(x=x, c=c))
    team_ref[me] = sums_ref[...]
    for x, c in others:
        wires.arrived(team_ref.at[x * C + c], team_sem.at[x * C + c])
    all_ref[row] = (team_ref[0] + team_ref[1]) + (team_ref[2] + team_ref[3])
    for r in far:
        wires.send(all_ref.at[row], all_ref.at[row], recv_sem.at[row], wires.peer(h=r // Z, z=r % Z))
    for r in far:
        wires.arrived(all_ref.at[r], recv_sem.at[r])
    wires.drain()
    loss, grad = contrast(all_ref[...].reshape(rows * texts, width), counts_ref[...], queries_ref[0])
    loss_ref[...] = jnp.full(loss_ref.shape, loss)
    all_ref[...] = grad.reshape(rows, texts, width)
    grad_two = dot(member, all_ref[row], (0,), (0,), peak_affinity)
    gain_two = jnp.sum(grad_two * unit_two, 0, keepdims=True)
    grad_ref[...] = normed_back(grad_two * gain_ref[1:2, :], unit_two, scale_two)
    low_back = grad_ref[...].astype(bf16)

    def store(n, k):
        return pltpu.make_async_copy(stage_ref.at[n, k % 2], terms[n].at[k], store_sem.at[n, k % 2])

    @pl.loop(0, Z)
    def _(k):
        @pl.when(k >= 2)
        def _():
            for n in range(3):
                store(n, k - 2).wait()

        grad_act = dot(low_back, w_down[k], (1,), (0,))
        stage_ref[2, k % 2] = dot(low_back, act_ref[k], (0,), (0,)).astype(bf16)
        gate, up = gate_ref[k], up_ref[k]
        share = 1.0 / (1.0 + jnp.exp(-gate))
        grad_gate = (grad_act * up * (share * (1.0 + gate * (1.0 - share)))).astype(bf16)
        grad_up = (grad_act * (gate * share)).astype(bf16)
        grad_ref[...] += dot(grad_gate, w_gate[k], (1,), (1,)) + dot(grad_up, w_up[k], (1,), (1,))
        stage_ref[0, k % 2] = dot(low_ref[...], grad_gate, (0,), (0,)).astype(bf16)
        stage_ref[1, k % 2] = dot(low_ref[...], grad_up, (0,), (0,)).astype(bf16)
        for n in range(3):
            store(n, k).start()

    gain_one = jnp.sum(grad_ref[...] * unit_ref[...], 0, keepdims=True)
    line = lax.broadcasted_iota(jnp.int32, (16, width), 0)
    lines = jnp.where(line == 0, gain_one, jnp.where(line == 1, gain_two, 0.0)).astype(bf16)
    gain_terms = dot(lines, selection(16, lanes, heads_width), (0,), (0,))
    first_ref[...] = normed_back(grad_ref[...] * gain_ref[0:1, :], unit_ref[...], scale_one)
    low_first = first_ref[...].astype(bf16)
    widen = selection(heads_width, lanes, 0)
    kept = lambda k: pltpu.make_async_copy(misc_ref.at[k], terms[3].at[k], misc_sem.at[k])
    for k in range(Z):
        swap_ref[k] = dot(low_first, w_misc[k, :, :heads_width], (1,), (0,)).astype(bf16)
        wide = dot(att_ref[k], widen, (1,), (0,)).astype(bf16)
        misc_ref[k] = (dot(low_first, wide, (0,), (0,)) + gain_terms).astype(bf16)
        kept(k).start()
    for k in range(Z):
        kept(k).wait()
    for k in (Z - 2, Z - 1):
        for n in range(3):
            store(n, k).wait()


def middle(queries, attended, x_own, seg_own, counts, weights, dims, number):
    H, X, C, Z = dims
    rows, team = H * Z, X * C
    own_len, width = x_own.shape
    part = weights[0].shape[2]
    vmem = lambda shape, dtype=bf16: pltpu.VMEM(shape, dtype)
    dma = lambda *shape: pltpu.SemaphoreType.DMA(shape)
    outs = call(
        partial(middle_kernel, dims),
        (queries, attended, x_own, seg_own[None, :], counts, *weights),
        [
            jax.ShapeDtypeStruct((8, 128), f32),
            jax.ShapeDtypeStruct(attended.shape, bf16),
            jax.ShapeDtypeStruct(x_own.shape, f32),
        ]
        + [jax.ShapeDtypeStruct(weight.shape, bf16) for weight in weights],
        [on_chip] * 3 + [anywhere] * 4,
        [vmem(weight.shape) for weight in weights]
        + [
            vmem((Z, own_len, part), f32),
            vmem((Z, own_len, part), f32),
            vmem((Z, own_len, part)),
            vmem((own_len, width), f32),
            vmem((own_len, width)),
            vmem((own_len, width), f32),
            vmem((own_len, width), f32),
            vmem((own_len, width), f32),
            vmem((3, 2, width, part)),
            vmem(weights[3].shape),
            vmem((SEGS, width), f32),
            vmem((team, SEGS, width), f32),
            vmem((rows, SEGS, width), f32),
            vmem((16, width), f32),
            dma(4, Z),
            dma(3, 2),
            dma(Z),
            dma(3 + rows),
            dma(team),
            dma(rows),
        ],
        number,
        in_specs=[pl.BlockSpec(memory_space=pltpu.SMEM)] + [on_chip] * 4 + [anywhere] * 4,
        vmem=62 * 2**20,
    )
    return outs[0][0, 0], outs[1], outs[2], list(outs[3:])


def contrast_all(hidden, seg_own, counts, queries, dims):
    H, X, C, Z = dims
    labels = jnp.arange(SEGS, dtype=jnp.int32)
    member = (seg_own[None, :] == labels[:, None]).astype(f32)
    sums = jnp.dot(member, hidden, precision=peak_affinity)
    total = lax.all_gather(lax.psum(sums, GROUP), ("h", "z"), axis=0, tiled=True)
    loss, grad = contrast(total, counts, queries[0])
    row = lax.axis_index("h") * Z + lax.axis_index("z")
    grad = lax.dynamic_slice_in_dim(grad, row * SEGS, SEGS, 0)
    return loss, dot(member, grad, (0,), (0,), peak_affinity)


def fetch_kernel(dims, x_ref, o_ref, send_sem, recv_sem):
    H, X, C, Z = dims
    wires = Wires(send_sem)
    at = wires.at
    h, x, c = at["h"], at["x"], at["c"]
    across, beside = wires.peer(x=1 - x), wires.peer(c=1 - c)
    away = [(h + k) % H for k in range(1, H)]
    wires.greet([(None, across), (None, beside)] + [(None, wires.peer(h=g)) for g in away])
    for g in away:
        wires.send(x_ref.at[g], o_ref.at[x, c, h], recv_sem.at[x, c, h], wires.peer(h=g))
    mine = (o_ref.at[x, c, h], recv_sem.at[x, c, h])
    wires.send(x_ref.at[h], *mine, across)
    wires.send(x_ref.at[h], *mine, beside)
    o_ref[x, c, h] = x_ref[h]
    for g in away:
        place = (o_ref.at[x, c, g], recv_sem.at[x, c, g])
        wires.arrived(*place)
        wires.send(place[0], *place, across)
        wires.send(place[0], *place, beside)
    for g in [h] + away:
        place = (o_ref.at[1 - x, c, g], recv_sem.at[1 - x, c, g])
        wires.arrived(*place)
        wires.send(place[0], *place, beside)
    for y in (x, 1 - x):
        for g in [h] + away:
            wires.arrived(o_ref.at[y, 1 - c, g], recv_sem.at[y, 1 - c, g])
    wires.drain()


def fetch_rows(rows, dims, number):
    H, X, C, Z = dims
    if H > 2:
        got = lax.all_to_all(rows, "h", split_axis=0, concat_axis=0, tiled=True)
        return lax.all_gather(got, GROUP, axis=0, tiled=False)
    return call(
        partial(fetch_kernel, dims),
        (rows,),
        jax.ShapeDtypeStruct((X, C) + rows.shape, rows.dtype),
        on_chip,
        [pltpu.SemaphoreType.DMA((4 * H,)), pltpu.SemaphoreType.DMA((X, C, H))],
        number,
    )


def along_line(wires, piece, recv_sem, extra=None):
    z, Z = wires.at["z"], wires.size_z
    right, left = wires.peer(z=z + 1), wires.peer(z=z - 1)
    for far in range(0, Z):
        for sign, onward, more in ((-1, right, z + 1 < Z), (1, left, z >= 1)):
            spot = z + sign * far
            there = None if far == 0 else (spot >= 0 if sign < 0 else spot < Z)
            for view, sem in zip(piece(spot), recv_sem(spot)):
                if far:
                    wires.arrived(view, sem, there)
                wires.send(view, view, sem, onward, both(there, more))
            if extra is not None and (far or sign < 0):
                extra(spot, there)


def settle_kernel(dims, x_ref, o_ref, beside_ref, across_ref, ready_ref, send_sem, beside_sem, across_sem, recv_sem):
    H, X, C, Z = dims
    wires = Wires(send_sem)
    wires.size_z = Z
    at = wires.at
    h, x, c, z = at["h"], at["x"], at["c"], at["z"]
    across, beside = wires.peer(x=1 - x), wires.peer(c=1 - c)
    away = [(h + k) % H for k in range(1, H)]
    wires.greet(
        [(None, across), (None, beside)]
        + [(None, wires.peer(h=g)) for g in away]
        + [(z + 1 < Z, wires.peer(z=z + 1)), (z >= 1, wires.peer(z=z - 1))]
    )
    for y in (1 - x, x):
        wires.send(x_ref.at[y, 1 - c], beside_ref.at[y], beside_sem.at[y], beside)
    wires.arrived(beside_ref.at[1 - x], beside_sem.at[1 - x])
    for g in away + [h]:
        total = x_ref[1 - x, c, g].astype(f32) + beside_ref[1 - x, g].astype(f32)
        ready_ref[g] = total.astype(ready_ref.dtype)
        wires.send(ready_ref.at[g], across_ref.at[g], across_sem.at[g], across)
    wires.arrived(beside_ref.at[x], beside_sem.at[x])
    for g in away + [h]:
        wires.arrived(across_ref.at[g], across_sem.at[g])
        total = x_ref[x, c, g].astype(f32) + beside_ref[x, g].astype(f32)
        total = (total + across_ref[g].astype(f32)).astype(o_ref.dtype)
        if g is h:
            o_ref[z, h] = total
        else:
            ready_ref[H + g] = total
            wires.send(ready_ref.at[H + g], o_ref.at[z, h], recv_sem.at[z, h], wires.peer(h=g))
    for g in away:
        wires.arrived(o_ref.at[z, g], recv_sem.at[z, g])
    along_line(wires, lambda s: [o_ref.at[s]], lambda s: [recv_sem.at[s, H]])
    wires.drain()


def settle_rows(terms, dims, number):
    H, X, C, Z = dims
    block = terms.shape[3:]
    if H > 2:
        terms = terms.reshape((X * C,) + (H,) + block)
        terms = lax.psum_scatter(terms, GROUP, scatter_dimension=0, tiled=True)[0]
        terms = lax.all_to_all(terms, "h", split_axis=0, concat_axis=0, tiled=True)
        return lax.all_gather(terms, "z", axis=0, tiled=False)
    return call(
        partial(settle_kernel, dims),
        (terms,),
        jax.ShapeDtypeStruct((Z, H) + block, terms.dtype),
        on_chip,
        [
            pltpu.VMEM((X, H) + block, terms.dtype),
            pltpu.VMEM((H,) + block, terms.dtype),
            pltpu.VMEM((2 * H,) + block, terms.dtype),
            pltpu.SemaphoreType.DMA((2 + 2 * H + 2 * Z,)),
            pltpu.SemaphoreType.DMA((X,)),
            pltpu.SemaphoreType.DMA((H,)),
            pltpu.SemaphoreType.DMA((Z, H + 1)),
        ],
        number,
    )


def gather_weights(pieces, dims):
    H, X, C, Z = dims
    rows = pieces[0].shape[0]
    outs = [lax.all_gather(piece, ALL, axis=0, tiled=False) for piece in pieces]
    outs = [whole.reshape(H * X * C, Z, rows, -1).transpose(1, 0, 2, 3) for whole in outs]
    return [whole.reshape(Z, H * X * C * rows, -1) for whole in outs]


def reduce_weights(pieces, dims):
    H, X, C, Z = dims
    batch = H * X * C
    rows = pieces[0].shape[1] // batch
    sums = []
    for piece in pieces:
        piece = piece.reshape(Z, batch, rows, -1).transpose(1, 0, 2, 3)
        piece = piece.reshape(batch * Z, rows, -1)
        sums.append(lax.psum_scatter(piece, ALL, scatter_dimension=0, tiled=True)[0].astype(f32))
    return sums


class Spread:
    def __init__(self, wires, dims, kinds, stages, outs, send_sem, recv_sem):
        self.wires, self.kinds, self.stages, self.outs = wires, kinds, stages, outs
        self.send_sem, self.recv_sem = send_sem, recv_sem
        self.Z = dims[3]
        self.spots = 2 * self.Z - 1

    def where(self, i):
        z = self.wires.at["z"]
        if isinstance(i, int) and i == 0:
            return z, 0, None
        sign = 1 - 2 * (i % 2)
        s = z + sign * ((i + 1) // 2)
        return s, sign, (s >= 0) & (s < self.Z)

    def place(self, a, s, h, x, c):
        return self.outs[a].at[s, h, x, c], self.recv_sem.at[a, s, (h * 2 + x) * 2 + c]

    def moves(self, phase, i):
        at, peer = self.wires.at, self.wires.peer
        h, x, c, z = at["h"], at["x"], at["c"], at["z"]
        s, sign, there = self.where(i)
        beside = peer(c=1 - c)
        moves = []

        def add(a, block, kind, target, when=there):
            view, sem = self.place(a, s, *block)
            fresh = isinstance(i, int) and i == 0 and phase < 2
            source = self.stages[a] if fresh else view
            moves.append((when, source, view, sem, self.send_sem.at[a, kind, i], target))

        for a, kind in enumerate(self.kinds):
            hops = [peer(h=1 - h), peer(x=1 - x)]
            if phase == 0:
                if isinstance(i, int) and i == 0:
                    add(a, (h, x, c), 0, peer(z=z + 1), z + 1 < self.Z)
                    add(a, (h, x, c), 1, peer(z=z - 1), z >= 1)
                else:
                    onward = z - sign
                    add(a, (h, x, c), 0, peer(z=onward), there & (onward >= 0) & (onward < self.Z))
            if phase == 1:
                add(a, (h, x, c), 2, hops[kind])
                add(a, (h, x, c), 3, hops[1 - kind])
                add(a, (h, x, c), 4, beside)
            if phase == 2:
                block = (1 - h, x, c) if kind == 0 else (h, 1 - x, c)
                add(a, block, 5, hops[1 - kind])
                add(a, block, 6, beside)
            if phase == 3:
                add(a, (h, 1 - x, c) if kind == 0 else (1 - h, x, c), 7, beside)
                add(a, (1 - h, 1 - x, c), 8, beside)
        return moves

    def copy(self, move):
        return pltpu.make_async_remote_copy(
            src_ref=move[1],
            dst_ref=move[2],
            send_sem=move[4],
            recv_sem=move[3],
            device_id=move[5],
            device_id_type=MESH,
        )

    def wait(self, phase, i):
        at = self.wires.at
        h, x, c = at["h"], at["x"], at["c"]
        s, _, there = self.where(i)
        for a, kind in enumerate(self.kinds):
            if phase == 0:
                blocks = [] if isinstance(i, int) and i == 0 else [(h, x, c)]
            elif phase == 1:
                blocks = []
            elif phase == 2:
                blocks = [(1 - h, x, c) if kind == 0 else (h, 1 - x, c)]
            elif phase == 3:
                blocks = [(h, 1 - x, c) if kind == 0 else (1 - h, x, c), (1 - h, 1 - x, c)]
            else:
                blocks = [(g, y, 1 - c) for g in range(2) for y in range(2)]
            for block in blocks:
                self.wires.arrived(*self.place(a, s, *block), there)

    def step(self, phase, i):
        self.wait(phase, i)
        if phase < 4:
            for move in self.moves(phase, i):
                guarded(move[0], lambda move=move: self.copy(move).start())

    def run(self, phases, first, last):
        if first == 0:
            for phase in phases:
                self.step(phase, 0)
        low = max(first, 1)
        if low < last:

            @pl.loop(low, last)
            def _(i):
                for phase in phases:
                    self.step(phase, i)

    def settle(self):
        def sent(i):
            for phase in (0, 1, 2, 3):
                for move in self.moves(phase, i):
                    guarded(move[0], lambda move=move: self.copy(move).wait_send())

        sent(0)

        @pl.loop(1, self.spots)
        def _(i):
            sent(i)


class Late:
    def __init__(self, wires, dims, stage, out, send_sem, recv_sem):
        self.wires, self.stage, self.out = wires, stage, out
        self.send_sem, self.recv_sem, self.Z = send_sem, recv_sem, dims[3]
        self.spots = 2 * self.Z - 1

    def where(self, i):
        z = self.wires.at["z"]
        if isinstance(i, int) and i == 0:
            return z, 0, None
        sign = 1 - 2 * (i % 2)
        s = z + sign * ((i + 1) // 2)
        return s, sign, (s >= 0) & (s < self.Z)

    def line(self, s, c):
        return self.out.at[s, :, :, c]

    def moves(self, i):
        at, peer = self.wires.at, self.wires.peer
        h, x, c, z = at["h"], at["x"], at["c"], at["z"]
        sent, got = self.send_sem, self.recv_sem
        if isinstance(i, str) and i == "across":
            view = self.out.at[z, h, x, c]
            return [(None, self.stage, view, sent.at[0, 0], got.at[0, 0], peer(x=1 - x))]
        if isinstance(i, str) and i == "away":
            view = self.out.at[z, h, :, c]
            return [(None, view, view, sent.at[0, 1], got.at[0, 1], peer(h=1 - h))]
        s, sign, there = self.where(i)
        view = self.line(s, c)
        if isinstance(i, int) and i == 0:
            moves = [
                (z + 1 < self.Z, view, view, sent.at[1, 0], got.at[1, s], peer(z=z + 1)),
                (z >= 1, view, view, sent.at[0, 2], got.at[1, s], peer(z=z - 1)),
            ]
        else:
            onward = z - sign
            when = there & (onward >= 0) & (onward < self.Z)
            moves = [(when, view, view, sent.at[1, i], got.at[1, s], peer(z=onward))]
        return moves + [(there, view, view, sent.at[2, i], got.at[2, s], peer(c=1 - c))]

    def copy(self, move):
        return pltpu.make_async_remote_copy(
            src_ref=move[1],
            dst_ref=move[2],
            send_sem=move[3],
            recv_sem=move[4],
            device_id=move[5],
            device_id_type=MESH,
        )

    def step(self, i):
        at = self.wires.at
        h, x, c, z = at["h"], at["x"], at["c"], at["z"]
        if isinstance(i, str) and i == "away":
            self.wires.arrived(self.out.at[z, h, 1 - x, c], self.recv_sem.at[0, 0])
        elif isinstance(i, int) and i == 0:
            self.wires.arrived(self.out.at[z, 1 - h, :, c], self.recv_sem.at[0, 1])
        elif not isinstance(i, str):
            s, _, there = self.where(i)
            self.wires.arrived(self.line(s, c), self.recv_sem.at[1, s], there)
        for move in self.moves(i):
            guarded(move[0], lambda move=move: self.copy(move).start())

    def settle(self):
        def sent(i):
            for move in self.moves(i):
                guarded(move[0], lambda move=move: self.copy(move).wait_send())

        for i in ("across", "away", 0):
            sent(i)

        @pl.loop(1, self.spots)
        def _(i):
            sent(i)

        @pl.loop(0, self.Z)
        def _(s):
            self.wires.arrived(self.line(s, 1 - self.wires.at["c"]), self.recv_sem.at[2, s])


def selection(rows, columns, shift):
    row = lax.broadcasted_iota(jnp.int32, (rows, columns), 0)
    column = lax.broadcasted_iota(jnp.int32, (rows, columns), 1)
    return (column == row + shift).astype(bf16)


def turned(values, cosine, sine):
    half = HEAD_DIM // 2
    lanes = values.shape[1]
    lane = lax.broadcasted_iota(jnp.int32, values.shape, 1) % HEAD_DIM
    after = pltpu.roll(values, lanes - half, 1)
    before = pltpu.roll(values, half, 1)
    wide = lambda t: jnp.concatenate([t] * (lanes // t.shape[1]), 1)
    return values * wide(cosine) + jnp.where(lane < half, -after, before) * wide(sine)


def attend_block(query, keys, values, apart, heads):
    lane = lax.broadcasted_iota(jnp.int32, query.shape, 1) // HEAD_DIM
    scaled = query * jnp.asarray(HEAD_DIM ** (-0.5), bf16)
    result = jnp.zeros(query.shape, f32)
    for head in range(heads):
        own = jnp.where(lane == head, scaled, jnp.zeros_like(query))
        scores = dot(own, keys, (1,), (1,)) + apart
        weights = jnp.exp(scores - jnp.max(scores, 1, keepdims=True))
        probs = (weights * (1.0 / jnp.sum(weights, 1, keepdims=True))).astype(bf16)
        result = jnp.where(lane == head, dot(probs, values, (1,), (0,)), result)
    return result.astype(bf16)


def front_kernel(
    dims,
    rows_ref,
    slot_ref,
    more_ref,
    place_ref,
    freq_ref,
    segq_ref,
    segk_ref,
    *refs,
):
    ins, outs, stages = refs[:5], refs[5:10], refs[18:23]
    x_ref, q_ref, k_ref, v_ref, swap_ref, own_ref, cos_ref, sin_ref = refs[10:18]
    (
        got_ref,
        heads_ref,
        pick_ref,
        send_ref,
        load_sem,
        store_sem,
        main_send,
        main_recv,
        small_send,
        small_recv,
        late_send,
        late_recv,
        row_send,
        row_recv,
        heads_sem,
        swap_send,
        swap_recv,
    ) = refs[23:]
    H, X, C, Z = dims
    wires = Wires(row_send)
    at = wires.at
    h, x, c, z = at["h"], at["x"], at["c"], at["z"]
    across, beside, away = wires.peer(x=1 - x), wires.peer(c=1 - c), wires.peer(h=1 - h)
    team = x * C + c
    wires.greet(
        [(None, across), (None, beside), (None, away), (None, wires.peer(x=1 - x, c=1 - c))]
        + [(z + 1 < Z, wires.peer(z=z + 1)), (z >= 1, wires.peer(z=z - 1))]
    )
    loads = [pltpu.make_async_copy(ins[i], stages[i], load_sem.at[i]) for i in range(5)]
    stores = [
        pltpu.make_async_copy(stages[i], outs[i].at[z, h, x, c], store_sem.at[i]) for i in range(5)
    ]
    for load in loads:
        load.start()

    def owner_rows(y, d, g):
        return got_ref.at[y, d, g], row_recv.at[y, d, g]

    wires.send(rows_ref.at[1 - h], *owner_rows(x, c, h), away)
    wires.send(rows_ref.at[h], *owner_rows(x, c, h), across)
    wires.send(rows_ref.at[h], *owner_rows(x, c, h), beside)
    got_ref[x, c, h] = rows_ref[h]
    for load, store in zip(loads, stores):
        load.wait()
        store.start()
    length, width = x_ref.shape
    block = min(256, length)
    blocks = length // block

    def tables(first, last):
        @pl.loop(first, last)
        def _(i):
            here = pl.ds(pl.multiple_of(i * block, block), block)
            angles = place_ref[here, :] * freq_ref[...]
            cos_ref[here, :] = jnp.cos(angles)
            sin_ref[here, :] = jnp.sin(angles)

    small = Spread(wires, dims, [1], stages[:1], outs[:1], small_send, small_recv)
    main = Spread(wires, dims, [0, 0, 1], stages[1:4], outs[1:4], main_send, main_recv)
    late = Late(wires, dims, stages[4], outs[4], late_send, late_recv)
    spots = main.spots
    small.run((0, 1), 0, 1)
    late.step("across")
    main.run((0,), 0, 1)
    tables(0, blocks // 3)
    small.run((0, 1), 1, 3)
    place = owner_rows(x, c, 1 - h)
    wires.arrived(*place)
    wires.send(place[0], *place, across)
    wires.send(place[0], *place, beside)
    small.run((2,), 0, 1)
    main.run((0,), 1, 3)
    stores[4].wait()
    late.step("away")
    tables(blocks // 3, 2 * blocks // 3)
    small.run((0, 1), 3, 5)
    small.run((2,), 1, 3)
    for g in (h, 1 - h):
        place = owner_rows(1 - x, c, g)
        wires.arrived(*place)
        wires.send(place[0], *place, beside)
    small.run((3,), 0, 1)
    small.run((0, 1), 5, spots)
    main.run((0,), 3, 5)
    small.run((2,), 3, 5)
    small.run((3,), 1, 3)
    late.step(0)
    tables(2 * blocks // 3, blocks)
    small.run((2,), 5, spots)
    main.run((1,), 0, 3)
    main.run((0,), 5, spots)
    main.run((1,), 3, spots)
    small.run((3,), 3, spots)
    stores[0].wait()
    small.run((4,), 0, spots)
    heads = pltpu.make_async_copy(outs[0].at[team], heads_ref, heads_sem)
    heads.start()
    for y in (x, 1 - x):
        for g in (h, 1 - h):
            wires.arrived(*owner_rows(y, 1 - c, g))
    heads.wait()

    heads_width = send_ref.shape[1]
    lanes = q_ref.shape[1]
    merged = heads_ref[...].reshape(width, heads_ref.shape[-1])
    for part in range(3):
        choose = selection(lanes, 3 * heads_width, part * heads_width)
        row = lax.broadcasted_iota(jnp.int32, choose.shape, 0)
        choose = jnp.where(row < heads_width, choose, jnp.zeros_like(choose))
        pick_ref[part] = dot(merged, choose, (1,), (1,)).astype(bf16)
    slots = got_ref.shape[0] * got_ref.shape[1] * got_ref.shape[2] * got_ref.shape[3]

    @pl.loop(0, blocks)
    def _(i):
        here = pl.ds(pl.multiple_of(i * block, block), block)
        slot = lax.broadcasted_iota(jnp.int32, (block, slots), 1)
        chosen = (slot_ref[here, :] == slot).astype(bf16)
        full = dot(chosen, got_ref[...].reshape(slots, width), (1,), (0,))
        low = (full + more_ref[here, :].astype(f32)).astype(bf16)
        x_ref[here, :] = low
        cosine, sine = cos_ref[here, :], sin_ref[here, :]
        q_ref[here, :] = turned(dot(low, pick_ref[0], (1,), (0,)), cosine, sine).astype(bf16)
        k_ref[here, :] = turned(dot(low, pick_ref[1], (1,), (0,)), cosine, sine).astype(bf16)
        v_ref[here, :] = dot(low, pick_ref[2], (1,), (0,)).astype(bf16)

        @pl.when(i == 2)
        def _():
            late.step(1)
            late.step(2)

    main.run((2,), 0, 3)
    own_len = length // (X * C)

    @pl.loop(0, blocks)
    def _(i):
        here = pl.ds(pl.multiple_of(i * block, block), block)
        apart = jnp.where(segq_ref[here, :] == segk_ref[...], 0.0, negative)
        heads = heads_width // HEAD_DIM
        result = attend_block(q_ref[here, :], k_ref[...], v_ref[...], apart, heads)
        send_ref[here, :] = result[:, :heads_width]

        @pl.when((i == 0) | (i == 2))
        def _():
            main.step(2, i + 3)
            main.step(2, i + 4)

        @pl.when(i == 1)
        def _():
            late.step(3)
            late.step(4)

        pl.when(i == 3)(lambda: main.step(3, 0))
        pl.when(i == 4)(lambda: main.step(3, 1))

    others = [(1 - x, c), (1 - x, 1 - c), (x, 1 - c)]

    def part_of(y, d):
        return send_ref.at[pl.ds(pl.multiple_of((y * C + d) * own_len, 128), own_len), :]

    swaps = [
        pltpu.make_async_remote_copy(
            src_ref=part_of(y, d),
            dst_ref=swap_ref.at[team],
            send_sem=swap_send.at[k],
            recv_sem=swap_recv.at[team],
            device_id=wires.peer(x=y, c=d),
            device_id_type=MESH,
        )
        for k, (y, d) in enumerate(others)
    ]
    for swap in swaps:
        swap.start()
    mine = pl.ds(pl.multiple_of(team * own_len, 128), own_len)
    swap_ref[team] = send_ref[mine, :]
    own_ref[...] = x_ref[mine, :]
    late.step(5)
    late.step(6)
    main.run((3,), 2, spots)
    main.run((4,), 0, spots)
    for y, d in others:
        wires.arrived(swap_ref.at[y * C + d], swap_recv.at[y * C + d])
    for swap in swaps:
        swap.wait_send()
    for store in stores[1:4]:
        store.wait()
    late.settle()
    main.settle()
    small.settle()
    wires.drain()


def front(rows, slot, more, places, freqs, segments, pieces, heads_width, dims, number):
    H, X, C, Z = dims
    length, width = more.shape
    team = X * C
    spots = 2 * Z - 1
    batch = H * team
    rows_in = pieces[0].shape[0]
    lanes = -(-heads_width // 128) * 128
    vmem = lambda shape, dtype=bf16: pltpu.VMEM(shape, dtype)
    dma = lambda *shape: pltpu.SemaphoreType.DMA(shape)
    outs = call(
        partial(front_kernel, dims),
        (rows, slot[:, None], more, places[:, None], freqs, segments[:, None], segments[None, :], *pieces),
        [jax.ShapeDtypeStruct((Z, H, X, C) + piece.shape, bf16) for piece in pieces]
        + [jax.ShapeDtypeStruct((length, width), bf16)]
        + [jax.ShapeDtypeStruct((length, lanes), bf16)] * 3
        + [jax.ShapeDtypeStruct((team, length // team, heads_width), bf16)]
        + [jax.ShapeDtypeStruct((length // team, width), bf16)]
        + [jax.ShapeDtypeStruct((length, 128), f32)] * 2,
        [anywhere] * 5 + [on_chip] * 8,
        [vmem(piece.shape) for piece in pieces]
        + [
            vmem((X, C) + rows.shape),
            vmem((H, X, C) + pieces[0].shape),
            vmem((3, width, lanes)),
            vmem((length, heads_width)),
            dma(5),
            dma(5),
            dma(3, 9, spots),
            dma(3, Z, batch),
            dma(1, 9, spots),
            dma(1, Z, batch),
            dma(3, spots),
            dma(3, Z),
            dma(7),
            dma(X, C, H),
            pltpu.SemaphoreType.DMA,
            dma(3),
            dma(team),
        ],
        number,
        in_specs=[on_chip] * 7 + [anywhere] * 5,
        vmem=60 * 2**20,
    )
    weights = [whole.reshape(Z, batch * rows_in, -1) for whole in outs[:5]]
    return weights, outs[5:]


def sum_rows(goal, sources):
    rows = goal.shape[0]
    step = 16 if rows % 16 == 0 else rows

    @pl.loop(0, rows // step)
    def _(i):
        part = pl.ds(pl.multiple_of(i * step, step), step)
        if len(sources) == 2 and goal.dtype == bf16:
            goal[part, :] = sources[0][part, :] + sources[1][part, :]
            return
        value = sources[0][part, :].astype(f32)
        for source in sources[1:]:
            value += source[part, :].astype(f32)
        goal[part, :] = value.astype(goal.dtype)


class Line:
    def __init__(self, wires, Z, buffers, send_sem, recv_sem):
        self.wires, self.Z, self.buffers = wires, Z, buffers
        self.send_sem, self.recv_sem = send_sem, recv_sem

    def onward(self, a, s, source):
        z = self.wires.at["z"]
        upward = z < s
        goal = jnp.where(upward, z + 1, z - 1)
        index = jnp.where((s < goal) | upward, s, self.Z)
        return pltpu.make_async_remote_copy(
            src_ref=source,
            dst_ref=self.buffers[a].at[index],
            send_sem=self.send_sem.at[a, s],
            recv_sem=self.recv_sem.at[a, index],
            device_id=self.wires.peer(z=goal),
            device_id_type=MESH,
        )

    def step(self, a, s, sources, running, final):
        z, Z = self.wires.at["z"], self.Z

        def took(index):
            view = self.buffers[a].at[index]
            self.wires.arrived(view, self.recv_sem.at[a, index])
            return view

        passing = z != s
        edge = ((z < s) & (z == 0)) | ((z > s) & (z == Z - 1))

        @pl.when(passing & edge)
        def _():
            sum_rows(running, sources)

        @pl.when(passing & ~edge)
        def _():
            sum_rows(running, sources + [took(s)])

        @pl.when(passing)
        def _():
            self.onward(a, s, running).start()

        @pl.when((z == s) & (z == 0))
        def _():
            sum_rows(final, sources + [took(Z)])

        @pl.when((z == s) & (z == Z - 1))
        def _():
            sum_rows(final, sources + [took(s)])

        @pl.when((z == s) & (z > 0) & (z < Z - 1))
        def _():
            sum_rows(final, sources + [took(s), took(Z)])

    def settle(self, a, s, running):
        @pl.when(self.wires.at["z"] != s)
        def _():
            self.onward(a, s, running).wait_send()


class Gathering:
    def __init__(self, wires, dims, kinds, ins, outs, own, near, first, second, lines, sems):
        self.wires, self.kinds, self.Z = wires, kinds, dims[3]
        self.ins, self.outs, self.own, self.near = ins, outs, own, near
        self.first, self.second = first, second
        self.load_sem, self.near_sem, self.first_sem, self.second_sem = sems[:4]
        self.near_send, self.first_send, self.second_send = sems[4:7]
        self.line = Line(wires, dims[3], lines, sems[7], sems[8])
        at = wires.at
        self.x, self.h, self.c, self.z = at["x"], at["h"], at["c"], at["z"]
        self.across, self.beside = wires.peer(x=1 - self.x), wires.peer(c=1 - self.c)
        self.away = wires.peer(h=1 - self.h)

    def turn(self, i):
        Z = self.Z
        low = self.z < Z // 2
        side = jnp.where(low, self.z, Z - 1 - self.z)
        s = jnp.where(i < Z - 1 - side, Z - 1 - i, jnp.where(i < Z - 1, i - (Z - 1 - side), side))
        return jnp.where(low, s, Z - 1 - s)

    def remote(self, source, goal, send_sem, recv_sem, target):
        return pltpu.make_async_remote_copy(
            src_ref=source,
            dst_ref=goal,
            send_sem=send_sem,
            recv_sem=recv_sem,
            device_id=target,
            device_id_type=MESH,
        )

    def load(self, a, s):
        return pltpu.make_async_copy(
            self.ins[a].at[s, :, :, self.c], self.own[a].at[s], self.load_sem.at[a, s]
        )

    def near_copy(self, a, s):
        return self.remote(
            self.ins[a].at[s, :, :, 1 - self.c],
            self.near[a].at[s],
            self.near_send.at[a, s],
            self.near_sem.at[a, s],
            self.beside,
        )

    def axes(self, a):
        return (self.x, self.h) if self.kinds[a] == 0 else (self.h, self.x)

    def spot(self, a, s, f, g):
        return (s, g, f) if self.kinds[a] == 0 else (s, f, g)

    def first_copy(self, a, s, g):
        f, _ = self.axes(a)
        return self.remote(
            self.own[a].at[self.spot(a, s, 1 - f, g)],
            self.first[a].at[s, g],
            self.first_send.at[a, s, g],
            self.first_sem.at[a, s, g],
            self.across if self.kinds[a] == 0 else self.away,
        )

    def second_copy(self, a, s):
        f, g = self.axes(a)
        return self.remote(
            self.own[a].at[self.spot(a, s, f, 1 - g)],
            self.second[a].at[s],
            self.second_send.at[a, s],
            self.second_sem.at[a, s],
            self.away if self.kinds[a] == 0 else self.across,
        )

    def begin(self):
        @pl.loop(0, self.Z)
        def _(i):
            s = self.turn(i)
            for a in range(len(self.kinds)):
                self.near_copy(a, s).start()
                self.load(a, s).start()

    def one(self, i):
        s = self.turn(i)
        for a in range(len(self.kinds)):
            self.wires.arrived(self.near[a].at[s], self.near_sem.at[a, s])
            self.load(a, s).wait()
            f, g = self.axes(a)
            for k in (1 - g, g):
                place = self.spot(a, s, 1 - f, k)
                sum_rows(self.own[a].at[place], [self.own[a].at[place], self.near[a].at[place]])
                self.first_copy(a, s, k).start()

    def two(self, i):
        s = self.turn(i)
        for a in range(len(self.kinds)):
            f, g = self.axes(a)
            for k in (1 - g, g):
                self.wires.arrived(self.first[a].at[s, k], self.first_sem.at[a, s, k])
            place = self.spot(a, s, f, 1 - g)
            sum_rows(
                self.own[a].at[place],
                [self.own[a].at[place], self.near[a].at[place], self.first[a].at[s, 1 - g]],
            )
            self.second_copy(a, s).start()

    def three(self, i):
        s = self.turn(i)
        for a in range(len(self.kinds)):
            f, g = self.axes(a)
            self.wires.arrived(self.second[a].at[s], self.second_sem.at[a, s])
            place = self.spot(a, s, f, g)
            own = self.own[a].at[place]
            sources = [own, self.near[a].at[place], self.first[a].at[s, g], self.second[a].at[s]]
            self.line.step(a, s, sources, own, self.outs[a])

    def settle(self):
        @pl.loop(0, self.Z)
        def _(s):
            for a in range(len(self.kinds)):
                self.near_copy(a, s).wait_send()
                for k in range(2):
                    self.first_copy(a, s, k).wait_send()
                self.second_copy(a, s).wait_send()
                f, g = self.axes(a)
                self.line.settle(a, s, self.own[a].at[self.spot(a, s, f, g)])


def attend_back_block(query, grad, keys, values, apart, heads, dk_ref, dv_ref):
    factor = HEAD_DIM ** (-0.5)
    lane = lax.broadcasted_iota(jnp.int32, query.shape, 1) // HEAD_DIM
    scaled = query * jnp.asarray(factor, bf16)
    result = jnp.zeros(query.shape, f32)
    for head in range(heads):
        own = jnp.where(lane == head, scaled, jnp.zeros_like(query))
        own_grad = jnp.where(lane == head, grad, jnp.zeros_like(grad))
        scores = dot(keys, own, (1,), (1,)) + apart
        weights = jnp.exp(scores - jnp.max(scores, 0, keepdims=True))
        probs = weights * (1.0 / jnp.sum(weights, 0, keepdims=True))
        grad_probs = dot(values, own_grad, (1,), (1,))
        inner = jnp.sum(probs * grad_probs, 0, keepdims=True)
        grad_scores = (probs * (grad_probs - inner)).astype(bf16)
        dk_ref[...] += dot(grad_scores, own, (1,), (0,))
        dv_ref[...] += dot(probs.astype(bf16), own_grad, (1,), (0,))
        result = jnp.where(lane == head, dot(grad_scores, keys, (0,), (0,)) * factor, result)
    return result


def back_kernel(
    dims,
    heads,
    swap_ref,
    q_ref,
    k_ref,
    v_ref,
    x_ref,
    cos_ref,
    sin_ref,
    segq_ref,
    segk_ref,
    slot_ref,
    first_ref,
    listk_ref,
    heads_ref,
    in_gate,
    in_up,
    in_down,
    in_misc,
    out_gate,
    out_up,
    out_down,
    out_misc,
    out_qkv,
    spread_ref,
    zero_ref,
    total_ref,
    *scratch,
):
    H, X, C, Z = dims
    scratch = list(scratch)
    take = lambda n: [scratch.pop(0) for _ in range(n)]
    own, near, first, second, lines = (take(4) for _ in range(5))
    (got_ref, grad_ref, dk_ref, dv_ref, low_ref, matrix_ref, heads_v) = take(7)
    (qsrc, qnear, qx, qh, qtot, qline) = take(6)
    (slots_ref, beside_ref, across_ref, ready_ref) = take(4)
    sems = take(9)
    (swap_send, swap_recv, heads_sem, qsend, qrecv, qline_send, qline_recv) = take(7)
    (row_send, beside_sem, across_sem, row_recv, norm_ref, norm_send, norm_recv) = take(7)
    wires = Wires(row_send)
    wires.size_z = Z
    at = wires.at
    h, x, c, z = at["h"], at["x"], at["c"], at["z"]
    across, beside, away = wires.peer(x=1 - x), wires.peer(c=1 - c), wires.peer(h=1 - h)
    team = x * C + c
    devices = H * X * C * Z
    me = (team + h * X * C) * Z + z

    def coordinates(flat):
        return (flat // (X * C * Z), flat // (C * Z) % X, flat // Z % C, flat % Z)

    wires.greet([(None, coordinates((me + k) % devices)) for k in range(1, devices)])
    others = [(1 - x, c), (1 - x, 1 - c), (x, 1 - c)]
    swaps = [
        pltpu.make_async_remote_copy(
            src_ref=swap_ref.at[y * C + d],
            dst_ref=got_ref.at[team],
            send_sem=swap_send.at[k],
            recv_sem=swap_recv.at[team],
            device_id=wires.peer(x=y, c=d),
            device_id_type=MESH,
        )
        for k, (y, d) in enumerate(others)
    ]
    for swap in swaps:
        swap.start()
    fetch = pltpu.make_async_copy(heads_ref.at[team], heads_v, heads_sem)
    fetch.start()
    job = Gathering(
        wires,
        dims,
        [1, 1, 0, 0],
        [in_gate, in_up, in_down, in_misc],
        [out_gate, out_up, out_down, out_misc],
        own,
        near,
        first,
        second,
        lines,
        sems,
    )
    job.begin()
    got_ref[team] = swap_ref[team]
    dk_ref[...] = jnp.zeros_like(dk_ref)
    dv_ref[...] = jnp.zeros_like(dv_ref)
    matrix_ref[...] = jnp.zeros_like(matrix_ref)
    length, lanes = q_ref.shape
    heads_width = got_ref.shape[2]
    own_len = got_ref.shape[1]
    width = x_ref.shape[1]
    edge = (z == 0) | (z == Z - 1)
    job.one(0)
    widen = selection(heads_width, lanes, 0)
    for y, d in others:
        wires.arrived(got_ref.at[y * C + d], swap_recv.at[y * C + d])
    job.one(1)

    @pl.loop(0, X * C)
    def _(k):
        part = pl.ds(pl.multiple_of(k * own_len, 128), own_len)
        grad_ref[part, :] = dot(got_ref[k], widen, (1,), (0,)).astype(bf16)

    block = min(256, length)
    blocks = length // block

    def narrow(values, part):
        choose = selection(lanes, 3 * heads_width, part * heads_width)
        row = lax.broadcasted_iota(jnp.int32, choose.shape, 0)
        choose = jnp.where(row < heads_width, choose, jnp.zeros_like(choose))
        return dot(values.astype(bf16), choose, (1,), (0,))

    @pl.loop(0, blocks)
    def _(i):
        here = pl.ds(pl.multiple_of(i * block, block), block)
        apart = jnp.where(segk_ref[...] == segq_ref[:, here], 0.0, negative)
        grad_query = attend_back_block(
            q_ref[here, :], grad_ref[here, :], k_ref[...], v_ref[...], apart, heads, dk_ref, dv_ref
        )
        low_ref[here, :] = narrow(turned(grad_query, cos_ref[here, :], -sin_ref[here, :]), 0).astype(bf16)

        pl.when((i == 1) | (i == 3))(lambda: job.two(i // 2))
        pl.when((i == 2) | (i == 5))(lambda: job.one(2 + i // 5))
        pl.when((i == 4) & edge)(lambda: job.three(0))

    fetch.wait()

    @pl.loop(0, X * C)
    def _(k):
        part = pl.ds(pl.multiple_of(k * own_len, 128), own_len)
        grad_keys = turned(dk_ref[part, :], cos_ref[part, :], -sin_ref[part, :])
        low = low_ref[part, :].astype(f32) + narrow(grad_keys, 1) + narrow(dv_ref[part, :], 2)
        low = low.astype(bf16)
        zero = dot(low, heads_v[...], (1,), (1,))
        zero_ref[part, :] = (zero + (k == team).astype(f32) * first_ref[...]).astype(bf16)
        matrix_ref[...] += dot(x_ref[part, :], low, (0,), (0,))
        pl.when(k == 1)(lambda: job.two(2))
        pl.when(k == 2)(lambda: job.three(edge.astype(jnp.int32)))

    capacity = slots_ref.shape[3]

    def fill(y, d):
        for g in range(H):
            slot = lax.broadcasted_iota(jnp.int32, (capacity, length), 0)
            slot += ((y * C + d) * H + g) * capacity
            chosen = (slot_ref[...] == slot).astype(bf16)
            slots_ref[y, d, g] = dot(chosen, zero_ref[...], (1,), (0,)).astype(bf16)

    def row_copy(y):
        wires.send(slots_ref.at[y, 1 - c], beside_ref.at[y], beside_sem.at[y], beside)

    qsrc[...] = matrix_ref[...].astype(bf16).reshape(qsrc.shape)

    def qcopy(source, goal, k, target):
        return pltpu.make_async_remote_copy(
            src_ref=source,
            dst_ref=goal,
            send_sem=qsend.at[k],
            recv_sem=qrecv.at[k],
            device_id=target,
            device_id_type=MESH,
        )

    qcopies = [
        qcopy(qsrc.at[:, :, 1 - c], qnear, 0, beside),
        qcopy(qsrc.at[:, 1 - x, c], qx.at[0], 1, across),
        qcopy(qnear.at[:, 1 - x], qx.at[1], 2, across),
        qcopy(qsrc.at[1 - h, x, c], qh.at[0], 3, away),
        qcopy(qnear.at[1 - h, x], qh.at[1], 4, away),
        qcopy(qx.at[0, 1 - h], qh.at[2], 5, away),
        qcopy(qx.at[1, 1 - h], qh.at[3], 6, away),
    ]
    qcopies[0].start()
    fill(1 - x, 1 - c)
    row_copy(1 - x)
    fill(x, 1 - c)
    row_copy(x)
    fill(1 - x, c)
    wires.arrived(beside_ref.at[1 - x], beside_sem.at[1 - x])
    for g in (1 - h, h):
        total = slots_ref[1 - x, c, g].astype(f32) + beside_ref[1 - x, g].astype(f32)
        ready_ref[g] = total.astype(bf16)
        wires.send(ready_ref.at[g], across_ref.at[g], across_sem.at[g], across)
    wires.arrived(qnear, qrecv.at[0])
    for k in range(1, 5):
        qcopies[k].start()
    fill(x, c)
    wires.arrived(beside_ref.at[x], beside_sem.at[x])
    job.three(2)
    pl.when(~edge)(lambda: job.three(1))

    def row_line(far, g):
        for sign in (-1, 1):
            spot = z + sign * far if far else z
            onward = z - sign
            more = (onward >= 0) & (onward < Z)
            there = None if far == 0 else (spot >= 0) & (spot < Z)
            piece = (spread_ref.at[spot, g], row_recv.at[spot, g])
            if far:
                wires.arrived(*piece, there)
            wires.send(piece[0], *piece, wires.peer(z=onward), both(there, more))

    for g in (1 - h, h):
        wires.arrived(across_ref.at[g], across_sem.at[g])
        total = slots_ref[x, c, g].astype(f32) + beside_ref[x, g].astype(f32)
        total = (total + across_ref[g].astype(f32)).astype(bf16)
        if g is h:
            spread_ref[z, h] = total
        else:
            ready_ref[2 + g] = total
            wires.send(ready_ref.at[2 + g], spread_ref.at[z, h], row_recv.at[z, h], away)
    row_line(0, h)
    job.two(3)
    wires.arrived(spread_ref.at[z, 1 - h], row_recv.at[z, 1 - h])
    row_line(0, 1 - h)
    row_line(1, h)
    for k in (1, 2):
        wires.arrived(qx.at[k - 1], qrecv.at[k])
    qcopies[5].start()
    qcopies[6].start()
    row_line(1, 1 - h)
    for k in range(4):
        wires.arrived(qh.at[k], qrecv.at[3 + k])
    terms = [qsrc.at[h, x, c], qnear.at[h, x], qx.at[0, h], qx.at[1, h]]
    pair = (team, x * C + 1 - c, (1 - x) * C + c, (1 - x) * C + 1 - c)
    for k in range(4):
        sum_rows(qtot.at[pair[k]], [terms[k], qh.at[k]])
    line = Line(wires, Z, [qline], qline_send, qline_recv)

    def heads_line(i):
        s = job.turn(i)
        line.step(0, s, [qtot.at[s]], qtot.at[s], out_qkv)

    pl.loop(0, 2)(heads_line)
    for far in range(2, Z - 1):
        row_line(far, h)
        row_line(far, 1 - h)
    pl.loop(2, Z - 1)(heads_line)
    row_line(Z - 1, h)
    row_line(Z - 1, 1 - h)
    heads_line(Z - 1)
    job.three(3)
    quarter = H * capacity
    products = dot(
        spread_ref[z].reshape(quarter, width), spread_ref[...].reshape(Z * quarter, width), (1,), (1,)
    )
    spot = lax.broadcasted_iota(jnp.int32, products.shape, 0) + z * quarter
    own_spot = spot == lax.broadcasted_iota(jnp.int32, products.shape, 1)
    own_list = jnp.sum(jnp.where(own_spot, listk_ref[...], 0), 1, keepdims=True)
    squares = jnp.sum(jnp.where(own_list == listk_ref[...], products, 0.0))
    for ref in (out_gate, out_up, out_down, out_qkv):
        squares += jnp.sum(ref[...] * ref[...])
    lane = lax.broadcasted_iota(jnp.int32, out_misc.shape, 1)
    squares += jnp.sum(out_misc[...] * out_misc[...] * jnp.where(lane < heads_width, 1.0, 1.0 / Z))
    norm_ref[me] = jnp.full(norm_ref.shape[1:], squares)

    @pl.loop(0, Z)
    def _(s):
        line.settle(0, s, qtot.at[s])

    for copy in qcopies:
        copy.wait_send()
    for swap in swaps:
        swap.wait_send()
    job.settle()
    wires.drain()
    tell = [
        pltpu.make_async_remote_copy(
            src_ref=norm_ref.at[me],
            dst_ref=norm_ref.at[me],
            send_sem=norm_send.at[k],
            recv_sem=norm_recv.at[k],
            device_id=coordinates((me + k) % devices),
            device_id_type=MESH,
        )
        for k in range(1, devices)
    ]
    for copy in tell:
        copy.start()
    for k in range(1, devices):
        wires.arrived(norm_ref.at[(me + devices - k) % devices], norm_recv.at[k])
    total_ref[...] = jnp.sum(norm_ref[...], 0)
    for copy in tell:
        copy.wait_send()


def back(swap, q, k, v, x_low, cosine, sine, segments, slot, listed, grad_first, w_heads, terms, heads, capacity, dims, number):
    H, X, C, Z = dims
    length, width = x_low.shape
    lanes = q.shape[1]
    team, own_len, heads_width = swap.shape
    batch = H * team
    rows = width // batch
    widths = [term.shape[2] for term in terms]
    wide = 3 * heads_width
    vmem = lambda shape, dtype=bf16: pltpu.VMEM(shape, dtype)
    dma = lambda *shape: pltpu.SemaphoreType.DMA(shape)
    shapes = [(Z, H, X), (Z, H, X), (Z, 2), (Z,), (Z + 1,)]
    n = len(terms)
    return call(
        partial(back_kernel, dims, heads),
        (
            swap,
            q,
            k,
            v,
            x_low,
            cosine,
            sine,
            segments[None, :],
            segments[:, None],
            slot[None, :],
            grad_first,
            listed[None, :],
            w_heads,
            *(term.reshape(Z, H, X, C, rows, -1) for term in terms),
        ),
        [jax.ShapeDtypeStruct((rows, w), f32) for w in widths + [wide]]
        + [
            jax.ShapeDtypeStruct((Z, H, capacity, width), bf16),
            jax.ShapeDtypeStruct((length, width), bf16),
            jax.ShapeDtypeStruct((8, 128), f32),
        ],
        [on_chip] * 8,
        [vmem(shape + (rows, w)) for shape in shapes for w in widths]
        + [
            vmem(swap.shape),
            vmem((length, lanes)),
            vmem((length, lanes), f32),
            vmem((length, lanes), f32),
            vmem((length, wide)),
            vmem((width, wide), f32),
            vmem(w_heads.shape[1:]),
            vmem((H, X, C, rows, wide)),
            vmem((H, X, rows, wide)),
            vmem((2, H, rows, wide)),
            vmem((4, rows, wide)),
            vmem((Z, rows, wide)),
            vmem((Z + 1, rows, wide)),
            vmem((X, C, H, capacity, width)),
            vmem((X, H, capacity, width)),
            vmem((H, capacity, width)),
            vmem((2 * H, capacity, width)),
            dma(n, Z),
            dma(n, Z),
            dma(n, Z, 2),
            dma(n, Z),
            dma(n, Z),
            dma(n, Z, 2),
            dma(n, Z),
            dma(n, Z),
            dma(n, Z + 1),
            dma(3),
            dma(team),
            pltpu.SemaphoreType.DMA,
            dma(7),
            dma(7),
            dma(1, Z),
            dma(1, Z + 1),
            dma(2 + 2 + 1 + 4 * Z),
            dma(X),
            dma(H),
            dma(Z, H + 1),
            vmem((batch * Z, 8, 128), f32),
            dma(batch * Z),
            dma(batch * Z),
        ],
        number,
        in_specs=[on_chip] * 12 + [anywhere] * 5,
        vmem=67_000_000,
    )


def adam_update(weight, grad, first, second, rate):
    first = 0.5 * first + 0.5 * grad
    second = 0.5 * second + 0.5 * grad * grad
    unbiased = 1.0 / (1.0 - 0.5**step_number)
    weight = weight - rate * (
        first * unbiased / (jnp.sqrt(second * unbiased) + 1e-08) + 0.01 * weight
    )
    return (weight, first, second)


def blank(shape, dtype):
    return pl.pallas_call(
        lambda o_ref: None, out_specs=anywhere, out_shape=jax.ShapeDtypeStruct(shape, dtype)
    )()


def rows_kernel(list_ref, table_ref, o_ref, hold_ref, sem):
    count = o_ref.shape[0]

    @pl.loop(0, count)
    def _(i):
        row = pl.ds(list_ref[i], 1)
        pltpu.make_async_copy(table_ref.at[row, :], hold_ref.at[pl.ds(i, 1), :], sem).start()

    pltpu.make_async_copy(hold_ref, hold_ref, sem).wait()
    o_ref[...] = hold_ref[...].astype(bf16)


def low_rows(table, listed):
    shape = (listed.shape[0], table.shape[1])
    return pl.pallas_call(
        rows_kernel,
        in_specs=[pl.BlockSpec(memory_space=pltpu.SMEM), anywhere],
        out_specs=on_chip,
        out_shape=jax.ShapeDtypeStruct(shape, bf16),
        scratch_shapes=[pltpu.VMEM(shape, f32), pltpu.SemaphoreType.DMA],
    )(listed, table)


def table_kernel(rate, rounds_ref, scale_ref, list_ref, rows_ref, more_ref, w_ref, m_ref, v_ref, nw_ref, g_ref, nv_ref, far_ref, sem):
    block, width = w_ref.shape
    count = list_ref.shape[1]
    start = pl.program_id(0) * block

    def placed(turn, rows):
        row = lax.broadcasted_iota(jnp.int32, (block, count), 0) + start
        pick = (row == list_ref[pl.ds(turn, 1), :]).astype(bf16)
        return dot(pick, rows, (1,), (0,))

    g_ref[...] = placed(0, rows_ref[...])

    @pl.loop(1, rounds_ref[0])
    def _(turn):
        copy = pltpu.make_async_copy(more_ref.at[turn - 1], far_ref, sem)
        copy.start()
        copy.wait()
        g_ref[...] += placed(turn, far_ref[...])

    grad = g_ref[...] * scale_ref[0]
    new_w, _, new_v = adam_update(w_ref[...], grad, m_ref[...], v_ref[...], rate)
    g_ref[...] = grad
    nw_ref[...] = new_w
    nv_ref[...] = new_v


def update_table(rounds, scale, lists, rows, more, table, first, second, rate):
    height, width = table.shape
    sizes = [n for n in range(8, 513, 8) if height % n == 0]
    block = max(sizes) if sizes else height
    part = pl.BlockSpec((block, width), lambda i: (i, 0))
    whole = lambda a: pl.BlockSpec(a.shape, lambda i: (0,) * a.ndim)
    single = pl.BlockSpec(memory_space=pltpu.SMEM)
    return pl.pallas_call(
        partial(table_kernel, rate),
        grid=(height // block,),
        in_specs=[single, single, whole(lists), whole(rows), anywhere, part, part, part],
        out_specs=[part] * 3,
        out_shape=[jax.ShapeDtypeStruct(table.shape, f32)] * 3,
        scratch_shapes=[pltpu.VMEM(rows.shape, bf16), pltpu.SemaphoreType.DMA],
        compiler_params=pltpu.CompilerParams(vmem_limit_bytes=56 * 2**20),
    )(rounds.reshape(1), scale.reshape(1), lists, rows, more, table, first, second)


def small_kernel(scale_ref, qkv_ref, misc_ref, gate_ref, up_ref, down_ref, *refs):
    ins, outs = refs[:15], refs[15:]
    scale = scale_ref[0]
    heads_width = ins[0].shape[2]
    turned_misc = misc_ref[...].T

    def update(k, grad, where):
        old, first, second = (ins[3 * k + n][where] for n in range(3))
        for n, value in enumerate(adam_update(old, grad * scale, first, second, rates[1 + k])):
            outs[3 * k + n][where] = value

    for part in range(3):
        grad = qkv_ref[:, part * heads_width : (part + 1) * heads_width]
        update(0, grad, part)
    update(1, turned_misc[:heads_width], (slice(None), slice(None)))
    update(2, gate_ref[...], (slice(None), 0, slice(None)))
    update(2, up_ref[...], (slice(None), 1, slice(None)))
    update(3, down_ref[...], (slice(None), slice(None)))
    count = ins[12].shape[0]
    update(4, turned_misc[heads_width : heads_width + count], (slice(None), slice(None)))


def update_small(scale, sums, olds, firsts, seconds):
    views = (lambda a: a.transpose(1, 0, 2), lambda a: a, lambda a: a, lambda a: a.T, lambda a: a)
    groups = zip(views, zip(olds, firsts, seconds))
    values = [view(value) for view, group in groups for value in group]
    whole = lambda a: pl.BlockSpec(a.shape, lambda i: (0,) * a.ndim)
    outs = pl.pallas_call(
        small_kernel,
        grid=(1,),
        in_specs=[pl.BlockSpec(memory_space=pltpu.SMEM)] + [whole(a) for a in (*sums, *values)],
        out_specs=[whole(a) for a in values],
        out_shape=[jax.ShapeDtypeStruct(value.shape, f32) for value in values],
        compiler_params=pltpu.CompilerParams(vmem_limit_bytes=50 * 2**20),
    )(scale.reshape(1), *sums, *values)
    return [tuple(view(new) for new in outs[3 * k : 3 * k + 3]) for k, view in enumerate(views)]


def local(
    dims,
    token_ids,
    segment_ids,
    row_of,
    query_count,
    table,
    qkv_weight,
    out_weight,
    gate_up_weight,
    down_weight,
    gains,
    table_m,
    qkv_m,
    out_m,
    gate_up_m,
    down_m,
    gains_m,
    table_v,
    qkv_v,
    out_v,
    gate_up_v,
    down_v,
    gains_v,
):
    H, X, C, Z = dims
    G = X * C
    batch = H * G
    at = {name: lax.axis_index(name) for name in ALL}
    team = at["x"] * C + at["c"]
    owner = at["h"] * G + team
    length = token_ids.shape[1]
    own_len = length // G
    part_len = length // Z
    shard_rows, width = table.shape
    rows_in = width // batch
    heads_width = qkv_weight.shape[2]
    ff_part = down_weight.shape[0]
    capacity = -(-3 * length // (64 * batch)) * 16

    position = jnp.arange(length, dtype=jnp.int32)
    start = at["z"] * part_len
    mine = lax.dynamic_slice_in_dim(token_ids[0], start, part_len, 0)
    mine_seg = lax.dynamic_slice_in_dim(segment_ids[0], start, part_len, 0)
    earlier = position[None, :] < (start + position[:part_len])[:, None]
    seen = jnp.any((mine[:, None] == token_ids[0][None, :]) & earlier, 1)
    tags = jnp.stack([row_of[mine] * 2 + seen.astype(jnp.int32), mine_seg])
    everyone = gather_everyone(tags, dims, 0)
    tags_all = everyone[:, 0].reshape(batch, length)
    segs_all = everyone[:, 1].reshape(batch, length)
    ids_all, fresh_all = tags_all // 2, tags_all % 2 == 0
    row = at["h"] * Z + at["z"]
    seg_row = lax.dynamic_index_in_dim(segs_all, row, 0, keepdims=False)
    ids_row = lax.dynamic_index_in_dim(ids_all, row, 0, keepdims=False)
    fresh_row = lax.dynamic_index_in_dim(fresh_all, row, 0, keepdims=False)

    def counted(flags):
        lanes = 128 if length % 128 == 0 else length
        steps = flags.astype(f32).reshape(-1, length // lanes, lanes)
        upto = jnp.arange(lanes)[:, None] <= jnp.arange(lanes)[None, :]
        inner = jnp.einsum("rgl,lk->rgk", steps, upto.astype(f32))
        sums = inner[:, :, -1]
        groups = jnp.arange(length // lanes)
        before = (groups[:, None] < groups[None, :]).astype(f32)
        outer = jnp.dot(sums, before, precision=peak_affinity)
        return (inner + outer[:, :, None]).reshape(-1, length).astype(jnp.int32)

    owned = fresh_all & (ids_all // shard_rows == owner)
    number = counted(owned)
    shares = (ids_all // shard_rows)[:, None, :] == jnp.arange(batch, dtype=jnp.int32)[None, :, None]
    shares = jnp.sum((shares & fresh_all[:, None, :]).astype(jnp.int32), 2)
    rounds = (jnp.max(shares) + capacity - 1) // capacity
    offset = jnp.where(owned, number, 0)
    spot = jnp.arange(1, capacity + 1, dtype=jnp.int32)

    def owned_list(turn, rows):
        ids = lax.dynamic_slice_in_dim(ids_all, rows[0], rows[1], 0) if rows else ids_all
        places = lax.dynamic_slice_in_dim(offset, rows[0], rows[1], 0) if rows else offset
        hit = (spot + turn * capacity)[None, :, None] == places[:, None, :]
        return jnp.sum(jnp.where(hit, (ids - owner * shard_rows + 1)[:, None, :], 0), 2) - 1

    holder_row = ids_row // shard_rows
    holders = jnp.arange(batch, dtype=jnp.int32)
    split = fresh_row[None, :] & (holder_row[None, :] == holders[:, None])
    number_row = jnp.sum(jnp.where(split, counted(split), 0), 0)
    same_row = ids_row[:, None] == ids_row[None, :]
    rank_row = jnp.sum(jnp.where(same_row, number_row[None, :], 0), 1) - 1
    slots = batch * capacity

    def listed_for(turn):
        return owned_list(turn, None).reshape(H, Z, capacity).transpose(1, 0, 2).reshape(-1)

    def slot_of(turn):
        rank = rank_row - turn * capacity
        slot = ((holder_row % G) * H + holder_row // G) * capacity + rank
        return jnp.where((rank >= 0) & (rank < capacity), slot, -1)

    def expander(turn):
        slot = slot_of(turn)
        return (slot[:, None] == jnp.arange(slots, dtype=jnp.int32)[None, :]).astype(bf16)

    labels = jnp.arange(SEGS, dtype=jnp.int32)
    marks = jnp.arange(SEGS + 1, dtype=jnp.int32)
    member_row = (seg_row[:, None] == marks[None, :]).astype(jnp.int32)
    counts_row = jnp.sum(member_row, 0)
    starts = jnp.cumsum(counts_row) - counts_row
    places = (position - jnp.sum(member_row * starts[None, :], 1)).astype(f32)
    cosine, sine = angles_of(places, HEAD_DIM)
    heads = heads_width // HEAD_DIM

    def rows_for(turn):
        listed = jnp.concatenate([owned_list(turn, (h * Z + at["z"], 1)) for h in range(H)])
        return low_rows(table, jnp.maximum(listed, 0).reshape(-1)).reshape(H, capacity, width)

    def fetch(turn):
        got = fetch_rows(rows_for(turn), dims, 1).reshape(slots, width)
        return jnp.dot(expander(turn), got, preferred_element_type=f32).astype(bf16)

    _, x_more = lax.while_loop(
        lambda s: s[0] < rounds,
        lambda s: (s[0] + 1, s[1] + fetch(s[0])),
        (jnp.int32(1), jnp.zeros((length, width), bf16)),
    )

    pad = -(-(heads_width + 2) // 128) * 128 - heads_width
    misc = jnp.concatenate([out_weight.T, gains.T, jnp.zeros((rows_in, pad - 2), f32)], 1)
    pieces = [
        qkv_weight.reshape(rows_in, -1).astype(bf16),
        misc.astype(bf16),
        gate_up_weight[:, 0].astype(bf16),
        gate_up_weight[:, 1].astype(bf16),
        down_weight.T.astype(bf16),
    ]
    if H == 2:
        freqs = jnp.power(1000.0, -2.0 * jnp.arange(HEAD_DIM // 2, dtype=f32) / HEAD_DIM)
        freqs = jnp.tile(freqs, 256 // HEAD_DIM)[None, :]
        weights, (x_low, query, keys, values, attended, x_own, *tables) = front(
            rows_for(0), slot_of(0), x_more, places, freqs, seg_row, pieces, heads_width, dims, 2
        )
    else:
        weights = gather_weights(pieces, dims)
    w_qkv, w_misc, w_gate, w_up, w_down = weights
    w_out = w_misc[:, :, :heads_width]
    gain = w_misc[0, :, heads_width : heads_width + 2].T.astype(f32)
    if H != 2:
        w_heads = lax.dynamic_index_in_dim(w_qkv, team, 0, keepdims=False)
        x_low = x_more + fetch(0)
        qkv = jnp.dot(x_low, w_heads, preferred_element_type=f32).reshape(length, 3, heads, HEAD_DIM)
        query = rotate(qkv[:, 0], cosine, sine).astype(bf16).reshape(length, -1)
        keys = rotate(qkv[:, 1], cosine, sine).astype(bf16).reshape(length, -1)
        values = qkv[:, 2].astype(bf16).reshape(length, -1)
        attended_heads = attend(query, keys, values, seg_row)
        attended = team_swap(attended_heads.reshape(G, own_len, heads_width), dims, 3)
        x_own = lax.dynamic_slice_in_dim(x_low, team * own_len, own_len, 0)
    seg_own = lax.dynamic_slice_in_dim(seg_row, team * own_len, own_len, 0)
    counts_all = jnp.sum((segs_all[:, None, :] == labels[None, :, None]).astype(f32), -1).reshape(-1, 1)
    if H == 2:
        loss_value, grad_attended, grad_first, terms = middle(
            query_count, attended, x_own, seg_own, counts_all, weights[2:] + [w_misc], dims, 4
        )
    else:
        attended = attended.transpose(1, 0, 2)
        attn = dot(attended, w_out, (1, 2), (0, 2))
        hidden_one, first_back = jax.vjp(layer_norm, x_own.astype(f32) + attn, gain[0])
        hidden_low = hidden_one.astype(bf16)
        gate = jnp.einsum("td,zdf->ztf", hidden_low, w_gate, preferred_element_type=f32)
        up = jnp.einsum("td,zdf->ztf", hidden_low, w_up, preferred_element_type=f32)
        active, swiglu_back = jax.vjp(swiglu, gate, up)
        active_low = active.astype(bf16)
        mlp = dot(active_low, w_down, (0, 2), (0, 2))
        hidden_two, second_back = jax.vjp(layer_norm, hidden_one + mlp, gain[1])

        loss_value, grad_two = contrast_all(hidden_two, seg_own, counts_all, query_count, dims)
        grad_second, grad_gain_two = second_back(grad_two)
        grad_mlp_low = grad_second.astype(bf16)
        grad_active = jnp.einsum("tn,znf->ztf", grad_mlp_low, w_down, preferred_element_type=f32)
        grad_down = jnp.einsum("tn,ztf->znf", grad_mlp_low, active_low, preferred_element_type=f32)
        grad_gate, grad_up = swiglu_back(grad_active)
        grad_gate_low, grad_up_low = grad_gate.astype(bf16), grad_up.astype(bf16)
        grad_one = grad_second + dot(grad_gate_low, w_gate, (0, 2), (0, 2))
        grad_one = grad_one + dot(grad_up_low, w_up, (0, 2), (0, 2))
        grad_first, grad_gain_one = first_back(grad_one)
        weight_grad = partial(jnp.einsum, "td,ztf->zdf", preferred_element_type=f32)
        grad_gate = weight_grad(hidden_low, grad_gate_low).astype(bf16)
        grad_up = weight_grad(hidden_low, grad_up_low).astype(bf16)
        grad_attn_low = grad_first.astype(bf16)
        grad_attended = jnp.einsum("tn,znk->tzk", grad_attn_low, w_out, preferred_element_type=f32)
        grad_attended = grad_attended.astype(bf16).transpose(1, 0, 2)
        grad_out = jnp.einsum("tn,tzk->znk", grad_attn_low, attended, preferred_element_type=f32)
        grad_gains = jnp.stack([grad_gain_one, grad_gain_two], 1)
        grad_misc = jnp.concatenate(
            [
                grad_out.astype(bf16),
                jnp.broadcast_to(grad_gains.astype(bf16)[None], (Z, width, 2)),
                jnp.zeros((Z, width, pad - 2), bf16),
            ],
            2,
        )
        terms = [grad_gate, grad_up, grad_down.astype(bf16), grad_misc]
    most_rounds = -(-length // capacity)
    listed = listed_for(0)
    _, lists = lax.while_loop(
        lambda s: s[0] < rounds,
        lambda s: (
            s[0] + 1,
            lax.dynamic_update_slice_in_dim(s[1], listed_for(s[0])[None], s[0], 0),
        ),
        (jnp.int32(1), jnp.broadcast_to(listed[None], (most_rounds,) + listed.shape)),
    )
    if H == 2:
        sum_gate, sum_up, sum_down, sum_misc, sum_qkv, spread, grad_zero_low, total = back(
            grad_attended,
            query,
            keys,
            values,
            x_low,
            *tables,
            seg_row,
            slot_of(0),
            listed,
            grad_first,
            w_qkv,
            terms,
            heads,
            capacity,
            dims,
            5,
        )
    else:
        grad_heads = team_swap(grad_attended, dims, 5).reshape(length, heads_width)
        grad_query, grad_keys, grad_values = attend_back(query, grad_heads, keys, values, seg_row)
        back_turn = lambda g: rotate(g.reshape(length, heads, HEAD_DIM), cosine, -sine).reshape(length, -1)
        grad_qkv_low = jnp.concatenate([back_turn(grad_query), back_turn(grad_keys), grad_values], 1)
        grad_qkv_low = grad_qkv_low.astype(bf16)
        grad_heads_w = dot(x_low, grad_qkv_low, (0,), (0,)).astype(bf16)
        grad_zero = dot(grad_qkv_low, w_heads, (1,), (1,))
        own_term = lax.dynamic_update_slice_in_dim(
            jnp.zeros_like(grad_zero), grad_first, team * own_len, 0
        )
        grad_zero_low = (grad_zero + own_term).astype(bf16)
        heads_grad = lax.dynamic_update_slice_in_dim(
            jnp.zeros((Z,) + grad_heads_w.shape, bf16), grad_heads_w[None], team, 0
        )
        sum_gate, sum_up, sum_down, sum_misc, sum_qkv = reduce_weights(terms + [heads_grad], dims)

    def collect(turn):
        terms = dot(expander(turn), grad_zero_low, (0,), (0,)).astype(bf16)
        terms = terms.reshape(X, C, H, capacity, width)
        return settle_rows(terms, dims, 6)

    flat = lambda rows: rows.reshape(Z * H * capacity, width)
    spread = flat(spread if H == 2 else collect(0))

    def between(left, left_list, right, right_list):
        same = left_list[:, None] == right_list[None, :]
        return jnp.sum(jnp.where(same, dot(left, right, (1,), (1,)), 0.0))

    def summed(squares):
        return jnp.sum(gather_everyone(jnp.full((8, 128), squares), dims, 8), 0)

    def further(state):
        turn, more, total = state
        rows = flat(collect(turn))
        listed = lists[turn]
        squares = between(rows, listed, rows, listed) + 2 * between(rows, listed, spread, lists[0])
        squares += 2 * lax.fori_loop(
            1, turn, lambda k, held: held + between(rows, listed, more[k - 1], lists[k]), jnp.zeros((), f32)
        )
        more = lax.dynamic_update_slice_in_dim(more, rows[None], turn - 1, 0)
        return turn + 1, more, total + summed(squares / Z)

    if H != 2:
        squares = between(spread, listed, spread, listed) + jnp.sum(sum_misc[:, heads_width:] ** 2)
        squares = squares / Z + jnp.sum(sum_misc[:, :heads_width] ** 2)
        for part in (sum_qkv, sum_gate, sum_up, sum_down):
            squares += jnp.sum(part * part)
        total = summed(squares)
    blank_rows = blank((max(most_rounds - 1, 1),) + spread.shape, bf16)
    _, more, total = lax.while_loop(
        lambda s: s[0] < rounds, further, (jnp.int32(1), blank_rows, total)
    )
    grad_norm = jnp.sqrt(total[0, 0])
    scale = clip_limit / jnp.maximum(grad_norm, clip_limit)
    new_table, clipped_table, new_table_v = update_table(
        rounds, scale, lists, spread, more, table, table_m, table_v, rates[0]
    )
    updated = update_small(
        scale,
        (sum_qkv, sum_misc, sum_gate, sum_up, sum_down),
        (qkv_weight, out_weight, gate_up_weight, down_weight, gains),
        (qkv_m, out_m, gate_up_m, down_m, gains_m),
        (qkv_v, out_v, gate_up_v, down_v, gains_v),
    )
    return (
        loss_value.reshape(1),
        grad_norm.reshape(1),
        new_table,
        *(new[0] for new in updated),
        clipped_table,
        *(new[1] for new in updated),
        new_table_v,
        *(new[2] for new in updated),
    )


def solution(mesh):
    batch, mp = mesh.shape["batch"], mesh.shape["mp"]
    dims = (batch // mp, mp // 2, 2, mp)
    split = Mesh(mesh.devices.reshape(dims), ALL)
    rows = ("h", "x", "c")
    weights = (
        P(rows, None),
        P(rows, None, "z"),
        P("z", rows),
        P(rows, None, "z"),
        P("z", rows),
        P(None, rows),
    )
    return jax.shard_map(
        partial(local, dims),
        mesh=split,
        in_specs=(P(rows, None), P(rows, None), P(), P()) + weights * 3,
        out_specs=(P(), P()) + weights + weights + weights,
        check_vma=False,
    )
```
